768 devices in a mesh: space: 64 (over z_hi, y, core), band: 12 (over x, z_lo).
Axes of the slice: x: 4, y: 8, z: 12 (z_hi: 4, z_lo: 3; z = z_hi * 3 + z_lo), core: 2. Of those that a mesh axis runs over, the one named last changes fastest.
Arguments:
- psi: float32 [192, 263424], P('band', 'space'), may hold values from -400 to 400
- ham: bfloat16 [768, 512, 512], P('space'), may hold values from -2 to 2, as said below
- conn: int32 [768, 512], P('space'), may hold values from 0 to 4703, as said below
- face_rows: int32 [37632], P('space'), may hold values from 0 to 4115, as said below
Outputs:
- ortho: float32 [192, 263424], P('band', 'space')
The draws below stay inside these ranges and needn't reach their ends.
Inputs may be any that keep to these rules, and one draw needn't show every extreme that they name: `conn`: rows s * 12 to (s + 1) * 12 - 1 are the elements of domain s. Entries at element-local nodes below 448 name the domain's own rows 0 to 4115; entries at and above 448 name ghost slots 4116 + j, where ghost slot j is the node listed at position j of face_rows of domain (s + 1) mod 64. Every own row and every ghost slot of a domain is named by some element. `face_rows`: entries s * 588 to (s + 1) * 588 - 1 are 588 distinct own rows of domain s: the nodes of its lower face. `ham`: each matrix is symmetric.
All inputs are finite; a program needn't handle non-finite values.
Results may differ from the reference program's by a relative error of at most 0.0037.
Values may be sent and summed in bfloat16 or wider, within the bound.
A program may use at most 32 MiB of HBM per device.

```python
import math
import jax
import jax.numpy as jnp
from jax import lax

P_SIZE = 8
EX = 4
EY = 3
STEPS = 2
NODE_EL = 512
E_DEV = 12
NODES = 4116
FACE = 588
DOMAINS = 64
BANDS = 192
TOTAL_NODES = 263424


def numbering(key):
    domain_keys = jax.random.split(jax.random.fold_in(key, 17), DOMAINS)
    shuffled = jax.vmap(lambda single: jax.random.permutation(single, NODES))(domain_keys)
    shuffled = shuffled.astype(jnp.int32)
    return ((shuffled - shuffled[:, :1] - 1) % NODES).astype(jnp.int32)


def draw_face_rows(key, part):
    local_rows = numbering(key)
    return local_rows[:, :FACE].reshape(DOMAINS * FACE).astype(jnp.int32)


def draw_conn(key, part):
    local_rows = numbering(key)
    element = jnp.arange(E_DEV, dtype=jnp.int32)
    elem_x = element % EX
    elem_y = element // EX
    local_node = jnp.arange(NODE_EL, dtype=jnp.int32)
    node_x = local_node % P_SIZE
    node_y = local_node // P_SIZE % P_SIZE
    node_z = local_node // (P_SIZE * P_SIZE)
    width_x = (P_SIZE - 1) * EX
    width_y = (P_SIZE - 1) * EY
    grid_x = (elem_x[:, None] * (P_SIZE - 1) + node_x[None, :]) % width_x
    grid_y = (elem_y[:, None] * (P_SIZE - 1) + node_y[None, :]) % width_y
    position = grid_y * width_x + grid_x
    canonical = jnp.minimum(node_z[None, :] * FACE + position, NODES - 1)
    owned = local_rows[:, canonical]
    result = jnp.where(node_z[None, None, :] == P_SIZE - 1, NODES + position[None, :, :], owned)
    return result.reshape(DOMAINS * E_DEV, NODE_EL).astype(jnp.int32)


def draw_ham(key, part):
    count = DOMAINS * E_DEV
    key_entries, key_diagonal = jax.random.split(jax.random.fold_in(key, 29))
    spread = 0.4 * (2.0 / NODE_EL) ** 0.5
    entries = jax.random.truncated_normal(key_entries, -4.0, 4.0, (count, NODE_EL, NODE_EL), jnp.float32)
    diagonal = jax.random.uniform(key_diagonal, (count, NODE_EL), jnp.float32, 0.5, 1.5)
    symmetric = (entries + jnp.swapaxes(entries, 1, 2)) * (0.5 * spread)
    identity = jnp.eye(NODE_EL, dtype=jnp.float32)
    result = symmetric * (1.0 - identity) + diagonal[:, :, None] * identity
    return result.astype(jnp.bfloat16)


def draw_psi(key, part):
    key_values, key_rows, key_cols = jax.random.split(jax.random.fold_in(key, 41), 3)
    row_scale = jnp.exp(jax.random.uniform(key_rows, (BANDS, 1), jnp.float32, 0.0, math.log(10.0)))
    col_scale = jnp.exp(jax.random.uniform(key_cols, (1, TOTAL_NODES), jnp.float32, 0.0, math.log(10.0)))
    values = jax.random.truncated_normal(key_values, -4.0, 4.0, (BANDS, TOTAL_NODES), jnp.float32)
    return (values * row_scale * col_scale).astype(jnp.float32)


def setup_inputs(seed: int = 0) -> dict:
    splits = jax.random.split(jax.random.key(seed), 5)
    return {
        "psi": draw_psi(jax.random.fold_in(splits[4], 71), 0),
        "ham": draw_ham(jax.random.fold_in(splits[4], 71), 0),
        "conn": draw_conn(jax.random.fold_in(splits[4], 71), 0),
        "face_rows": draw_face_rows(jax.random.fold_in(splits[4], 71), 0),
    }


CENTER = 6.25
HALF_WIDTH = 7.5

def take_face(field, rows_list):
    return jnp.take(field, rows_list, axis=1)

def add_face(field, values, rows_list):
    return field.at[:, rows_list].add(values)

def domain_product(operands):
    field, ghost, matrices, links = operands
    extended = jnp.concatenate([field, ghost], axis=1)
    flat_links = links.reshape(-1)
    gathered = jnp.take(extended, flat_links, axis=1).reshape(BANDS, E_DEV, NODE_EL).astype(jnp.float32)
    products = jnp.einsum('bem,eml->bel', gathered, matrices.astype(jnp.float32))
    summed = jnp.zeros((BANDS, NODES + FACE), jnp.float32)
    return summed.at[:, flat_links].add(products.reshape(BANDS, E_DEV * NODE_EL))

def apply_operator(fields, ham_domains, conn_domains, face_domains):
    rounded = fields.astype(jnp.bfloat16)
    face_values = jax.vmap(take_face)(rounded, face_domains)
    ghosts = jnp.roll(face_values, -1, axis=0)
    summed = lax.map(domain_product, (rounded, ghosts, ham_domains, conn_domains))
    received = jnp.roll(summed[:, :, NODES:], 1, axis=0)
    return jax.vmap(add_face)(summed[:, :, :NODES], received, face_domains)

def reference(psi, ham, conn, face_rows):
    fields = psi.reshape(BANDS, DOMAINS, NODES).transpose(1, 0, 2)
    ham_domains = ham.reshape(DOMAINS, E_DEV, NODE_EL, NODE_EL)
    conn_domains = conn.reshape(DOMAINS, E_DEV, NODE_EL)
    face_domains = face_rows.reshape(DOMAINS, FACE)
    previous = fields
    current = (apply_operator(fields, ham_domains, conn_domains, face_domains) - CENTER * fields) / HALF_WIDTH
    for iteration in range(STEPS - 1):
        scaled = (apply_operator(current, ham_domains, conn_domains, face_domains) - CENTER * current) / HALF_WIDTH
        following = 2.0 * scaled - previous
        previous = current
        current = following
    filtered = current.transpose(1, 0, 2).reshape(BANDS, TOTAL_NODES)
    correlation = lax.dot_general(filtered.astype(jnp.float32), filtered.astype(jnp.float32), (((1,), (1,)), ((), ())), precision=lax.Precision.HIGHEST, preferred_element_type=jnp.float32) / TOTAL_NODES
    factor = jnp.linalg.cholesky(correlation)
    return jax.scipy.linalg.solve_triangular(factor, filtered, lower=True)
```

```python
import functools

import jax
import jax.numpy as jnp
from jax import lax
from jax.experimental import pallas as pl
from jax.experimental.pallas import tpu as pltpu
from jax.sharding import PartitionSpec as P

NODE_EL = 512
OWN_EL = 448
CENTER = 6.25
HALF_WIDTH = 7.5
LO = 256
MESH = pl.DeviceIdType.MESH
BF = jnp.bfloat16
F32 = jnp.float32
VMEM_LIMIT = 60 * 1024 * 1024

CORES, YS, ZS = 2, 8, 4
NT = (((1,), (1,)), ((), ()))
TN = (((0,), (0,)), ((), ()))


def nn(a, b):
    return jnp.dot(a, b, preferred_element_type=F32)


def nt(a, b):
    return lax.dot_general(a, b, NT, preferred_element_type=F32)


def remote(src, dst, send, recv, where):
    return pltpu.make_async_remote_copy(
        src_ref=src, dst_ref=dst, send_sem=send, recv_sem=recv, device_id=where, device_id_type=MESH
    )


def split(value):
    high = value.astype(BF)
    return high, (value - high.astype(F32)).astype(BF)


def filter_kernel(
    psi_ref, ham_ref, conn_ref, face_ref, out_ref,
    onehot, onehot_face, hi_ref, hi_face, base, field, sums, xb, xg, gathered, products,
    send1, send2, send3, send4, got1, got2, got3, got4, send_sem, recv_sem,
):
    bands, nodes = psi_ref.shape
    elems = conn_ref.shape[0]
    faces = face_ref.shape[1]
    own_blocks = pl.cdiv(nodes, LO)
    ghost_blocks = pl.cdiv(faces, LO)
    face_pad = got1.shape[1]
    shift = own_blocks * LO - nodes
    domains = lax.axis_size("space")
    me = lax.axis_index("space")
    below = {"space": lax.rem(me + domains - 1, domains)}
    above = {"space": lax.rem(me + 1, domains)}

    barrier = pltpu.get_barrier_semaphore()
    for there in (below, above):
        pl.semaphore_signal(barrier, inc=1, device_id=there, device_id_type=MESH)

    for h in range(own_blocks):
        rows = slice(h * bands, (h + 1) * bands)
        if (h + 1) * LO <= nodes:
            value = psi_ref[:, h * LO:(h + 1) * LO]
            base[rows, :] = value
            xb[rows, :] = value.astype(BF)
        else:
            base[rows, :] = jnp.zeros((bands, LO), F32)
            base[rows, 0:nodes - h * LO] = psi_ref[:, h * LO:nodes]
            xb[rows, :] = base[rows, :].astype(BF)

    hi_face[...] = jnp.full(hi_face.shape, -1, jnp.int32)
    hi_face[:, 0:faces] = jnp.broadcast_to(face_ref[...], (bands, faces))
    named = hi_face[...]
    lanes = lax.broadcasted_iota(jnp.int32, (LO, face_pad), 0)
    onehot_face[...] = jnp.where(lanes == (named[0:1, :] & (LO - 1)), 1.0, 0.0).astype(BF)
    hi_face[...] = named >> 8

    def take_face(blocks):
        table = nn(blocks, onehot_face[...])
        which = hi_face[...]
        total = jnp.zeros((bands, face_pad), F32)
        for h in range(own_blocks):
            total = jnp.where(which == h, table[h * bands:(h + 1) * bands, :], total)
        return total

    send1[...] = take_face(xb[...]).astype(BF)
    pl.semaphore_wait(barrier, 2)
    copy1 = remote(send1, got1, send_sem.at[0], recv_sem.at[0], below)
    copy1.start()

    spot = lax.broadcasted_iota(jnp.int32, (1, NODE_EL), 1)
    depth = lax.broadcasted_iota(jnp.int32, (LO, NODE_EL), 0)

    def prepare(e, carry):
        cols = pl.ds(pl.multiple_of(e * NODE_EL, NODE_EL), NODE_EL)
        named = conn_ref[pl.ds(e, 1), :]
        named = jnp.where(spot >= OWN_EL, named + shift, named)
        onehot[:, cols] = jnp.where(depth == (named & (LO - 1)), 1.0, 0.0).astype(BF)
        hi_ref[:, cols] = jnp.broadcast_to(named >> 8, (bands, NODE_EL))
        return carry

    lax.fori_loop(0, elems, prepare, 0)

    def gather_own(e, carry):
        cols = pl.ds(pl.multiple_of(e * NODE_EL, NODE_EL), NODE_EL)
        table = nn(xb[...], onehot[:, cols])
        which = hi_ref[:, cols]
        total = jnp.zeros((bands, NODE_EL), F32)
        for h in range(own_blocks):
            total = jnp.where(which == h, table[h * bands:(h + 1) * bands, :], total)
        gathered[:, cols] = total.astype(BF)
        return carry

    def multiply(e, carry):
        cols = pl.ds(pl.multiple_of(e * NODE_EL, NODE_EL), NODE_EL)
        tail = pl.ds(pl.multiple_of(e * NODE_EL + NODE_EL - 128, 128), 128)
        table = nn(xg[...], onehot[:, tail])
        which = hi_ref[:, tail]
        total = gathered[:, tail].astype(F32)
        for h in range(ghost_blocks):
            total = jnp.where(which == own_blocks + h, table[h * bands:(h + 1) * bands, :], total)
        gathered[:, tail] = total.astype(BF)
        products[:, cols] = nn(gathered[:, cols], ham_ref[e])
        return carry

    def scatter_all(e, carry):
        cols = pl.ds(pl.multiple_of(e * NODE_EL, NODE_EL), NODE_EL)
        high, low = split(products[:, cols])
        which = hi_ref[:, cols]
        zero = jnp.zeros_like(high)
        keep = [which == h for h in range(own_blocks + ghost_blocks)]
        left = jnp.concatenate([jnp.where(k, high, zero) for k in keep], axis=0)
        right = jnp.concatenate([jnp.where(k, low, zero) for k in keep], axis=0)
        sums[...] += nt(left, onehot[:, cols]) + nt(right, onehot[:, cols])
        return carry

    def put_face(received):
        high, low = split(received)
        which = hi_face[...]
        zero = jnp.zeros_like(high)
        keep = [which == h for h in range(own_blocks)]
        left = jnp.concatenate([jnp.where(k, high, zero) for k in keep], axis=0)
        right = jnp.concatenate([jnp.where(k, low, zero) for k in keep], axis=0)
        return nt(left, onehot_face[...]) + nt(right, onehot_face[...])

    def put_ghost(values):
        for h in range(ghost_blocks):
            width = min(LO, face_pad - h * LO)
            xg[h * bands:(h + 1) * bands, 0:width] = values[:, h * LO:h * LO + width].astype(BF)

    own = slice(0, own_blocks * bands)

    def upper():
        parts = []
        for h in range(ghost_blocks):
            width = min(LO, face_pad - h * LO)
            start = (own_blocks + h) * bands
            parts.append(sums[start:start + bands, 0:width])
        return jnp.concatenate(parts, axis=1)

    xg[...] = jnp.zeros(xg.shape, BF)
    lax.fori_loop(0, elems, gather_own, 0)
    copy1.wait()
    put_ghost(got1[...])
    sums[...] = jnp.zeros(sums.shape, F32)
    lax.fori_loop(0, elems, multiply, 0)
    lax.fori_loop(0, elems, scatter_all, 0)

    send2[...] = upper()
    copy2 = remote(send2, got2, send_sem.at[1], recv_sem.at[1], above)
    copy2.start()
    partial_value = (sums[own, :] - CENTER * base[...]) / HALF_WIDTH
    field[...] = partial_value
    high, low = split(partial_value)
    send3[...] = take_face(high) + take_face(low)
    copy3 = remote(send3, got3, send_sem.at[2], recv_sem.at[2], below)
    copy3.start()
    copy2.wait()
    field[...] += put_face(got2[...] / HALF_WIDTH)
    xb[...] = field[...].astype(BF)
    lax.fori_loop(0, elems, gather_own, 0)
    copy3.wait()
    put_ghost(got3[...] + send2[...] / HALF_WIDTH)
    sums[...] = jnp.zeros(sums.shape, F32)
    lax.fori_loop(0, elems, multiply, 0)
    lax.fori_loop(0, elems, scatter_all, 0)

    send4[...] = upper()
    copy4 = remote(send4, got4, send_sem.at[3], recv_sem.at[3], above)
    copy4.start()
    partial_value = sums[own, :] - CENTER * field[...]
    copy4.wait()
    field[...] = 2.0 * ((partial_value + put_face(got4[...])) / HALF_WIDTH) - base[...]

    groups, _, width = out_ref.shape
    per = width // 128
    for piece in range(groups * per):
        dst = slice((piece % per) * 128, (piece % per + 1) * 128)
        if piece // 2 < own_blocks:
            rows = slice(piece // 2 * bands, (piece // 2 + 1) * bands)
            src = slice((piece % 2) * 128, (piece % 2 + 1) * 128)
            out_ref[piece // per, :, dst] = field[rows, src].astype(BF)
        else:
            out_ref[piece // per, :, dst] = jnp.zeros((bands, 128), BF)


def factor_inverse(mat):
    size, wide = mat.shape
    step = 8
    lane = lax.broadcasted_iota(jnp.int32, (step, 128), 1)
    sub = lax.broadcasted_iota(jnp.int32, (step, 128), 0)
    halves = wide // 128
    for start in range(0, size, step):
        tile, at = start // 128, start % 128
        block = [mat[start:start + step, t * 128:(t + 1) * 128] for t in range(halves)]
        head = block[tile]
        d = {}
        for j in range(step):
            column = jnp.broadcast_to(head[:, at + j:at + j + 1], (step, 128))
            for i in range(j, step):
                d[i, j] = jnp.broadcast_to(column[i:i + 1, :], (step, 128))
        inverse = []
        factor = {}
        for k in range(step):
            scale = lax.rsqrt(d[k, k])
            inverse.append(scale)
            for i in range(k + 1, step):
                factor[i, k] = d[i, k] * scale
            for i in range(k + 1, step):
                for m in range(k + 1, i + 1):
                    d[i, m] = d[i, m] - factor[i, k] * factor[m, k]
        inside = (lane >= at) & (lane < at + step)
        fresh = []
        for t in range(halves):
            rows = []
            result = jnp.zeros((step, 128), F32)
            for i in range(step):
                row = jnp.broadcast_to(block[t][i:i + 1, :], (step, 128))
                if t == tile:
                    row = jnp.where(inside, jnp.where(lane == at + i, 1.0, 0.0), row)
                for j in range(i):
                    row = row - factor[i, j] * rows[j]
                row = row * inverse[i]
                rows.append(row)
                result = jnp.where(sub == i, row, result)
            fresh.append(result)
        fresh = jnp.concatenate(fresh, axis=1)
        mat[start:start + step, :] = fresh
        if start + step < size:
            first = (start + step) // 128 * 128
            update = lax.dot_general(
                fresh[:, first:], fresh, TN, precision=lax.Precision.HIGHEST, preferred_element_type=F32
            )
            rest = mat[start + step:size, :]
            column = lax.broadcasted_iota(jnp.int32, rest.shape, 1)
            rest = jnp.where((column >= start) & (column < start + step), 0.0, rest)
            mat[start + step:size, :] = rest - update[start + step - first:size - first, :]


def tail_kernel(
    total_nodes, in_ref, out_ref,
    rows_all, gram, half_in, half, band_in, y_in, z_in, whole, mat, ortho, back,
    a_send, a_recv, c_send, c_recv, r_send, r_recv, y_send, y_recv, z_send, z_recv,
    g_send, g_recv, b_send, b_recv,
):
    groups, bands, width = in_ref.shape
    count = groups * bands
    wide = gram.shape[1]
    band = lax.axis_index("band")
    space = lax.axis_index("space")
    core = lax.rem(space, CORES)
    y = lax.rem(space // CORES, YS)
    z = space // (CORES * YS)

    def band_peer(d):
        return {"band": lax.rem(band + d, groups)}

    def y_peer(d):
        return {"space": (z * YS + lax.rem(y + d, YS)) * CORES + core}

    def z_peer(d):
        return {"space": (lax.rem(z + d, ZS) * YS + y) * CORES + core}

    twin = {"space": space + 1 - 2 * core}
    peers = [band_peer(d) for d in range(1, groups)]
    peers += [y_peer(d) for d in range(1, YS)]
    peers += [z_peer(d) for d in range(1, ZS)]
    peers.append(twin)
    barrier = pltpu.get_barrier_semaphore()
    for there in peers:
        pl.semaphore_signal(barrier, inc=1, device_id=there, device_id_type=MESH)
    rows_all[count:, :] = jnp.zeros((rows_all.shape[0] - count, width), BF)
    pl.semaphore_wait(barrier, len(peers))

    def finish(copies):
        for c in copies:
            c.wait()

    mine = pl.ds(pl.multiple_of(band * bands, bands), bands)
    copies = []
    for d in range(1, groups):
        there = band_peer(d)
        copies.append(remote(in_ref.at[there["band"]], rows_all.at[mine], a_send.at[d - 1], a_recv.at[d - 1], there))
        copies[-1].start()
    rows_all[mine, :] = in_ref[band]
    finish(copies)

    local = nt(rows_all[0:count, :], rows_all[...])
    gram[...] = local
    part = count // CORES
    theirs = pl.ds(pl.multiple_of((1 - core) * part, 8), part)
    ours = pl.ds(pl.multiple_of(core * part, 8), part)
    copy = remote(gram.at[theirs], half_in, c_send.at[0], c_recv.at[0], twin)
    copy.start()
    copy.wait()
    half[...] = (gram[ours, :] + half_in[...]).reshape(half.shape)

    copies = []
    for d in range(1, groups):
        there = band_peer(d)
        copies.append(remote(half.at[there["band"]], band_in.at[d - 1], r_send.at[d - 1], r_recv.at[d - 1], there))
        copies[-1].start()
    finish(copies)
    value = half[band]
    for d in range(1, groups):
        value = value + band_in[d - 1]
    y_in[y] = value

    copies = []
    for d in range(1, YS):
        copies.append(remote(y_in.at[y], y_in.at[y], y_send.at[d - 1], y_recv.at[d - 1], y_peer(d)))
        copies[-1].start()
    finish(copies)
    value = y_in[0]
    for k in range(1, YS):
        value = value + y_in[k]
    z_in[z] = value

    copies = []
    for d in range(1, ZS):
        copies.append(remote(z_in.at[z], z_in.at[z], z_send.at[d - 1], z_recv.at[d - 1], z_peer(d)))
        copies[-1].start()
    finish(copies)
    value = z_in[0]
    for k in range(1, ZS):
        value = value + z_in[k]
    whole[core, band] = value

    copies = []
    for d in range(1, groups):
        piece = whole.at[core, band]
        copies.append(remote(piece, piece, g_send.at[d - 1], g_recv.at[d - 1], band_peer(d)))
        copies[-1].start()
    finish(copies)
    copy = remote(whole.at[core], whole.at[core], c_send.at[1], c_recv.at[1], twin)
    copy.start()
    copy.wait()

    mat[...] = whole[...].reshape(count, wide) / total_nodes
    factor_inverse(mat)
    row = lax.broadcasted_iota(jnp.int32, (count, wide), 0)
    column = lax.broadcasted_iota(jnp.int32, (count, wide), 1)
    high, low = split(jnp.where(column <= row, mat[...], 0.0))
    filtered = rows_all[...]
    result = nn(high, filtered) + nn(low, filtered)
    ortho[...] = result.astype(BF).reshape(ortho.shape)

    copies = []
    for d in range(1, groups):
        there = band_peer(d)
        copies.append(remote(ortho.at[there["band"]], back.at[band], b_send.at[d - 1], b_recv.at[d - 1], there))
        copies[-1].start()
    back[band] = ortho[band]
    finish(copies)
    nodes = out_ref.shape[1]
    for k in range(groups):
        size = min(width, nodes - k * width)
        if size > 0:
            out_ref[:, k * width:k * width + size] = back[k, :, 0:size].astype(F32)


def per_device(psi, ham, conn, face_rows):
    bands, nodes = psi.shape
    elems = conn.shape[0]
    faces = face_rows.shape[0]
    groups = lax.axis_size("band")
    own_blocks = pl.cdiv(nodes, LO)
    ghost_blocks = pl.cdiv(faces, LO)
    face_pad = pl.cdiv(faces, 128) * 128
    width = pl.cdiv(pl.cdiv(nodes, 128), groups) * 128
    own = own_blocks * bands
    entries = elems * NODE_EL
    vmem = pl.BlockSpec(memory_space=pltpu.VMEM)
    dma = pltpu.SemaphoreType.DMA

    filtered = pl.pallas_call(
        filter_kernel,
        out_shape=jax.ShapeDtypeStruct((groups, bands, width), BF),
        in_specs=[vmem] * 4,
        out_specs=vmem,
        scratch_shapes=[
            pltpu.VMEM((LO, entries), BF),
            pltpu.VMEM((LO, face_pad), BF),
            pltpu.VMEM((bands, entries), jnp.int32),
            pltpu.VMEM((bands, face_pad), jnp.int32),
            pltpu.VMEM((own, LO), F32),
            pltpu.VMEM((own, LO), F32),
            pltpu.VMEM((own + ghost_blocks * bands, LO), F32),
            pltpu.VMEM((own, LO), BF),
            pltpu.VMEM((ghost_blocks * bands, LO), BF),
            pltpu.VMEM((bands, entries), BF),
            pltpu.VMEM((bands, entries), F32),
            pltpu.VMEM((bands, face_pad), BF),
            pltpu.VMEM((bands, face_pad), F32),
            pltpu.VMEM((bands, face_pad), F32),
            pltpu.VMEM((bands, face_pad), F32),
            pltpu.VMEM((bands, face_pad), BF),
            pltpu.VMEM((bands, face_pad), F32),
            pltpu.VMEM((bands, face_pad), F32),
            pltpu.VMEM((bands, face_pad), F32),
            dma((4,)),
            dma((4,)),
        ],
        compiler_params=pltpu.CompilerParams(
            collective_id=0, has_side_effects=True, vmem_limit_bytes=VMEM_LIMIT
        ),
        name="filter",
    )(psi, ham, conn, face_rows.reshape(1, faces))

    count = groups * bands
    wide = pl.cdiv(count, 128) * 128
    unit = count // CORES // groups
    return pl.pallas_call(
        functools.partial(tail_kernel, float(nodes * lax.axis_size("space"))),
        out_shape=jax.ShapeDtypeStruct((bands, nodes), F32),
        in_specs=[vmem],
        out_specs=vmem,
        scratch_shapes=[
            pltpu.VMEM((wide, width), BF),
            pltpu.VMEM((count, wide), F32),
            pltpu.VMEM((count // CORES, wide), F32),
            pltpu.VMEM((groups, unit, wide), F32),
            pltpu.VMEM((groups - 1, unit, wide), F32),
            pltpu.VMEM((YS, unit, wide), F32),
            pltpu.VMEM((ZS, unit, wide), F32),
            pltpu.VMEM((CORES, groups, unit, wide), F32),
            pltpu.VMEM((count, wide), F32),
            pltpu.VMEM((groups, bands, width), BF),
            pltpu.VMEM((groups, bands, width), BF),
            dma((groups - 1,)), dma((groups - 1,)),
            dma((2,)), dma((2,)),
            dma((groups - 1,)), dma((groups - 1,)),
            dma((YS - 1,)), dma((YS - 1,)),
            dma((ZS - 1,)), dma((ZS - 1,)),
            dma((groups - 1,)), dma((groups - 1,)),
            dma((groups - 1,)), dma((groups - 1,)),
        ],
        compiler_params=pltpu.CompilerParams(
            collective_id=1, has_side_effects=True, vmem_limit_bytes=VMEM_LIMIT
        ),
        name="tail",
    )(filtered)


def solution(mesh):
    placed = (P("band", "space"), P("space", None, None), P("space", None), P("space"))
    return jax.shard_map(
        per_device, mesh=mesh, in_specs=placed, out_specs=P("band", "space"), check_vma=False
    )
```

```python
import functools

import jax
import jax.numpy as jnp
from jax import lax
from jax.experimental import pallas as pl
from jax.experimental.pallas import tpu as pltpu
from jax.sharding import PartitionSpec as P

NODE_EL = 512
OWN_EL = 448
CENTER = 6.25
HALF_WIDTH = 7.5
LO = 256
TAIL = 128
MESH = pl.DeviceIdType.MESH
BF = jnp.bfloat16
F32 = jnp.float32
VMEM_LIMIT = 60 * 1024 * 1024

CORES, YS, ZS = 2, 8, 4
HAM_PARTS = 4
NT = (((1,), (1,)), ((), ()))
TN = (((0,), (0,)), ((), ()))


def nn(a, b):
    return jnp.dot(a, b, preferred_element_type=F32)


def nt(a, b):
    return lax.dot_general(a, b, NT, preferred_element_type=F32)


def remote(src, dst, send, recv, where):
    return pltpu.make_async_remote_copy(
        src_ref=src, dst_ref=dst, send_sem=send, recv_sem=recv, device_id=where, device_id_type=MESH
    )


def split(value):
    high = value.astype(BF)
    return high, (value - high.astype(F32)).astype(BF)


def split3(value):
    high = value.astype(BF)
    rest = value - high.astype(F32)
    middle = rest.astype(BF)
    return high, middle, (rest - middle.astype(F32)).astype(BF)


def lanes(start, size):
    return pl.ds(pl.multiple_of(start, 128), size)


def pick(table, which, first, count, total):
    bands = total.shape[0]
    for h in range(count):
        total = jnp.where(which == first + h, table[h * bands:(h + 1) * bands, :], total)
    return total


def place(parts, which, first, count, columns):
    zero = jnp.zeros_like(parts[0])
    keep = [which == first + h for h in range(count)]
    rows = [jnp.where(k, part, zero) for part in parts for k in keep]
    result = nt(jnp.concatenate(rows, axis=0), columns)
    size = result.shape[0] // len(parts)
    return sum(result[n * size:(n + 1) * size] for n in range(1, len(parts))) + result[0:size]


def indicator(low, depth):
    shape = depth.shape
    return jnp.where(depth == jnp.broadcast_to(low, shape), jnp.ones(shape, BF), jnp.zeros(shape, BF))


def as_bf(value, rows):
    return jnp.broadcast_to(value.astype(F32), (rows, value.shape[1])).astype(BF)


def factor_inverse(mat, panel=32):
    size, wide = mat.shape
    step = 8
    lane = lax.broadcasted_iota(jnp.int32, (step, 128), 1)
    sub = lax.broadcasted_iota(jnp.int32, (step, 128), 0)
    tiles = range(wide // 128)

    def spread_lane(value, j):
        return jnp.broadcast_to(value[:, j:j + 1], (step, 128))

    def spread_row(value, i):
        return jnp.broadcast_to(value[i:i + 1, :], (step, 128))

    for top in range(0, size, panel):
        groups = min(panel, size - top) // step
        block = [
            [mat[top + step * g:top + step * (g + 1), t * 128:(t + 1) * 128] for t in tiles] for g in range(groups)
        ]
        for s in range(groups):
            start = top + step * s
            tile, at = start // 128, start % 128
            columns = [spread_lane(block[s][tile], at + j) for j in range(step)]
            d = {(i, j): spread_row(columns[j], i) for j in range(step) for i in range(j, step)}
            below = [[spread_lane(block[g][tile], at + j) for j in range(step)] for g in range(s + 1, groups)]
            inside = (lane >= at) & (lane < at + step)
            base = [[spread_row(block[s][t], i) for i in range(step)] for t in tiles]
            for i in range(step):
                base[tile][i] = jnp.where(inside, jnp.where(lane == at + i, 1.0, 0.0), base[tile][i])
            rows = [[] for _ in tiles]
            for k in range(step):
                scale = lax.rsqrt(d[k, k])
                factor = {i: d[i, k] * scale for i in range(k + 1, step)}
                for i in range(k + 1, step):
                    for m in range(k + 1, i + 1):
                        d[i, m] = d[i, m] - factor[i] * factor[m]
                for t in tiles:
                    rows[t].append(base[t][k] * scale)
                    for i in range(k + 1, step):
                        base[t][i] = base[t][i] - factor[i] * rows[t][k]
                for part in below:
                    part[k] = part[k] * scale
                    for i in range(k + 1, step):
                        part[i] = part[i] - part[k] * factor[i]
            for t in tiles:
                fresh = rows[t][0]
                for i in range(1, step):
                    fresh = jnp.where(sub == i, rows[t][i], fresh)
                block[s][t] = fresh
            for n, g in enumerate(range(s + 1, groups)):
                for t in tiles:
                    value = block[g][t]
                    if t == tile:
                        value = jnp.where(inside, 0.0, value)
                    for k in range(step):
                        value = value - below[n][k] * rows[t][k]
                    block[g][t] = value
        for g in range(groups):
            for t in tiles:
                mat[top + step * g:top + step * (g + 1), t * 128:(t + 1) * 128] = block[g][t]
        end = top + step * groups
        if end < size:
            first = end // 128 * 128
            fresh = mat[top:end, :]
            row = top + lax.broadcasted_iota(jnp.int32, fresh.shape, 0)
            column = lax.broadcasted_iota(jnp.int32, fresh.shape, 1)
            a, b, c = split3(fresh[:, first:])
            d, e, f = split3(jnp.where((column > row) & (column < end), 0.0, fresh))
            update = lax.dot_general(
                jnp.concatenate([a, a, b, b, a, c], axis=0),
                jnp.concatenate([d, e, d, e, f, d], axis=0),
                TN,
                preferred_element_type=F32,
            )
            rest = mat[end:size, :]
            column = lax.broadcasted_iota(jnp.int32, rest.shape, 1)
            rest = jnp.where((column >= top) & (column < end), 0.0, rest)
            mat[end:size, :] = rest - update[end - first:size - first, :]


def step_kernel(
    total_nodes, psi_ref, ham_hbm, conn_ref, face_ref, out_ref,
    ham, onehot, onehot_ghost, onehot_face, hi_ref, hi_ghost, hi_face, base, field, xb, xg,
    gathered, high_ref, low_ref,
    send1, send2, send3, send4, got1, got2, got3, got4,
    pieces, rows_all, gram, half_in, half, band_in, y_in, z_in, whole, mat, ortho,
    ham_sem, own_sem, f_send, f_recv, a_send, a_recv, c_send, c_recv, r_send, r_recv, y_send, y_recv, z_send, z_recv,
    g_send, g_recv, t_send, t_recv, b_send, b_recv,
):
    bands, nodes = psi_ref.shape
    elems = conn_ref.shape[0]
    faces = face_ref.shape[0]
    own_blocks = pl.cdiv(nodes, LO)
    ghost_blocks = pl.cdiv(faces, LO)
    face_pad = got1.shape[1]
    shift = own_blocks * LO - nodes
    domains = lax.axis_size("space")
    space = lax.axis_index("space")
    band = lax.axis_index("band")
    groups, _, width = pieces.shape
    count = groups * bands
    wide = mat.shape[1]
    core = lax.rem(space, CORES)
    y = lax.rem(space // CORES, YS)
    z = space // (CORES * YS)
    below = {"space": lax.rem(space + domains - 1, domains)}
    above = {"space": lax.rem(space + 1, domains)}
    twin = {"space": space + 1 - 2 * core}

    def band_peer(d):
        return {"band": lax.rem(band + d, groups)}

    def y_peer(d):
        return {"space": (z * YS + lax.rem(y + d, YS)) * CORES + core}

    def z_peer(d):
        return {"space": (lax.rem(z + d, ZS) * YS + y) * CORES + core}

    peers = [below, above, twin]
    peers += [band_peer(d) for d in range(1, groups)]
    peers += [y_peer(d) for d in range(1, YS)]
    peers += [z_peer(d) for d in range(1, ZS)]
    barrier = pltpu.get_barrier_semaphore()
    for there in peers:
        pl.semaphore_signal(barrier, inc=1, device_id=there, device_id_type=MESH)

    per = elems // HAM_PARTS
    ham_copies = []
    for k in range(HAM_PARTS):
        part = slice(k * per, (k + 1) * per)
        ham_copies.append(pltpu.make_async_copy(ham_hbm.at[part], ham.at[part], ham_sem.at[k]))
        ham_copies[-1].start()

    for h in range(own_blocks):
        rows = slice(h * bands, (h + 1) * bands)
        if (h + 1) * LO <= nodes:
            value = psi_ref[:, h * LO:(h + 1) * LO]
            base[rows, :] = value
            xb[rows, :] = value.astype(BF)
        else:
            base[rows, :] = jnp.zeros((bands, LO), F32)
            base[rows, 0:nodes - h * LO] = psi_ref[:, h * LO:nodes]
            xb[rows, :] = base[rows, :].astype(BF)

    depth = lax.broadcasted_iota(jnp.int32, (LO, NODE_EL), 0).astype(F32).astype(BF)
    for k in range(face_pad // 128):
        size = min(128, faces - k * 128)
        named = jnp.full((1, 128), -1, jnp.int32)
        spot = lax.broadcasted_iota(jnp.int32, (1, 128), 1)
        if size == 128:
            named = face_ref[k * 128:(k + 1) * 128].reshape(1, 128)
        else:
            tail = face_ref[faces - 128:faces].reshape(1, 128)
            named = jnp.where(spot < size, pltpu.roll(tail, size, 1), -1)
        cols = slice(k * 128, (k + 1) * 128)
        onehot_face[:, cols] = indicator(as_bf(named & (LO - 1), 1), depth[:, 0:128])
        hi_face[:, cols] = as_bf(named >> 8, bands)

    def take_face(blocks):
        table = nn(blocks, onehot_face[...]).astype(BF)
        return pick(table, hi_face[...], 0, own_blocks, jnp.zeros((bands, face_pad), BF))

    send1[...] = take_face(xb[...])
    pl.semaphore_wait(barrier, len(peers))
    copy1 = remote(send1, got1, f_send.at[0], f_recv.at[0], below)
    copy1.start()

    spot = lax.broadcasted_iota(jnp.int32, (1, NODE_EL), 1)

    def prepare(e, carry):
        named = conn_ref[pl.ds(e, 1), :]
        named = jnp.where(spot >= OWN_EL, named + shift, named)
        marks = indicator(as_bf(named & (LO - 1), 1), depth)
        which = as_bf(named >> 8, bands)
        cols = lanes(e * NODE_EL, NODE_EL)
        onehot[:, cols] = marks
        hi_ref[:, cols] = which
        cols = lanes(e * TAIL, TAIL)
        onehot_ghost[:, cols] = marks[:, NODE_EL - TAIL:]
        hi_ghost[:, cols] = which[:, NODE_EL - TAIL:]
        return carry

    lax.fori_loop(0, elems, prepare, 0, unroll=2)
    xg[...] = jnp.zeros(xg.shape, BF)
    rows_all[count:, :] = jnp.zeros((rows_all.shape[0] - count, width), BF)

    def gather_own():
        def body(e, carry):
            cols = lanes(e * NODE_EL, NODE_EL)
            table = nn(xb[...], onehot[:, cols]).astype(BF)
            gathered[:, cols] = pick(table, hi_ref[:, cols], 0, own_blocks, jnp.zeros((bands, NODE_EL), BF))
            return carry

        lax.fori_loop(0, elems, body, 0, unroll=4)

    def gather_ghost(values):
        for h in range(ghost_blocks):
            size = min(LO, face_pad - h * LO)
            xg[h * bands:(h + 1) * bands, 0:size] = values[:, h * LO:h * LO + size].astype(BF)
        table = nn(xg[...], onehot_ghost[...]).astype(BF)
        found = pick(table, hi_ghost[...], own_blocks, ghost_blocks, jnp.zeros((bands, elems * TAIL), BF))
        for e in range(elems):
            cols = slice((e + 1) * NODE_EL - TAIL, (e + 1) * NODE_EL)
            gathered[:, cols] = gathered[:, cols] + found[:, e * TAIL:(e + 1) * TAIL]

    def multiply():
        def body(e, carry):
            cols = lanes(e * NODE_EL, NODE_EL)
            high_ref[:, cols], low_ref[:, cols] = split(nn(gathered[:, cols], ham[e]))
            return carry

        lax.fori_loop(0, elems, body, 0, unroll=4)

    def upper():
        cols = [slice((e + 1) * NODE_EL - TAIL, (e + 1) * NODE_EL) for e in range(elems)]
        high = jnp.concatenate([high_ref[:, c] for c in cols], axis=1)
        low = jnp.concatenate([low_ref[:, c] for c in cols], axis=1)
        total = place([high, low], hi_ghost[...], own_blocks, ghost_blocks, onehot_ghost[...])
        parts = [
            total[h * bands:(h + 1) * bands, 0:min(LO, face_pad - h * LO)] for h in range(ghost_blocks)
        ]
        return jnp.concatenate(parts, axis=1)

    def scatter_own():
        half_cols = elems * NODE_EL // 2
        total = None
        for k in range(2):
            cols = slice(k * half_cols, (k + 1) * half_cols)
            value = place([high_ref[:, cols], low_ref[:, cols]], hi_ref[:, cols], 0, own_blocks, onehot[:, cols])
            total = value if total is None else total + value
        return total

    def put_face(received):
        return place(list(split(received)), hi_face[...], 0, own_blocks, onehot_face[...])

    gather_own()
    copy1.wait()
    gather_ghost(got1[...])
    for c in ham_copies:
        c.wait()
    multiply()
    send2[...] = upper()
    copy2 = remote(send2, got2, f_send.at[1], f_recv.at[1], above)
    copy2.start()
    partial_value = (scatter_own() - CENTER * base[...]) / HALF_WIDTH
    field[...] = partial_value
    high, low = split(partial_value)
    send3[...] = take_face(high).astype(F32) + take_face(low).astype(F32)
    copy3 = remote(send3, got3, f_send.at[2], f_recv.at[2], below)
    copy3.start()
    copy2.wait()
    field[...] += put_face(got2[...] / HALF_WIDTH)
    xb[...] = field[...].astype(BF)
    gather_own()
    copy3.wait()
    gather_ghost(got3[...] + send2[...] / HALF_WIDTH)
    multiply()
    send4[...] = upper()
    copy4 = remote(send4, got4, f_send.at[3], f_recv.at[3], above)
    copy4.start()
    partial_value = scatter_own() - CENTER * field[...]
    copy4.wait()
    field[...] = 2.0 * ((partial_value + put_face(got4[...])) / HALF_WIDTH) - base[...]

    blocks = width // 128
    for piece in range(groups * blocks):
        dst = slice((piece % blocks) * 128, (piece % blocks + 1) * 128)
        if piece // 2 < own_blocks:
            rows = slice(piece // 2 * bands, (piece // 2 + 1) * bands)
            src = slice((piece % 2) * 128, (piece % 2 + 1) * 128)
            pieces[piece // blocks, :, dst] = field[rows, src].astype(BF)
        else:
            pieces[piece // blocks, :, dst] = jnp.zeros((bands, 128), BF)

    def finish(copies):
        for c in copies:
            c.wait()

    mine = pl.ds(pl.multiple_of(band * bands, bands), bands)
    copies = []
    for d in range(1, groups):
        there = band_peer(d)
        copies.append(remote(pieces.at[there["band"]], rows_all.at[mine], a_send.at[d - 1], a_recv.at[d - 1], there))
        copies[-1].start()
    rows_all[mine, :] = pieces[band]
    finish(copies)

    part = count // CORES
    theirs = pl.ds(pl.multiple_of((1 - core) * part, 16), part)
    ours = pl.ds(pl.multiple_of(core * part, 16), part)
    gram[0] = nt(rows_all[theirs, :], rows_all[...])
    copy = remote(gram.at[0], half_in, c_send.at[0], c_recv.at[0], twin)
    copy.start()
    gram[1] = nt(rows_all[ours, :], rows_all[...])
    copy.wait()
    half[...] = (gram[1] + half_in[...]).reshape(half.shape)

    copies = []
    for d in range(1, groups):
        there = band_peer(d)
        copies.append(remote(half.at[there["band"]], band_in.at[d - 1], r_send.at[d - 1], r_recv.at[d - 1], there))
        copies[-1].start()
    finish(copies)
    value = half[band]
    for d in range(1, groups):
        value = value + band_in[d - 1]
    y_in[y] = value

    copies = []
    for d in range(1, YS):
        copies.append(remote(y_in.at[y], y_in.at[y], y_send.at[d - 1], y_recv.at[d - 1], y_peer(d)))
        copies[-1].start()
    finish(copies)
    value = y_in[0]
    for k in range(1, YS):
        value = value + y_in[k]
    z_in[z] = value

    copies = []
    for d in range(1, ZS):
        copies.append(remote(z_in.at[z], z_in.at[z], z_send.at[d - 1], z_recv.at[d - 1], z_peer(d)))
        copies[-1].start()
    finish(copies)
    value = z_in[0]
    for k in range(1, ZS):
        value = value + z_in[k]
    whole[core, band] = value

    copies = {}
    piece = whole.at[core, band]
    for d in range(1, groups):
        copies[d] = remote(piece, piece, g_send.at[d - 1], g_recv.at[d - 1], band_peer(d))
        copies[d].start()
    forwarded = [remote(piece, piece, t_send.at[0], t_recv.at[0], twin)]
    forwarded[0].start()
    for d in sorted(copies, key=lambda d: (min(d, groups - d) not in (1, 3), d)):
        copies[d].wait_recv()
        piece = whole.at[core, lax.rem(band + groups - d, groups)]
        forwarded.append(remote(piece, piece, t_send.at[d], t_recv.at[d], twin))
        forwarded[-1].start()
    for d in copies:
        copies[d].wait_send()
    finish(forwarded)

    mat[...] = whole[...].reshape(count, wide) / total_nodes
    factor_inverse(mat)
    row = lax.broadcasted_iota(jnp.int32, (count, wide), 0)
    column = lax.broadcasted_iota(jnp.int32, (count, wide), 1)
    high, low = split(jnp.where(column <= row, mat[...], 0.0))
    filtered = rows_all[...]
    result = nn(high, filtered) + nn(low, filtered)
    ortho[...] = result.astype(BF).reshape(ortho.shape)

    copies = []
    landing = out_ref.at[:, lanes(band * width, width)]
    for d in range(1, groups):
        there = band_peer(d)
        copies.append(remote(ortho.at[there["band"]], landing, b_send.at[d - 1], b_recv.at[d - 1], there))
        copies[-1].start()
    copy = pltpu.make_async_copy(ortho.at[band], landing, own_sem)
    copy.start()
    copy.wait()
    finish(copies)


def per_device(psi, ham, conn, face_rows):
    bands, nodes = psi.shape
    elems = conn.shape[0]
    faces = face_rows.shape[0]
    groups = lax.axis_size("band")
    own_blocks = pl.cdiv(nodes, LO)
    ghost_blocks = pl.cdiv(faces, LO)
    face_pad = pl.cdiv(faces, 128) * 128
    width = pl.cdiv(pl.cdiv(nodes, 128), groups) * 128
    own = own_blocks * bands
    entries = elems * NODE_EL
    count = groups * bands
    wide = pl.cdiv(count, 128) * 128
    unit = count // CORES // groups
    vmem = pl.BlockSpec(memory_space=pltpu.VMEM)
    anywhere = pl.BlockSpec(memory_space=pl.ANY)
    dma = pltpu.SemaphoreType.DMA

    result = pl.pallas_call(
        functools.partial(step_kernel, float(nodes * lax.axis_size("space"))),
        out_shape=jax.ShapeDtypeStruct((bands, groups * width), BF),
        in_specs=[vmem, anywhere, vmem, vmem],
        out_specs=anywhere,
        scratch_shapes=[
            pltpu.VMEM(ham.shape, BF),
            pltpu.VMEM((LO, entries), BF),
            pltpu.VMEM((LO, elems * TAIL), BF),
            pltpu.VMEM((LO, face_pad), BF),
            pltpu.VMEM((bands, entries), BF),
            pltpu.VMEM((bands, elems * TAIL), BF),
            pltpu.VMEM((bands, face_pad), BF),
            pltpu.VMEM((own, LO), F32),
            pltpu.VMEM((own, LO), F32),
            pltpu.VMEM((own, LO), BF),
            pltpu.VMEM((ghost_blocks * bands, LO), BF),
            pltpu.VMEM((bands, entries), BF),
            pltpu.VMEM((bands, entries), BF),
            pltpu.VMEM((bands, entries), BF),
            pltpu.VMEM((bands, face_pad), BF),
            pltpu.VMEM((bands, face_pad), F32),
            pltpu.VMEM((bands, face_pad), F32),
            pltpu.VMEM((bands, face_pad), F32),
            pltpu.VMEM((bands, face_pad), BF),
            pltpu.VMEM((bands, face_pad), F32),
            pltpu.VMEM((bands, face_pad), F32),
            pltpu.VMEM((bands, face_pad), F32),
            pltpu.VMEM((groups, bands, width), BF),
            pltpu.VMEM((wide, width), BF),
            pltpu.VMEM((CORES, count // CORES, wide), F32),
            pltpu.VMEM((count // CORES, wide), F32),
            pltpu.VMEM((groups, unit, wide), F32),
            pltpu.VMEM((groups - 1, unit, wide), F32),
            pltpu.VMEM((YS, unit, wide), F32),
            pltpu.VMEM((ZS, unit, wide), F32),
            pltpu.VMEM((CORES, groups, unit, wide), F32),
            pltpu.VMEM((count, wide), F32),
            pltpu.VMEM((groups, bands, width), BF),
            dma((HAM_PARTS,)), dma,
            dma((4,)), dma((4,)),
            dma((groups - 1,)), dma((groups - 1,)),
            dma((1,)), dma((1,)),
            dma((groups - 1,)), dma((groups - 1,)),
            dma((YS - 1,)), dma((YS - 1,)),
            dma((ZS - 1,)), dma((ZS - 1,)),
            dma((groups - 1,)), dma((groups - 1,)),
            dma((groups,)), dma((groups,)),
            dma((groups - 1,)), dma((groups - 1,)),
        ],
        compiler_params=pltpu.CompilerParams(
            collective_id=0, has_side_effects=True, vmem_limit_bytes=VMEM_LIMIT
        ),
        name="step",
    )(psi, ham, conn, face_rows)
    return result[:, 0:nodes].astype(F32)


def solution(mesh):
    placed = (P("band", "space"), P("space", None, None), P("space", None), P("space"))
    return jax.shard_map(
        per_device, mesh=mesh, in_specs=placed, out_specs=P("band", "space"), check_vma=False
    )
```

```python
import functools

import jax
import jax.numpy as jnp
from jax import lax
from jax.experimental import pallas as pl
from jax.experimental.pallas import tpu as pltpu
from jax.sharding import PartitionSpec as P

NODE_EL = 512
OWN_EL = 448
CENTER = 6.25
HALF_WIDTH = 7.5
LO = 256
TAIL = 128
MESH = pl.DeviceIdType.MESH
BF = jnp.bfloat16
F32 = jnp.float32
VMEM_LIMIT = 60 * 1024 * 1024

CORES, YS, ZS = 2, 8, 4
HAM_PARTS = 4
NT = (((1,), (1,)), ((), ()))
TN = (((0,), (0,)), ((), ()))


def nn(a, b):
    return jnp.dot(a, b, preferred_element_type=F32)


def nt(a, b):
    return lax.dot_general(a, b, NT, preferred_element_type=F32)


def remote(src, dst, send, recv, where):
    return pltpu.make_async_remote_copy(
        src_ref=src, dst_ref=dst, send_sem=send, recv_sem=recv, device_id=where, device_id_type=MESH
    )


def split(value):
    high = value.astype(BF)
    return high, (value - high.astype(F32)).astype(BF)


def split3(value):
    high = value.astype(BF)
    rest = value - high.astype(F32)
    middle = rest.astype(BF)
    return high, middle, (rest - middle.astype(F32)).astype(BF)


def lanes(start, size):
    return pl.ds(pl.multiple_of(start, 128), size)


def pick(table, which, first, count, total):
    bands = total.shape[0]
    for h in range(count):
        total = jnp.where(which == first + h, table[h * bands:(h + 1) * bands, :], total)
    return total


def place(parts, which, first, count, columns):
    zero = jnp.zeros_like(parts[0])
    keep = [which == first + h for h in range(count)]
    rows = [jnp.where(k, part, zero) for part in parts for k in keep]
    result = nt(jnp.concatenate(rows, axis=0), columns)
    size = result.shape[0] // len(parts)
    return sum(result[n * size:(n + 1) * size] for n in range(1, len(parts))) + result[0:size]


def indicator(low, depth):
    shape = depth.shape
    return jnp.where(depth == jnp.broadcast_to(low, shape), jnp.ones(shape, BF), jnp.zeros(shape, BF))


def as_bf(value, rows):
    return jnp.broadcast_to(value.astype(F32), (rows, value.shape[1])).astype(BF)


def factor_inverse(mat, panel, beside, after):
    size, wide = mat.shape
    step = 8
    lane = lax.broadcasted_iota(jnp.int32, (step, 128), 1)
    sub = lax.broadcasted_iota(jnp.int32, (step, 128), 0)
    tiles = range(wide // 128)

    def spread_lane(value, j):
        return jnp.broadcast_to(value[:, j:j + 1], (step, 128))

    def spread_row(value, i):
        return jnp.broadcast_to(value[i:i + 1, :], (step, 128))

    for top in range(0, size, panel):
        if top > 0:
            beside(top - panel, top)
        groups = min(panel, size - top) // step
        block = [
            [mat[top + step * g:top + step * (g + 1), t * 128:(t + 1) * 128] for t in tiles] for g in range(groups)
        ]
        for s in range(groups):
            start = top + step * s
            tile, at = start // 128, start % 128
            columns = [spread_lane(block[s][tile], at + j) for j in range(step)]
            d = {(i, j): spread_row(columns[j], i) for j in range(step) for i in range(j, step)}
            below = [[spread_lane(block[g][tile], at + j) for j in range(step)] for g in range(s + 1, groups)]
            inside = (lane >= at) & (lane < at + step)
            base = [[spread_row(block[s][t], i) for i in range(step)] for t in tiles]
            for i in range(step):
                base[tile][i] = jnp.where(inside, jnp.where(lane == at + i, 1.0, 0.0), base[tile][i])
            rows = [[] for _ in tiles]
            for k in range(step):
                scale = lax.rsqrt(d[k, k])
                factor = {i: d[i, k] * scale for i in range(k + 1, step)}
                for i in range(k + 1, step):
                    for m in range(k + 1, i + 1):
                        d[i, m] = d[i, m] - factor[i] * factor[m]
                for t in tiles:
                    rows[t].append(base[t][k] * scale)
                    for i in range(k + 1, step):
                        base[t][i] = base[t][i] - factor[i] * rows[t][k]
                for part in below:
                    part[k] = part[k] * scale
                    for i in range(k + 1, step):
                        part[i] = part[i] - part[k] * factor[i]
            for t in tiles:
                fresh = rows[t][0]
                for i in range(1, step):
                    fresh = jnp.where(sub == i, rows[t][i], fresh)
                block[s][t] = fresh
            for n, g in enumerate(range(s + 1, groups)):
                for t in tiles:
                    value = block[g][t]
                    if t == tile:
                        value = jnp.where(inside, 0.0, value)
                    for k in range(step):
                        value = value - below[n][k] * rows[t][k]
                    block[g][t] = value
        for g in range(groups):
            for t in tiles:
                mat[top + step * g:top + step * (g + 1), t * 128:(t + 1) * 128] = block[g][t]
        end = top + step * groups
        if end < size:
            first = end // 128 * 128
            fresh = mat[top:end, :]
            row = top + lax.broadcasted_iota(jnp.int32, fresh.shape, 0)
            column = lax.broadcasted_iota(jnp.int32, fresh.shape, 1)
            a, b, c = split3(fresh[:, first:])
            d, e, f = split3(jnp.where((column > row) & (column < end), 0.0, fresh))
            update = lax.dot_general(
                jnp.concatenate([a, a, b, b, a, c], axis=0),
                jnp.concatenate([d, e, d, e, f, d], axis=0),
                TN,
                preferred_element_type=F32,
            )
            rest = mat[end:size, :]
            column = lax.broadcasted_iota(jnp.int32, rest.shape, 1)
            rest = jnp.where((column >= top) & (column < end), 0.0, rest)
            mat[end:size, :] = rest - update[end - first:size - first, :]
        if top > 0:
            after(top - panel, top)


def fold(matrix):
    half = matrix.shape[0] // 2
    upper, lower = matrix[0:half, :], matrix[half:, :]
    row = lax.broadcasted_iota(jnp.int32, lower.shape, 0)
    lane = lax.broadcasted_iota(jnp.int32, lower.shape, 1)
    diagonal = jnp.sum(jnp.where(lane == row + half, lower, 0.0), axis=1, keepdims=True)
    mixed = jnp.where((lane >= half) & (lane - half <= row), pltpu.roll(upper, half, 1), lower)
    return jnp.where(lane < 2 * half, mixed, diagonal)


def unfold(folded):
    half, wide = folded.shape
    row = lax.broadcasted_iota(jnp.int32, folded.shape, 0)
    lane = lax.broadcasted_iota(jnp.int32, folded.shape, 1)
    diagonal = jnp.broadcast_to(folded[:, 2 * half:2 * half + 1], folded.shape)
    mixed = pltpu.roll(folded, wide - half, 1)
    zeros = jnp.zeros((128 - half, 128), F32)

    def flip(value):
        square = jnp.concatenate([value[:, 0:128], zeros], axis=0).T[0:half, :]
        return jnp.concatenate([square, jnp.zeros((half, wide - 128), F32)], axis=1)

    other = flip(jnp.where(lane < half, mixed, 0.0))
    corner = flip(jnp.where(lane < half, folded, 0.0))
    first = jnp.where(lane < half, jnp.where(lane <= row, mixed, other), pltpu.roll(corner, half, 1))
    last = jnp.where(lane == row, diagonal, jnp.where(lane > row, mixed, other))
    last = jnp.where(lane < half, folded, pltpu.roll(last, half, 1))
    inside = lane < 2 * half
    return jnp.where(inside, first, 0.0), jnp.where(inside, last, 0.0)


def step_kernel(
    total_nodes, psi_ref, ham_hbm, conn_ref, face_ref, out_ref,
    ham, onehot, onehot_ghost, onehot_face, hi_ref, hi_ghost, hi_face, base, field, xb, xg,
    gathered, high_ref, low_ref,
    send1, send2, send3, send4, got1, got2, got3, got4,
    pieces, rows_all, gram, group_in, y_in, z_in, whole, mat, ortho,
    ham_sem, own_sem, f_send, f_recv, a_send, a_recv, r_send, r_recv, y_send, y_recv, z_send, z_recv,
    g_send, g_recv, b_send, b_recv,
):
    bands, nodes = psi_ref.shape
    elems = conn_ref.shape[0]
    faces = face_ref.shape[0]
    own_blocks = pl.cdiv(nodes, LO)
    ghost_blocks = pl.cdiv(faces, LO)
    face_pad = got1.shape[1]
    shift = own_blocks * LO - nodes
    domains = lax.axis_size("space")
    space = lax.axis_index("space")
    band = lax.axis_index("band")
    groups, _, width = pieces.shape
    count = groups * bands
    wide = mat.shape[1]
    core = lax.rem(space, CORES)
    y = lax.rem(space // CORES, YS)
    z = space // (CORES * YS)
    below = {"space": lax.rem(space + domains - 1, domains)}
    above = {"space": lax.rem(space + 1, domains)}
    twin = {"space": space + 1 - 2 * core}

    def band_peer(d):
        return {"band": lax.rem(band + d, groups)}

    def y_peer(d):
        return {"space": (z * YS + lax.rem(y + d, YS)) * CORES + core}

    def z_peer(d):
        return {"space": (lax.rem(z + d, ZS) * YS + y) * CORES + core}

    def group_peer(c, d):
        there = {"band": lax.rem(band + d, groups)}
        if c > 0:
            there["space"] = twin["space"]
        return there

    members = [(c, d) for c in range(CORES) for d in range(groups) if c + d > 0]
    peers = [below, above]
    peers += [group_peer(c, d) for c, d in members]
    peers += [y_peer(d) for d in range(1, YS)]
    peers += [z_peer(d) for d in range(1, ZS)]
    barrier = pltpu.get_barrier_semaphore()
    for there in peers:
        pl.semaphore_signal(barrier, inc=1, device_id=there, device_id_type=MESH)

    per = elems // HAM_PARTS
    ham_copies = []
    for k in range(HAM_PARTS):
        part = slice(k * per, (k + 1) * per)
        ham_copies.append(pltpu.make_async_copy(ham_hbm.at[part], ham.at[part], ham_sem.at[k]))
        ham_copies[-1].start()

    for h in range(own_blocks):
        rows = slice(h * bands, (h + 1) * bands)
        if (h + 1) * LO <= nodes:
            value = psi_ref[:, h * LO:(h + 1) * LO]
            base[rows, :] = value
            xb[rows, :] = value.astype(BF)
        else:
            base[rows, :] = jnp.zeros((bands, LO), F32)
            base[rows, 0:nodes - h * LO] = psi_ref[:, h * LO:nodes]
            xb[rows, :] = base[rows, :].astype(BF)

    depth = lax.broadcasted_iota(jnp.int32, (LO, NODE_EL), 0).astype(F32).astype(BF)
    for k in range(face_pad // 128):
        size = min(128, faces - k * 128)
        named = jnp.full((1, 128), -1, jnp.int32)
        spot = lax.broadcasted_iota(jnp.int32, (1, 128), 1)
        if size == 128:
            named = face_ref[k * 128:(k + 1) * 128].reshape(1, 128)
        else:
            tail = face_ref[faces - 128:faces].reshape(1, 128)
            named = jnp.where(spot < size, pltpu.roll(tail, size, 1), -1)
        cols = slice(k * 128, (k + 1) * 128)
        onehot_face[:, cols] = indicator(as_bf(named & (LO - 1), 1), depth[:, 0:128])
        hi_face[:, cols] = as_bf(named >> 8, bands)

    def take_face(blocks):
        table = nn(blocks, onehot_face[...]).astype(BF)
        return pick(table, hi_face[...], 0, own_blocks, jnp.zeros((bands, face_pad), BF))

    send1[...] = take_face(xb[...])
    pl.semaphore_wait(barrier, len(peers))
    copy1 = remote(send1, got1, f_send.at[0], f_recv.at[0], below)
    copy1.start()

    spot = lax.broadcasted_iota(jnp.int32, (1, NODE_EL), 1)

    def prepare(e, carry):
        named = conn_ref[pl.ds(e, 1), :]
        named = jnp.where(spot >= OWN_EL, named + shift, named)
        marks = indicator(as_bf(named & (LO - 1), 1), depth)
        which = as_bf(named >> 8, bands)
        cols = lanes(e * NODE_EL, NODE_EL)
        onehot[:, cols] = marks
        hi_ref[:, cols] = which
        cols = lanes(e * TAIL, TAIL)
        onehot_ghost[:, cols] = marks[:, NODE_EL - TAIL:]
        hi_ghost[:, cols] = which[:, NODE_EL - TAIL:]
        return carry

    lax.fori_loop(0, elems, prepare, 0, unroll=2)
    xg[...] = jnp.zeros(xg.shape, BF)
    rows_all[count:, :] = jnp.zeros((rows_all.shape[0] - count, width), BF)

    def gather_own():
        def body(e, carry):
            cols = lanes(e * NODE_EL, NODE_EL)
            table = nn(xb[...], onehot[:, cols]).astype(BF)
            gathered[:, cols] = pick(table, hi_ref[:, cols], 0, own_blocks, jnp.zeros((bands, NODE_EL), BF))
            return carry

        lax.fori_loop(0, elems, body, 0, unroll=4)

    def gather_ghost(values):
        for h in range(ghost_blocks):
            size = min(LO, face_pad - h * LO)
            xg[h * bands:(h + 1) * bands, 0:size] = values[:, h * LO:h * LO + size].astype(BF)
        table = nn(xg[...], onehot_ghost[...]).astype(BF)
        found = pick(table, hi_ghost[...], own_blocks, ghost_blocks, jnp.zeros((bands, elems * TAIL), BF))
        for e in range(elems):
            cols = slice((e + 1) * NODE_EL - TAIL, (e + 1) * NODE_EL)
            gathered[:, cols] = gathered[:, cols] + found[:, e * TAIL:(e + 1) * TAIL]

    def multiply():
        def body(e, carry):
            cols = lanes(e * NODE_EL, NODE_EL)
            high_ref[:, cols], low_ref[:, cols] = split(nn(gathered[:, cols], ham[e]))
            return carry

        lax.fori_loop(0, elems, body, 0, unroll=4)

    def upper():
        cols = [slice((e + 1) * NODE_EL - TAIL, (e + 1) * NODE_EL) for e in range(elems)]
        high = jnp.concatenate([high_ref[:, c] for c in cols], axis=1)
        low = jnp.concatenate([low_ref[:, c] for c in cols], axis=1)
        total = place([high, low], hi_ghost[...], own_blocks, ghost_blocks, onehot_ghost[...])
        parts = [
            total[h * bands:(h + 1) * bands, 0:min(LO, face_pad - h * LO)] for h in range(ghost_blocks)
        ]
        return jnp.concatenate(parts, axis=1)

    def scatter_own():
        half_cols = elems * NODE_EL // 2
        total = None
        for k in range(2):
            cols = slice(k * half_cols, (k + 1) * half_cols)
            value = place([high_ref[:, cols], low_ref[:, cols]], hi_ref[:, cols], 0, own_blocks, onehot[:, cols])
            total = value if total is None else total + value
        return total

    def put_face(received):
        return place(list(split(received)), hi_face[...], 0, own_blocks, onehot_face[...])

    gather_own()
    copy1.wait()
    gather_ghost(got1[...])
    for c in ham_copies:
        c.wait()
    multiply()
    send2[...] = upper()
    copy2 = remote(send2, got2, f_send.at[1], f_recv.at[1], above)
    copy2.start()
    partial_value = (scatter_own() - CENTER * base[...]) / HALF_WIDTH
    field[...] = partial_value
    high, low = split(partial_value)
    send3[...] = take_face(high).astype(F32) + take_face(low).astype(F32)
    copy3 = remote(send3, got3, f_send.at[2], f_recv.at[2], below)
    copy3.start()
    copy2.wait()
    field[...] += put_face(got2[...] / HALF_WIDTH)
    xb[...] = field[...].astype(BF)
    gather_own()
    copy3.wait()
    gather_ghost(got3[...] + send2[...] / HALF_WIDTH)
    multiply()
    send4[...] = upper()
    copy4 = remote(send4, got4, f_send.at[3], f_recv.at[3], above)
    copy4.start()
    partial_value = scatter_own() - CENTER * field[...]
    copy4.wait()
    field[...] = 2.0 * ((partial_value + put_face(got4[...])) / HALF_WIDTH) - base[...]

    blocks = width // 128
    for piece in range(groups * blocks):
        dst = slice((piece % blocks) * 128, (piece % blocks + 1) * 128)
        if piece // 2 < own_blocks:
            rows = slice(piece // 2 * bands, (piece // 2 + 1) * bands)
            src = slice((piece % 2) * 128, (piece % 2 + 1) * 128)
            pieces[piece // blocks, :, dst] = field[rows, src].astype(BF)
        else:
            pieces[piece // blocks, :, dst] = jnp.zeros((bands, 128), BF)

    def finish(copies):
        for c in copies:
            c.wait()

    mine = pl.ds(pl.multiple_of(band * bands, bands), bands)
    copies = []
    for d in range(1, groups):
        there = band_peer(d)
        copies.append(remote(pieces.at[there["band"]], rows_all.at[mine], a_send.at[d - 1], a_recv.at[d - 1], there))
        copies[-1].start()
    rows_all[mine, :] = pieces[band]
    finish(copies)

    folded = fold(nt(rows_all[0:count, :], rows_all[...]))
    for c in range(CORES):
        gram[c] = folded[:, c * 128:(c + 1) * 128].reshape(gram.shape[1:])
    copies = []
    for n, (c, d) in enumerate(members):
        there = group_peer(c, d)
        tile = gram.at[core if c == 0 else 1 - core, there["band"]]
        copies.append(remote(tile, group_in.at[n], r_send.at[n], r_recv.at[n], there))
        copies[-1].start()
    finish(copies)
    value = gram[core, band]
    for n in range(len(members)):
        value = value + group_in[n]
    y_in[y] = value

    copies = []
    for d in range(1, YS):
        copies.append(remote(y_in.at[y], y_in.at[y], y_send.at[d - 1], y_recv.at[d - 1], y_peer(d)))
        copies[-1].start()
    finish(copies)
    value = y_in[0]
    for k in range(1, YS):
        value = value + y_in[k]
    z_in[z] = value

    copies = []
    for d in range(1, ZS):
        copies.append(remote(z_in.at[z], z_in.at[z], z_send.at[d - 1], z_recv.at[d - 1], z_peer(d)))
        copies[-1].start()
    finish(copies)
    value = z_in[0]
    for k in range(1, ZS):
        value = value + z_in[k]
    whole[core, band] = value

    copies = []
    piece = whole.at[core, band]
    for n, (c, d) in enumerate(members):
        copies.append(remote(piece, piece, g_send.at[n], g_recv.at[n], group_peer(c, d)))
        copies[-1].start()
    finish(copies)

    part = count // 2
    folded = jnp.concatenate([whole[c].reshape(part, 128) for c in range(CORES)], axis=1) / total_nodes
    mat[0:part, :], mat[part:, :] = unfold(folded)

    def landing(source):
        return out_ref.at[:, lanes(source * width, width)]

    def back(k):
        return remote(ortho.at[k], landing(band), b_send.at[k], b_recv.at[band], {"band": k})

    def keep(k):
        return pltpu.make_async_copy(ortho.at[k], landing(band), own_sem)

    def rows_of(start, end):
        value = mat[start:end, :]
        row = start + lax.broadcasted_iota(jnp.int32, value.shape, 0)
        column = lax.broadcasted_iota(jnp.int32, value.shape, 1)
        parts = jnp.concatenate(split(jnp.where(column <= row, value, 0.0)), axis=0)
        both = nn(parts, rows_all[...])
        value = (both[0:end - start] + both[end - start:]).astype(BF)
        ortho[start // bands:end // bands] = value.reshape((end - start) // bands, bands, width)

    def deliver(start, end):
        for k in range(start // bands, end // bands):
            @pl.when(band != k)
            def _():
                back(k).start()

            @pl.when(band == k)
            def _():
                keep(k).start()

    panel = 2 * bands
    factor_inverse(mat, panel, rows_of, deliver)
    rows_of(count - panel, count)
    deliver(count - panel, count)
    for k in range(groups):
        @pl.when(band != k)
        def _():
            back(k).wait_send()
            remote(ortho.at[k], landing(k), b_send.at[k], b_recv.at[k], {"band": k}).wait_recv()

        @pl.when(band == k)
        def _():
            keep(k).wait()


def per_device(psi, ham, conn, face_rows):
    bands, nodes = psi.shape
    elems = conn.shape[0]
    faces = face_rows.shape[0]
    groups = lax.axis_size("band")
    own_blocks = pl.cdiv(nodes, LO)
    ghost_blocks = pl.cdiv(faces, LO)
    face_pad = pl.cdiv(faces, 128) * 128
    width = pl.cdiv(pl.cdiv(nodes, 128), groups) * 128
    own = own_blocks * bands
    entries = elems * NODE_EL
    count = groups * bands
    wide = pl.cdiv(count, 128) * 128
    unit = count // 2 // groups
    vmem = pl.BlockSpec(memory_space=pltpu.VMEM)
    anywhere = pl.BlockSpec(memory_space=pl.ANY)
    dma = pltpu.SemaphoreType.DMA

    result = pl.pallas_call(
        functools.partial(step_kernel, float(nodes * lax.axis_size("space"))),
        out_shape=jax.ShapeDtypeStruct((bands, groups * width), BF),
        in_specs=[vmem, anywhere, vmem, vmem],
        out_specs=anywhere,
        scratch_shapes=[
            pltpu.VMEM(ham.shape, BF),
            pltpu.VMEM((LO, entries), BF),
            pltpu.VMEM((LO, elems * TAIL), BF),
            pltpu.VMEM((LO, face_pad), BF),
            pltpu.VMEM((bands, entries), BF),
            pltpu.VMEM((bands, elems * TAIL), BF),
            pltpu.VMEM((bands, face_pad), BF),
            pltpu.VMEM((own, LO), F32),
            pltpu.VMEM((own, LO), F32),
            pltpu.VMEM((own, LO), BF),
            pltpu.VMEM((ghost_blocks * bands, LO), BF),
            pltpu.VMEM((bands, entries), BF),
            pltpu.VMEM((bands, entries), BF),
            pltpu.VMEM((bands, entries), BF),
            pltpu.VMEM((bands, face_pad), BF),
            pltpu.VMEM((bands, face_pad), F32),
            pltpu.VMEM((bands, face_pad), F32),
            pltpu.VMEM((bands, face_pad), F32),
            pltpu.VMEM((bands, face_pad), BF),
            pltpu.VMEM((bands, face_pad), F32),
            pltpu.VMEM((bands, face_pad), F32),
            pltpu.VMEM((bands, face_pad), F32),
            pltpu.VMEM((groups, bands, width), BF),
            pltpu.VMEM((wide, width), BF),
            pltpu.VMEM((CORES, groups, unit, 128), F32),
            pltpu.VMEM((CORES * groups - 1, unit, 128), F32),
            pltpu.VMEM((YS, unit, 128), F32),
            pltpu.VMEM((ZS, unit, 128), F32),
            pltpu.VMEM((CORES, groups, unit, 128), F32),
            pltpu.VMEM((count, wide), F32),
            pltpu.VMEM((groups, bands, width), BF),
            dma((HAM_PARTS,)), dma,
            dma((4,)), dma((4,)),
            dma((groups - 1,)), dma((groups - 1,)),
            dma((CORES * groups - 1,)), dma((CORES * groups - 1,)),
            dma((YS - 1,)), dma((YS - 1,)),
            dma((ZS - 1,)), dma((ZS - 1,)),
            dma((CORES * groups - 1,)), dma((CORES * groups - 1,)),
            dma((groups,)), dma((groups,)),
        ],
        compiler_params=pltpu.CompilerParams(
            collective_id=0, has_side_effects=True, vmem_limit_bytes=VMEM_LIMIT
        ),
        name="step",
    )(psi, ham, conn, face_rows)
    return result[:, 0:nodes].astype(F32)


def solution(mesh):
    placed = (P("band", "space"), P("space", None, None), P("space", None), P("space"))
    return jax.shard_map(
        per_device, mesh=mesh, in_specs=placed, out_specs=P("band", "space"), check_vma=False
    )
```

```python
import functools

import jax
import jax.numpy as jnp
from jax import lax
from jax.experimental import pallas as pl
from jax.experimental.pallas import tpu as pltpu
from jax.sharding import PartitionSpec as P

NODE_EL = 512
OWN_EL = 448
CENTER = 6.25
HALF_WIDTH = 7.5
LO = 256
TAIL = 128
MESH = pl.DeviceIdType.MESH
BF = jnp.bfloat16
F32 = jnp.float32
VMEM_LIMIT = 60 * 1024 * 1024

CORES, YS, ZS = 2, 8, 4
HAM_PARTS = 4
NT = (((1,), (1,)), ((), ()))
TN = (((0,), (0,)), ((), ()))


def nn(a, b):
    return jnp.dot(a, b, preferred_element_type=F32)


def nt(a, b):
    return lax.dot_general(a, b, NT, preferred_element_type=F32)


def remote(src, dst, send, recv, where):
    return pltpu.make_async_remote_copy(
        src_ref=src, dst_ref=dst, send_sem=send, recv_sem=recv, device_id=where, device_id_type=MESH
    )


def split(value):
    high = value.astype(BF)
    return high, (value - high.astype(F32)).astype(BF)


def split3(value):
    high = value.astype(BF)
    rest = value - high.astype(F32)
    middle = rest.astype(BF)
    return high, middle, (rest - middle.astype(F32)).astype(BF)


def lanes(start, size):
    return pl.ds(pl.multiple_of(start, 128), size)


def pick(table, which, first, count, total):
    bands = total.shape[0]
    for h in range(count):
        total = jnp.where(which == first + h, table[h * bands:(h + 1) * bands, :], total)
    return total


def place(parts, which, first, count, columns):
    zero = jnp.zeros_like(parts[0])
    keep = [which == first + h for h in range(count)]
    total = None
    for part in parts:
        value = nt(jnp.concatenate([jnp.where(k, part, zero) for k in keep], axis=0), columns)
        total = value if total is None else total + value
    return total


def indicator(low, depth):
    shape = depth.shape
    return jnp.where(depth == jnp.broadcast_to(low, shape), jnp.ones(shape, BF), jnp.zeros(shape, BF))


def as_bf(value, rows):
    return jnp.broadcast_to(value.astype(F32), (rows, value.shape[1])).astype(BF)


def factor_inverse(mat, panel, beside, after):
    size, wide = mat.shape
    step = 8
    lane = lax.broadcasted_iota(jnp.int32, (step, 128), 1)
    sub = lax.broadcasted_iota(jnp.int32, (step, 128), 0)
    tiles = range(wide // 128)

    def spread_lane(value, j):
        return jnp.broadcast_to(value[:, j:j + 1], (step, 128))

    def spread_row(value, i):
        return jnp.broadcast_to(value[i:i + 1, :], (step, 128))

    for top in range(0, size, panel):
        if top > 0:
            beside(top - panel, top)
        groups = min(panel, size - top) // step
        block = [
            [mat[top + step * g:top + step * (g + 1), t * 128:(t + 1) * 128] for t in tiles] for g in range(groups)
        ]
        for s in range(groups):
            start = top + step * s
            tile, at = start // 128, start % 128
            columns = [spread_lane(block[s][tile], at + j) for j in range(step)]
            d = {(i, j): spread_row(columns[j], i) for j in range(step) for i in range(j, step)}
            below = [[spread_lane(block[g][tile], at + j) for j in range(step)] for g in range(s + 1, groups)]
            inside = (lane >= at) & (lane < at + step)
            base = [[spread_row(block[s][t], i) for i in range(step)] for t in tiles]
            for i in range(step):
                base[tile][i] = jnp.where(inside, jnp.where(lane == at + i, 1.0, 0.0), base[tile][i])
            rows = [[] for _ in tiles]
            for k in range(step):
                scale = lax.rsqrt(d[k, k])
                factor = {i: d[i, k] * scale for i in range(k + 1, step)}
                for i in range(k + 1, step):
                    for m in range(k + 1, i + 1):
                        d[i, m] = d[i, m] - factor[i] * factor[m]
                for t in tiles:
                    rows[t].append(base[t][k] * scale)
                    for i in range(k + 1, step):
                        base[t][i] = base[t][i] - factor[i] * rows[t][k]
                for part in below:
                    part[k] = part[k] * scale
                    for i in range(k + 1, step):
                        part[i] = part[i] - part[k] * factor[i]
            for t in tiles:
                fresh = rows[t][0]
                for i in range(1, step):
                    fresh = jnp.where(sub == i, rows[t][i], fresh)
                block[s][t] = fresh
            for n, g in enumerate(range(s + 1, groups)):
                for t in tiles:
                    value = block[g][t]
                    if t == tile:
                        value = jnp.where(inside, 0.0, value)
                    for k in range(step):
                        value = value - below[n][k] * rows[t][k]
                    block[g][t] = value
        for g in range(groups):
            for t in tiles:
                mat[top + step * g:top + step * (g + 1), t * 128:(t + 1) * 128] = block[g][t]
        end = top + step * groups
        if end < size:
            first = end // 128 * 128
            fresh = mat[top:end, :]
            row = top + lax.broadcasted_iota(jnp.int32, fresh.shape, 0)
            column = lax.broadcasted_iota(jnp.int32, fresh.shape, 1)
            a, b, c = split3(fresh[:, first:])
            d, e, f = split3(jnp.where((column > row) & (column < end), 0.0, fresh))
            update = lax.dot_general(
                jnp.concatenate([a, a, b, b, a, c], axis=0),
                jnp.concatenate([d, e, d, e, f, d], axis=0),
                TN,
                preferred_element_type=F32,
            )
            rest = mat[end:size, :]
            column = lax.broadcasted_iota(jnp.int32, rest.shape, 1)
            rest = jnp.where((column >= top) & (column < end), 0.0, rest)
            mat[end:size, :] = rest - update[end - first:size - first, :]
        if top > 0:
            after(top - panel, top)


def fold(matrix):
    half = matrix.shape[0] // 2
    upper, lower = matrix[0:half, :], matrix[half:, :]
    row = lax.broadcasted_iota(jnp.int32, lower.shape, 0)
    lane = lax.broadcasted_iota(jnp.int32, lower.shape, 1)
    diagonal = jnp.sum(jnp.where(lane == row + half, lower, 0.0), axis=1, keepdims=True)
    mixed = jnp.where((lane >= half) & (lane - half <= row), pltpu.roll(upper, half, 1), lower)
    return jnp.where(lane < 2 * half, mixed, diagonal)


def unfold(folded):
    half, wide = folded.shape
    row = lax.broadcasted_iota(jnp.int32, folded.shape, 0)
    lane = lax.broadcasted_iota(jnp.int32, folded.shape, 1)
    diagonal = jnp.broadcast_to(folded[:, 2 * half:2 * half + 1], folded.shape)
    mixed = pltpu.roll(folded, wide - half, 1)
    zeros = jnp.zeros((128 - half, 128), F32)

    def flip(value):
        square = jnp.concatenate([value[:, 0:128], zeros], axis=0).T[0:half, :]
        return jnp.concatenate([square, jnp.zeros((half, wide - 128), F32)], axis=1)

    other = flip(jnp.where(lane < half, mixed, 0.0))
    corner = flip(jnp.where(lane < half, folded, 0.0))
    first = jnp.where(lane < half, jnp.where(lane <= row, mixed, other), pltpu.roll(corner, half, 1))
    last = jnp.where(lane == row, diagonal, jnp.where(lane > row, mixed, other))
    last = jnp.where(lane < half, folded, pltpu.roll(last, half, 1))
    inside = lane < 2 * half
    return jnp.where(inside, first, 0.0), jnp.where(inside, last, 0.0)


def step_kernel(
    total_nodes, psi_hbm, ham_hbm, conn_hbm, face_hbm, out_ref,
    psi_ref, conn_ref, face_ref, ham, onehot, onehot_ghost, onehot_face, hi_ref, hi_ghost, hi_face, base, field, xb, xg,
    gathered, ghosted, products, high_ref, low_ref, tail_high, tail_low, kept,
    send1, send2, send3, send4, got1, got2, got3, got4,
    pieces, rows_all, gram, group_in, y_in, z_in, whole, mat, ortho,
    in_sem, ham_sem, own_sem, f_send, f_recv, a_send, a_recv, r_send, r_recv, y_send, y_recv, z_send, z_recv,
    g_send, g_recv, b_send, b_recv,
):
    bands, nodes = psi_ref.shape
    elems = conn_ref.shape[0]
    faces = face_ref.shape[0]
    own_blocks = pl.cdiv(nodes, LO)
    ghost_blocks = pl.cdiv(faces, LO)
    face_pad = got1.shape[1]
    shift = own_blocks * LO - nodes
    domains = lax.axis_size("space")
    space = lax.axis_index("space")
    band = lax.axis_index("band")
    groups, _, width = pieces.shape
    count = groups * bands
    wide = mat.shape[1]
    core = lax.rem(space, CORES)
    y = lax.rem(space // CORES, YS)
    z = space // (CORES * YS)
    below = {"space": lax.rem(space + domains - 1, domains)}
    above = {"space": lax.rem(space + 1, domains)}
    twin = {"space": space + 1 - 2 * core}

    inputs = [
        pltpu.make_async_copy(source, held, in_sem.at[n])
        for n, (source, held) in enumerate([(face_hbm, face_ref), (psi_hbm, psi_ref), (conn_hbm, conn_ref)])
    ]
    for c in inputs:
        c.start()

    def band_peer(d):
        return {"band": lax.rem(band + d, groups)}

    def y_peer(d):
        return {"space": (z * YS + lax.rem(y + d, YS)) * CORES + core}

    def z_peer(d):
        return {"space": (lax.rem(z + d, ZS) * YS + y) * CORES + core}

    def group_peer(c, d):
        there = {"band": lax.rem(band + d, groups)}
        if c > 0:
            there["space"] = twin["space"]
        return there

    members = [(c, d) for c in range(CORES) for d in range(groups) if c + d > 0]
    peers = [below, above]
    peers += [group_peer(c, d) for c, d in members]
    peers += [y_peer(d) for d in range(1, YS)]
    peers += [z_peer(d) for d in range(1, ZS)]
    barrier = pltpu.get_barrier_semaphore()
    for there in peers:
        pl.semaphore_signal(barrier, inc=1, device_id=there, device_id_type=MESH)

    per = elems // HAM_PARTS
    ham_copies = []
    for k in range(HAM_PARTS):
        part = slice(k * per, (k + 1) * per)
        ham_copies.append(pltpu.make_async_copy(ham_hbm.at[part], ham.at[part], ham_sem.at[k]))
        ham_copies[-1].start()

    inputs[0].wait()
    depth = lax.broadcasted_iota(jnp.int32, (LO, NODE_EL), 0).astype(F32).astype(BF)
    for k in range(face_pad // 128):
        size = min(128, faces - k * 128)
        named = jnp.full((1, 128), -1, jnp.int32)
        spot = lax.broadcasted_iota(jnp.int32, (1, 128), 1)
        if size == 128:
            named = face_ref[k * 128:(k + 1) * 128].reshape(1, 128)
        else:
            tail = face_ref[faces - 128:faces].reshape(1, 128)
            named = jnp.where(spot < size, pltpu.roll(tail, size, 1), -1)
        cols = slice(k * 128, (k + 1) * 128)
        onehot_face[:, cols] = indicator(as_bf(named & (LO - 1), 1), depth[:, 0:128])
        hi_face[:, cols] = as_bf(named >> 8, bands)

    def take_face(blocks):
        table = nn(blocks, onehot_face[...]).astype(BF)
        return pick(table, hi_face[...], 0, own_blocks, jnp.zeros((bands, face_pad), BF))

    inputs[1].wait()
    for h in range(own_blocks):
        rows = slice(h * bands, (h + 1) * bands)
        if (h + 1) * LO <= nodes:
            value = psi_ref[:, h * LO:(h + 1) * LO]
            base[rows, :] = value
            xb[rows, :] = value.astype(BF)
        else:
            base[rows, :] = jnp.zeros((bands, LO), F32)
            base[rows, 0:nodes - h * LO] = psi_ref[:, h * LO:nodes]
            xb[rows, :] = base[rows, :].astype(BF)
    send1[...] = take_face(xb[...])
    pl.semaphore_wait(barrier, len(peers))
    copy1 = remote(send1, got1, f_send.at[0], f_recv.at[0], below)
    copy1.start()

    inputs[2].wait()
    spot = lax.broadcasted_iota(jnp.int32, (1, NODE_EL), 1)

    def prepare(e, carry):
        named = conn_ref[pl.ds(e, 1), :]
        named = jnp.where(spot >= OWN_EL, named + shift, named)
        marks = indicator(as_bf(named & (LO - 1), 1), depth)
        which = as_bf(named >> 8, bands)
        cols = lanes(e * NODE_EL, NODE_EL)
        onehot[:, cols] = marks
        hi_ref[:, cols] = which
        cols = lanes(e * TAIL, TAIL)
        onehot_ghost[:, cols] = marks[:, NODE_EL - TAIL:]
        hi_ghost[:, cols] = which[:, NODE_EL - TAIL:]
        return carry

    lax.fori_loop(0, elems, prepare, 0, unroll=2)
    xg[...] = jnp.zeros(xg.shape, BF)
    rows_all[count:, :] = jnp.zeros((rows_all.shape[0] - count, width), BF)

    def gather_own():
        def body(e, carry):
            cols = lanes(e * NODE_EL, NODE_EL)
            table = nn(xb[...], onehot[:, cols]).astype(BF)
            gathered[:, cols] = pick(table, hi_ref[:, cols], 0, own_blocks, jnp.zeros((bands, NODE_EL), BF))
            return carry

        lax.fori_loop(0, elems, body, 0, unroll=4)

    def gather_ghost(values):
        for h in range(ghost_blocks):
            size = min(LO, face_pad - h * LO)
            xg[h * bands:(h + 1) * bands, 0:size] = values[:, h * LO:h * LO + size].astype(BF)
        table = nn(xg[...], onehot_ghost[...]).astype(BF)
        ghosted[...] = pick(table, hi_ghost[...], own_blocks, ghost_blocks, jnp.zeros((bands, elems * TAIL), BF))

    def multiply_own():
        def body(e, carry):
            cols = lanes(e * NODE_EL, NODE_EL)
            products[:, cols] = nn(gathered[:, cols], ham[e])
            return carry

        lax.fori_loop(0, elems, body, 0, unroll=4)

    def upper():
        for e in range(elems):
            some = slice(e * TAIL, (e + 1) * TAIL)
            cols = slice((e + 1) * NODE_EL - TAIL, (e + 1) * NODE_EL)
            value = products[:, cols] + nn(ghosted[:, some], ham[e, NODE_EL - TAIL:, NODE_EL - TAIL:])
            high, low = split(value)
            tail_high[:, some], tail_low[:, some] = high, low
            high_ref[:, cols], low_ref[:, cols] = high, low
        total = place([tail_high[...], tail_low[...]], hi_ghost[...], own_blocks, ghost_blocks, onehot_ghost[...])
        parts = [
            total[h * bands:(h + 1) * bands, 0:min(LO, face_pad - h * LO)] for h in range(ghost_blocks)
        ]
        return jnp.concatenate(parts, axis=1)

    def multiply_ghost():
        def body(e, carry):
            some = lanes(e * TAIL, TAIL)
            cols = lanes(e * NODE_EL, NODE_EL - TAIL)
            value = products[:, cols] + nn(ghosted[:, some], ham[e, NODE_EL - TAIL:, 0:NODE_EL - TAIL])
            high_ref[:, cols], low_ref[:, cols] = split(value)
            return carry

        lax.fori_loop(0, elems, body, 0, unroll=4)

    def scatter_own():
        size = elems * NODE_EL // 4
        total = None
        for k in range(4):
            cols = slice(k * size, (k + 1) * size)
            value = place([high_ref[:, cols], low_ref[:, cols]], hi_ref[:, cols], 0, own_blocks, onehot[:, cols])
            total = value if total is None else total + value
        return total

    def put_face(received):
        return place([received], hi_face[...], 0, own_blocks, onehot_face[...])

    gather_own()
    for c in ham_copies:
        c.wait()
    multiply_own()
    copy1.wait()
    gather_ghost(got1[...])
    kept[...] = upper()
    send2[...] = kept[...].astype(BF)
    copy2 = remote(send2, got2, f_send.at[1], f_recv.at[1], above)
    copy2.start()
    multiply_ghost()
    partial_value = (scatter_own() - CENTER * base[...]) / HALF_WIDTH
    field[...] = partial_value
    send3[...] = take_face(partial_value.astype(BF))
    copy3 = remote(send3, got3, f_send.at[2], f_recv.at[2], below)
    copy3.start()
    copy2.wait()
    field[...] += put_face(got2[...]) / HALF_WIDTH
    xb[...] = field[...].astype(BF)
    gather_own()
    multiply_own()
    copy3.wait()
    gather_ghost(got3[...].astype(F32) + kept[...] / HALF_WIDTH)
    send4[...] = upper().astype(BF)
    copy4 = remote(send4, got4, f_send.at[3], f_recv.at[3], above)
    copy4.start()
    multiply_ghost()
    partial_value = scatter_own() - CENTER * field[...]
    copy4.wait()
    field[...] = 2.0 * ((partial_value + put_face(got4[...])) / HALF_WIDTH) - base[...]

    blocks = width // 128
    for piece in range(groups * blocks):
        dst = slice((piece % blocks) * 128, (piece % blocks + 1) * 128)
        if piece // 2 < own_blocks:
            rows = slice(piece // 2 * bands, (piece // 2 + 1) * bands)
            src = slice((piece % 2) * 128, (piece % 2 + 1) * 128)
            pieces[piece // blocks, :, dst] = field[rows, src].astype(BF)
        else:
            pieces[piece // blocks, :, dst] = jnp.zeros((bands, 128), BF)

    def finish(copies):
        for c in copies:
            c.wait()

    mine = pl.ds(pl.multiple_of(band * bands, bands), bands)
    copies = []
    for d in range(1, groups):
        there = band_peer(d)
        copies.append(remote(pieces.at[there["band"]], rows_all.at[mine], a_send.at[d - 1], a_recv.at[d - 1], there))
        copies[-1].start()
    rows_all[mine, :] = pieces[band]
    finish(copies)

    folded = fold(nt(rows_all[0:count, :], rows_all[...]))
    for c in range(CORES):
        gram[c] = folded[:, c * 128:(c + 1) * 128].reshape(gram.shape[1:])
    copies = []
    for n, (c, d) in enumerate(members):
        there = group_peer(c, d)
        tile = gram.at[core if c == 0 else 1 - core, there["band"]]
        copies.append(remote(tile, group_in.at[n], r_send.at[n], r_recv.at[n], there))
        copies[-1].start()
    finish(copies)
    value = gram[core, band]
    for n in range(len(members)):
        value = value + group_in[n]
    y_in[y] = value

    copies = []
    for d in range(1, YS):
        copies.append(remote(y_in.at[y], y_in.at[y], y_send.at[d - 1], y_recv.at[d - 1], y_peer(d)))
        copies[-1].start()
    finish(copies)
    value = y_in[0]
    for k in range(1, YS):
        value = value + y_in[k]
    z_in[z] = value

    copies = []
    for d in range(1, ZS):
        copies.append(remote(z_in.at[z], z_in.at[z], z_send.at[d - 1], z_recv.at[d - 1], z_peer(d)))
        copies[-1].start()
    finish(copies)
    value = z_in[0]
    for k in range(1, ZS):
        value = value + z_in[k]
    whole[core, band] = value

    copies = []
    piece = whole.at[core, band]
    for n, (c, d) in enumerate(members):
        copies.append(remote(piece, piece, g_send.at[n], g_recv.at[n], group_peer(c, d)))
        copies[-1].start()
    finish(copies)

    part = count // 2
    folded = jnp.concatenate([whole[c].reshape(part, 128) for c in range(CORES)], axis=1) / total_nodes
    mat[0:part, :], mat[part:, :] = unfold(folded)

    def landing(source):
        return out_ref.at[:, lanes(source * width, width)]

    def back(k):
        return remote(ortho.at[k], landing(band), b_send.at[k], b_recv.at[band], {"band": k})

    def keep(k):
        return pltpu.make_async_copy(ortho.at[k], landing(band), own_sem)

    def rows_of(start, end):
        value = mat[start:end, :]
        row = start + lax.broadcasted_iota(jnp.int32, value.shape, 0)
        column = lax.broadcasted_iota(jnp.int32, value.shape, 1)
        parts = jnp.concatenate(split(jnp.where(column <= row, value, 0.0)), axis=0)
        both = nn(parts, rows_all[...])
        value = (both[0:end - start] + both[end - start:]).astype(BF)
        ortho[start // bands:end // bands] = value.reshape((end - start) // bands, bands, width)

    def deliver(start, end):
        for k in range(start // bands, end // bands):
            @pl.when(band != k)
            def _():
                back(k).start()

            @pl.when(band == k)
            def _():
                keep(k).start()

    panel = 2 * bands
    factor_inverse(mat, panel, rows_of, deliver)
    rows_of(count - panel, count)
    deliver(count - panel, count)
    for k in range(groups):
        @pl.when(band != k)
        def _():
            back(k).wait_send()
            remote(ortho.at[k], landing(k), b_send.at[k], b_recv.at[k], {"band": k}).wait_recv()

        @pl.when(band == k)
        def _():
            keep(k).wait()


def per_device(psi, ham, conn, face_rows):
    bands, nodes = psi.shape
    elems = conn.shape[0]
    faces = face_rows.shape[0]
    groups = lax.axis_size("band")
    own_blocks = pl.cdiv(nodes, LO)
    ghost_blocks = pl.cdiv(faces, LO)
    face_pad = pl.cdiv(faces, 128) * 128
    width = pl.cdiv(pl.cdiv(nodes, 128), groups) * 128
    own = own_blocks * bands
    entries = elems * NODE_EL
    count = groups * bands
    wide = pl.cdiv(count, 128) * 128
    unit = count // 2 // groups
    anywhere = pl.BlockSpec(memory_space=pl.ANY)
    dma = pltpu.SemaphoreType.DMA

    result = pl.pallas_call(
        functools.partial(step_kernel, float(nodes * lax.axis_size("space"))),
        out_shape=jax.ShapeDtypeStruct((bands, groups * width), BF),
        in_specs=[anywhere] * 4,
        out_specs=anywhere,
        scratch_shapes=[
            pltpu.VMEM(psi.shape, F32),
            pltpu.VMEM(conn.shape, jnp.int32),
            pltpu.VMEM(face_rows.shape, jnp.int32),
            pltpu.VMEM(ham.shape, BF),
            pltpu.VMEM((LO, entries), BF),
            pltpu.VMEM((LO, elems * TAIL), BF),
            pltpu.VMEM((LO, face_pad), BF),
            pltpu.VMEM((bands, entries), BF),
            pltpu.VMEM((bands, elems * TAIL), BF),
            pltpu.VMEM((bands, face_pad), BF),
            pltpu.VMEM((own, LO), F32),
            pltpu.VMEM((own, LO), F32),
            pltpu.VMEM((own, LO), BF),
            pltpu.VMEM((ghost_blocks * bands, LO), BF),
            pltpu.VMEM((bands, entries), BF),
            pltpu.VMEM((bands, elems * TAIL), BF),
            pltpu.VMEM((bands, entries), F32),
            pltpu.VMEM((bands, entries), BF),
            pltpu.VMEM((bands, entries), BF),
            pltpu.VMEM((bands, elems * TAIL), BF),
            pltpu.VMEM((bands, elems * TAIL), BF),
            pltpu.VMEM((bands, face_pad), F32),
            pltpu.VMEM((bands, face_pad), BF),
            pltpu.VMEM((bands, face_pad), BF),
            pltpu.VMEM((bands, face_pad), BF),
            pltpu.VMEM((bands, face_pad), BF),
            pltpu.VMEM((bands, face_pad), BF),
            pltpu.VMEM((bands, face_pad), BF),
            pltpu.VMEM((bands, face_pad), BF),
            pltpu.VMEM((bands, face_pad), BF),
            pltpu.VMEM((groups, bands, width), BF),
            pltpu.VMEM((wide, width), BF),
            pltpu.VMEM((CORES, groups, unit, 128), F32),
            pltpu.VMEM((CORES * groups - 1, unit, 128), F32),
            pltpu.VMEM((YS, unit, 128), F32),
            pltpu.VMEM((ZS, unit, 128), F32),
            pltpu.VMEM((CORES, groups, unit, 128), F32),
            pltpu.VMEM((count, wide), F32),
            pltpu.VMEM((groups, bands, width), BF),
            dma((3,)), dma((HAM_PARTS,)), dma,
            dma((4,)), dma((4,)),
            dma((groups - 1,)), dma((groups - 1,)),
            dma((CORES * groups - 1,)), dma((CORES * groups - 1,)),
            dma((YS - 1,)), dma((YS - 1,)),
            dma((ZS - 1,)), dma((ZS - 1,)),
            dma((CORES * groups - 1,)), dma((CORES * groups - 1,)),
            dma((groups,)), dma((groups,)),
        ],
        compiler_params=pltpu.CompilerParams(
            collective_id=0, has_side_effects=True, vmem_limit_bytes=VMEM_LIMIT
        ),
        name="step",
    )(psi, ham, conn, face_rows)
    return result[:, 0:nodes].astype(F32)


def solution(mesh):
    placed = (P("band", "space"), P("space", None, None), P("space", None), P("space"))
    return jax.shard_map(
        per_device, mesh=mesh, in_specs=placed, out_specs=P("band", "space"), check_vma=False
    )
```

```python
import functools

import jax
import jax.numpy as jnp
from jax import lax
from jax.experimental import pallas as pl
from jax.experimental.pallas import tpu as pltpu
from jax.sharding import PartitionSpec as P

NODE_EL = 512
OWN_EL = 448
CENTER = 6.25
HALF_WIDTH = 7.5
LO = 256
TAIL = 128
MESH = pl.DeviceIdType.MESH
BF = jnp.bfloat16
F32 = jnp.float32
VMEM_LIMIT = 60 * 1024 * 1024

CORES, YS, ZS, BAND_Z = 2, 8, 4, 3
HAM_PARTS = 4
NT = (((1,), (1,)), ((), ()))
TN = (((0,), (0,)), ((), ()))


def nn(a, b):
    return jnp.dot(a, b, preferred_element_type=F32)


def nt(a, b):
    return lax.dot_general(a, b, NT, preferred_element_type=F32)


def remote(src, dst, send, recv, where):
    return pltpu.make_async_remote_copy(
        src_ref=src, dst_ref=dst, send_sem=send, recv_sem=recv, device_id=where, device_id_type=MESH
    )


def split(value):
    high = value.astype(BF)
    return high, (value - high.astype(F32)).astype(BF)


def split3(value):
    high = value.astype(BF)
    rest = value - high.astype(F32)
    middle = rest.astype(BF)
    return high, middle, (rest - middle.astype(F32)).astype(BF)


def lanes(start, size):
    return pl.ds(pl.multiple_of(start, 128), size)


def pick(table, which, first, count, total):
    bands = total.shape[0]
    for h in range(count):
        total = jnp.where(which == first + h, table[h * bands:(h + 1) * bands, :], total)
    return total


def place(parts, which, first, count, columns):
    zero = jnp.zeros_like(parts[0])
    keep = [which == first + h for h in range(count)]
    total = None
    for part in parts:
        value = nt(jnp.concatenate([jnp.where(k, part, zero) for k in keep], axis=0), columns)
        total = value if total is None else total + value
    return total


def indicator(low, depth):
    shape = depth.shape
    return jnp.where(depth == jnp.broadcast_to(low, shape), jnp.ones(shape, BF), jnp.zeros(shape, BF))


def as_bf(value, rows):
    return jnp.broadcast_to(value.astype(F32), (rows, value.shape[1])).astype(BF)


def factor_inverse(mat, panel, beside, after):
    size, wide = mat.shape
    step = 8
    lane = lax.broadcasted_iota(jnp.int32, (step, 128), 1)
    sub = lax.broadcasted_iota(jnp.int32, (step, 128), 0)
    tiles = range(wide // 128)

    def spread_lane(value, j):
        return jnp.broadcast_to(value[:, j:j + 1], (step, 128))

    def spread_row(value, i):
        return jnp.broadcast_to(value[i:i + 1, :], (step, 128))

    for top in range(0, size, panel):
        if top > 0:
            beside(top - panel, top)
        groups = min(panel, size - top) // step
        block = [
            [mat[top + step * g:top + step * (g + 1), t * 128:(t + 1) * 128] for t in tiles] for g in range(groups)
        ]
        for s in range(groups):
            start = top + step * s
            tile, at = start // 128, start % 128
            columns = [spread_lane(block[s][tile], at + j) for j in range(step)]
            d = {(i, j): spread_row(columns[j], i) for j in range(step) for i in range(j, step)}
            below = [[spread_lane(block[g][tile], at + j) for j in range(step)] for g in range(s + 1, groups)]
            inside = (lane >= at) & (lane < at + step)
            base = [[spread_row(block[s][t], i) for i in range(step)] for t in tiles]
            for i in range(step):
                base[tile][i] = jnp.where(inside, jnp.where(lane == at + i, 1.0, 0.0), base[tile][i])
            rows = [[] for _ in tiles]
            for k in range(step):
                scale = lax.rsqrt(d[k, k])
                factor = {i: d[i, k] * scale for i in range(k + 1, step)}
                for i in range(k + 1, step):
                    for m in range(k + 1, i + 1):
                        d[i, m] = d[i, m] - factor[i] * factor[m]
                for t in tiles:
                    rows[t].append(base[t][k] * scale)
                    for i in range(k + 1, step):
                        base[t][i] = base[t][i] - factor[i] * rows[t][k]
                for part in below:
                    part[k] = part[k] * scale
                    for i in range(k + 1, step):
                        part[i] = part[i] - part[k] * factor[i]
            for t in tiles:
                fresh = rows[t][0]
                for i in range(1, step):
                    fresh = jnp.where(sub == i, rows[t][i], fresh)
                block[s][t] = fresh
            for n, g in enumerate(range(s + 1, groups)):
                for t in tiles:
                    value = block[g][t]
                    if t == tile:
                        value = jnp.where(inside, 0.0, value)
                    for k in range(step):
                        value = value - below[n][k] * rows[t][k]
                    block[g][t] = value
        for g in range(groups):
            for t in tiles:
                mat[top + step * g:top + step * (g + 1), t * 128:(t + 1) * 128] = block[g][t]
        end = top + step * groups
        if end < size:
            first = end // 128 * 128
            fresh = mat[top:end, :]
            row = top + lax.broadcasted_iota(jnp.int32, fresh.shape, 0)
            column = lax.broadcasted_iota(jnp.int32, fresh.shape, 1)
            a, b, c = split3(fresh[:, first:])
            d, e, f = split3(jnp.where((column > row) & (column < end), 0.0, fresh))
            update = lax.dot_general(
                jnp.concatenate([a, a, b, b, a, c], axis=0),
                jnp.concatenate([d, e, d, e, f, d], axis=0),
                TN,
                preferred_element_type=F32,
            )
            rest = mat[end:size, :]
            column = lax.broadcasted_iota(jnp.int32, rest.shape, 1)
            rest = jnp.where((column >= top) & (column < end), 0.0, rest)
            mat[end:size, :] = rest - update[end - first:size - first, :]
        if top > 0:
            after(top - panel, top)


def fold(matrix):
    rest = matrix.shape[0] - 128
    corner = pltpu.roll(matrix[128:, 128:], rest, 1)
    lane = lax.broadcasted_iota(jnp.int32, corner.shape, 1)
    first = jnp.where(lane < rest, matrix[0:rest, 0:128], corner)
    return jnp.concatenate([first, matrix[rest:, 0:128]], axis=0)


def unfold(folded):
    count = folded.shape[0]
    rest = count - 128
    turned = pltpu.roll(folded[rest:, :].T, rest, 1)
    lane = lax.broadcasted_iota(jnp.int32, folded.shape, 1)
    first = jnp.where(lane[0:rest] < rest, folded[0:rest, :], turned[0:rest, :])
    left = jnp.concatenate([first, folded[rest:, :]], axis=0)
    right = jnp.concatenate([turned, pltpu.roll(folded[0:rest, :], rest, 1)], axis=0)
    return jnp.concatenate([left, jnp.where(lane < rest, right, 0.0)], axis=1)


def step_kernel(
    total_nodes, psi_hbm, ham_hbm, conn_hbm, face_hbm, out_ref,
    psi_ref, conn_ref, face_ref, ham, onehot, onehot_ghost, onehot_face, hi_ref, hi_ghost, hi_face, base, field, xb, xg,
    gathered, ghosted, products, high_ref, low_ref, tail_high, tail_low, kept,
    send1, send2, send3, send4, got1, got2, got3, got4,
    pieces, rows_all, gram, group_in, y_in, z_in, whole, mat, ortho,
    in_sem, ham_sem, own_sem, f_send, f_recv, a_send, a_recv, r_send, r_recv, y_send, y_recv, z_send, z_recv,
    g_send, g_recv, b_send, b_recv,
):
    bands, nodes = psi_ref.shape
    elems = conn_ref.shape[0]
    faces = face_ref.shape[0]
    own_blocks = pl.cdiv(nodes, LO)
    ghost_blocks = pl.cdiv(faces, LO)
    face_pad = got1.shape[1]
    shift = own_blocks * LO - nodes
    domains = lax.axis_size("space")
    space = lax.axis_index("space")
    band = lax.axis_index("band")
    groups, _, width = pieces.shape
    count = groups * bands
    wide = mat.shape[1]
    core = lax.rem(space, CORES)
    y = lax.rem(space // CORES, YS)
    z = space // (CORES * YS)
    below = {"space": lax.rem(space + domains - 1, domains)}
    above = {"space": lax.rem(space + 1, domains)}
    twin = {"space": space + 1 - 2 * core}

    inputs = [
        pltpu.make_async_copy(source, held, in_sem.at[n])
        for n, (source, held) in enumerate([(face_hbm, face_ref), (psi_hbm, psi_ref), (conn_hbm, conn_ref)])
    ]
    for c in inputs:
        c.start()

    band_x = groups // BAND_Z
    steps = [(i, k) for i in range(band_x) for k in range(BAND_Z) if i + k > 0]
    steps.sort(key=lambda step: -(min(step[0], band_x - step[0]) + 1.5 * (step[1] > 0)))

    def band_at(step):
        i, k = step
        return lax.rem(band // BAND_Z + i, band_x) * BAND_Z + lax.rem(lax.rem(band, BAND_Z) + k, BAND_Z)

    def band_peer(step):
        return {"band": band_at(step)}

    def y_peer(d):
        return {"space": (z * YS + lax.rem(y + d, YS)) * CORES + core}

    def z_peer(d):
        return {"space": (lax.rem(z + d, ZS) * YS + y) * CORES + core}

    def group_peer(c, step):
        there = {"band": band_at(step)}
        if c > 0:
            there["space"] = twin["space"]
        return there

    members = [(c, step) for step in steps for c in range(CORES)] + [(1, (0, 0))]
    y_steps = sorted(range(1, YS), key=lambda d: -min(d, YS - d))
    z_steps = sorted(range(1, ZS), key=lambda d: -min(d, ZS - d))
    peers = [below, above]
    peers += [group_peer(c, d) for c, d in members]
    peers += [y_peer(d) for d in y_steps]
    peers += [z_peer(d) for d in z_steps]
    barrier = pltpu.get_barrier_semaphore()
    for there in peers:
        pl.semaphore_signal(barrier, inc=1, device_id=there, device_id_type=MESH)

    per = elems // HAM_PARTS
    ham_copies = []
    for k in range(HAM_PARTS):
        part = slice(k * per, (k + 1) * per)
        ham_copies.append(pltpu.make_async_copy(ham_hbm.at[part], ham.at[part], ham_sem.at[k]))
        ham_copies[-1].start()

    inputs[0].wait()
    depth = lax.broadcasted_iota(jnp.int32, (LO, NODE_EL), 0).astype(F32).astype(BF)
    for k in range(face_pad // 128):
        size = min(128, faces - k * 128)
        named = jnp.full((1, 128), -1, jnp.int32)
        spot = lax.broadcasted_iota(jnp.int32, (1, 128), 1)
        if size == 128:
            named = face_ref[k * 128:(k + 1) * 128].reshape(1, 128)
        else:
            tail = face_ref[faces - 128:faces].reshape(1, 128)
            named = jnp.where(spot < size, pltpu.roll(tail, size, 1), -1)
        cols = slice(k * 128, (k + 1) * 128)
        onehot_face[:, cols] = indicator(as_bf(named & (LO - 1), 1), depth[:, 0:128])
        hi_face[:, cols] = as_bf(named >> 8, bands)

    def take_face(blocks):
        table = nn(blocks, onehot_face[...]).astype(BF)
        return pick(table, hi_face[...], 0, own_blocks, jnp.zeros((bands, face_pad), BF))

    inputs[1].wait()
    for h in range(own_blocks):
        rows = slice(h * bands, (h + 1) * bands)
        if (h + 1) * LO <= nodes:
            value = psi_ref[:, h * LO:(h + 1) * LO]
            base[rows, :] = value
            xb[rows, :] = value.astype(BF)
        else:
            base[rows, :] = jnp.zeros((bands, LO), F32)
            base[rows, 0:nodes - h * LO] = psi_ref[:, h * LO:nodes]
            xb[rows, :] = base[rows, :].astype(BF)
    send1[...] = take_face(xb[...])
    pl.semaphore_wait(barrier, len(peers))
    copy1 = remote(send1, got1, f_send.at[0], f_recv.at[0], below)
    copy1.start()

    inputs[2].wait()
    spot = lax.broadcasted_iota(jnp.int32, (1, NODE_EL), 1)

    def prepare(e, carry):
        named = conn_ref[pl.ds(e, 1), :]
        named = jnp.where(spot >= OWN_EL, named + shift, named)
        marks = indicator(as_bf(named & (LO - 1), 1), depth)
        which = as_bf(named >> 8, bands)
        cols = lanes(e * NODE_EL, NODE_EL)
        onehot[:, cols] = marks
        hi_ref[:, cols] = which
        cols = lanes(e * TAIL, TAIL)
        onehot_ghost[:, cols] = marks[:, NODE_EL - TAIL:]
        hi_ghost[:, cols] = which[:, NODE_EL - TAIL:]
        return carry

    lax.fori_loop(0, elems, prepare, 0, unroll=2)
    xg[...] = jnp.zeros(xg.shape, BF)
    rows_all[count:, :] = jnp.zeros((rows_all.shape[0] - count, width), BF)

    def gather_own():
        def body(e, carry):
            cols = lanes(e * NODE_EL, NODE_EL)
            table = nn(xb[...], onehot[:, cols]).astype(BF)
            gathered[:, cols] = pick(table, hi_ref[:, cols], 0, own_blocks, jnp.zeros((bands, NODE_EL), BF))
            return carry

        lax.fori_loop(0, elems, body, 0, unroll=4)

    def gather_ghost(values):
        for h in range(ghost_blocks):
            size = min(LO, face_pad - h * LO)
            xg[h * bands:(h + 1) * bands, 0:size] = values[:, h * LO:h * LO + size].astype(BF)
        table = nn(xg[...], onehot_ghost[...]).astype(BF)
        ghosted[...] = pick(table, hi_ghost[...], own_blocks, ghost_blocks, jnp.zeros((bands, elems * TAIL), BF))

    def multiply_own():
        def body(e, carry):
            cols = lanes(e * NODE_EL, NODE_EL)
            products[:, cols] = nn(gathered[:, cols], ham[e])
            return carry

        lax.fori_loop(0, elems, body, 0, unroll=4)

    def upper():
        for e in range(elems):
            some = slice(e * TAIL, (e + 1) * TAIL)
            cols = slice((e + 1) * NODE_EL - TAIL, (e + 1) * NODE_EL)
            value = products[:, cols] + nn(ghosted[:, some], ham[e, NODE_EL - TAIL:, NODE_EL - TAIL:])
            high, low = split(value)
            tail_high[:, some], tail_low[:, some] = high, low
            high_ref[:, cols], low_ref[:, cols] = high, low
        total = place([tail_high[...], tail_low[...]], hi_ghost[...], own_blocks, ghost_blocks, onehot_ghost[...])
        parts = [
            total[h * bands:(h + 1) * bands, 0:min(LO, face_pad - h * LO)] for h in range(ghost_blocks)
        ]
        return jnp.concatenate(parts, axis=1)

    def multiply_ghost():
        def body(e, carry):
            some = lanes(e * TAIL, TAIL)
            cols = lanes(e * NODE_EL, NODE_EL - TAIL)
            value = products[:, cols] + nn(ghosted[:, some], ham[e, NODE_EL - TAIL:, 0:NODE_EL - TAIL])
            high_ref[:, cols], low_ref[:, cols] = split(value)
            return carry

        lax.fori_loop(0, elems, body, 0, unroll=4)

    def scatter_own():
        size = elems * NODE_EL // 4
        total = None
        for k in range(4):
            cols = slice(k * size, (k + 1) * size)
            value = place([high_ref[:, cols], low_ref[:, cols]], hi_ref[:, cols], 0, own_blocks, onehot[:, cols])
            total = value if total is None else total + value
        return total

    def put_face(received):
        return place([received], hi_face[...], 0, own_blocks, onehot_face[...])

    gather_own()
    for c in ham_copies:
        c.wait()
    multiply_own()
    copy1.wait()
    gather_ghost(got1[...])
    kept[...] = upper()
    send2[...] = kept[...].astype(BF)
    copy2 = remote(send2, got2, f_send.at[1], f_recv.at[1], above)
    copy2.start()
    multiply_ghost()
    partial_value = (scatter_own() - CENTER * base[...]) / HALF_WIDTH
    field[...] = partial_value
    send3[...] = take_face(partial_value.astype(BF))
    copy3 = remote(send3, got3, f_send.at[2], f_recv.at[2], below)
    copy3.start()
    copy2.wait()
    field[...] += put_face(got2[...]) / HALF_WIDTH
    xb[...] = field[...].astype(BF)
    gather_own()
    multiply_own()
    copy3.wait()
    gather_ghost(got3[...].astype(F32) + kept[...] / HALF_WIDTH)
    send4[...] = upper().astype(BF)
    copy4 = remote(send4, got4, f_send.at[3], f_recv.at[3], above)
    copy4.start()
    multiply_ghost()
    partial_value = scatter_own() - CENTER * field[...]
    copy4.wait()
    field[...] = 2.0 * ((partial_value + put_face(got4[...])) / HALF_WIDTH) - base[...]

    blocks = width // 128
    for piece in range(groups * blocks):
        dst = slice((piece % blocks) * 128, (piece % blocks + 1) * 128)
        if piece // 2 < own_blocks:
            rows = slice(piece // 2 * bands, (piece // 2 + 1) * bands)
            src = slice((piece % 2) * 128, (piece % 2 + 1) * 128)
            pieces[piece // blocks, :, dst] = field[rows, src].astype(BF)
        else:
            pieces[piece // blocks, :, dst] = jnp.zeros((bands, 128), BF)

    def finish(copies):
        for c in copies:
            c.wait()

    mine = pl.ds(pl.multiple_of(band * bands, bands), bands)
    copies = []
    for n, step in enumerate(steps):
        there = band_peer(step)
        copies.append(remote(pieces.at[there["band"]], rows_all.at[mine], a_send.at[n], a_recv.at[n], there))
        copies[-1].start()
    rows_all[mine, :] = pieces[band]
    finish(copies)

    folded = fold(nt(rows_all[0:count, :], rows_all[...]))
    gram[...] = folded.reshape(gram.shape)
    copies = []
    for n, (c, d) in enumerate(members):
        there = group_peer(c, d)
        tile = gram.at[core if c == 0 else 1 - core, there["band"]]
        copies.append(remote(tile, group_in.at[n], r_send.at[n], r_recv.at[n], there))
        copies[-1].start()
    finish(copies)
    value = gram[core, band]
    for n in range(len(members)):
        value = value + group_in[n]
    y_in[y] = value

    copies = []
    for d in y_steps:
        copies.append(remote(y_in.at[y], y_in.at[y], y_send.at[d - 1], y_recv.at[d - 1], y_peer(d)))
        copies[-1].start()
    finish(copies)
    value = y_in[0]
    for k in range(1, YS):
        value = value + y_in[k]
    z_in[z] = value

    copies = []
    for d in z_steps:
        copies.append(remote(z_in.at[z], z_in.at[z], z_send.at[d - 1], z_recv.at[d - 1], z_peer(d)))
        copies[-1].start()
    finish(copies)
    value = z_in[0]
    for k in range(1, ZS):
        value = value + z_in[k]
    whole[core, band] = value

    copies = []
    piece = whole.at[core, band]
    for n, (c, d) in enumerate(members):
        copies.append(remote(piece, piece, g_send.at[n], g_recv.at[n], group_peer(c, d)))
        copies[-1].start()
    finish(copies)

    mat[...] = unfold(whole[...].reshape(count, 128) / total_nodes)

    def landing(source):
        return out_ref.at[:, lanes(source * width, width)]

    def back(k):
        return remote(ortho.at[k], landing(band), b_send.at[k], b_recv.at[band], {"band": k})

    def keep(k):
        return pltpu.make_async_copy(ortho.at[k], landing(band), own_sem)

    def rows_of(start, end):
        value = mat[start:end, :]
        row = start + lax.broadcasted_iota(jnp.int32, value.shape, 0)
        column = lax.broadcasted_iota(jnp.int32, value.shape, 1)
        parts = jnp.concatenate(split(jnp.where(column <= row, value, 0.0)), axis=0)
        both = nn(parts, rows_all[...])
        value = (both[0:end - start] + both[end - start:]).astype(BF)
        ortho[start // bands:end // bands] = value.reshape((end - start) // bands, bands, width)

    def deliver(start, end):
        for k in range(start // bands, end // bands):
            @pl.when(band != k)
            def _():
                back(k).start()

            @pl.when(band == k)
            def _():
                keep(k).start()

    panel = 2 * bands
    factor_inverse(mat, panel, rows_of, deliver)
    rows_of(count - panel, count)
    deliver(count - panel, count)
    for k in range(groups):
        @pl.when(band != k)
        def _():
            back(k).wait_send()
            remote(ortho.at[k], landing(k), b_send.at[k], b_recv.at[k], {"band": k}).wait_recv()

        @pl.when(band == k)
        def _():
            keep(k).wait()


def per_device(psi, ham, conn, face_rows):
    bands, nodes = psi.shape
    elems = conn.shape[0]
    faces = face_rows.shape[0]
    groups = lax.axis_size("band")
    own_blocks = pl.cdiv(nodes, LO)
    ghost_blocks = pl.cdiv(faces, LO)
    face_pad = pl.cdiv(faces, 128) * 128
    width = pl.cdiv(pl.cdiv(nodes, 128), groups) * 128
    own = own_blocks * bands
    entries = elems * NODE_EL
    count = groups * bands
    wide = pl.cdiv(count, 128) * 128
    unit = count // 2 // groups
    anywhere = pl.BlockSpec(memory_space=pl.ANY)
    dma = pltpu.SemaphoreType.DMA

    result = pl.pallas_call(
        functools.partial(step_kernel, float(nodes * lax.axis_size("space"))),
        out_shape=pltpu.VMEM((bands, groups * width), BF),
        in_specs=[anywhere] * 4,
        out_specs=pl.BlockSpec(memory_space=pltpu.VMEM),
        scratch_shapes=[
            pltpu.VMEM(psi.shape, F32),
            pltpu.VMEM(conn.shape, jnp.int32),
            pltpu.VMEM(face_rows.shape, jnp.int32),
            pltpu.VMEM(ham.shape, BF),
            pltpu.VMEM((LO, entries), BF),
            pltpu.VMEM((LO, elems * TAIL), BF),
            pltpu.VMEM((LO, face_pad), BF),
            pltpu.VMEM((bands, entries), BF),
            pltpu.VMEM((bands, elems * TAIL), BF),
            pltpu.VMEM((bands, face_pad), BF),
            pltpu.VMEM((own, LO), F32),
            pltpu.VMEM((own, LO), F32),
            pltpu.VMEM((own, LO), BF),
            pltpu.VMEM((ghost_blocks * bands, LO), BF),
            pltpu.VMEM((bands, entries), BF),
            pltpu.VMEM((bands, elems * TAIL), BF),
            pltpu.VMEM((bands, entries), F32),
            pltpu.VMEM((bands, entries), BF),
            pltpu.VMEM((bands, entries), BF),
            pltpu.VMEM((bands, elems * TAIL), BF),
            pltpu.VMEM((bands, elems * TAIL), BF),
            pltpu.VMEM((bands, face_pad), F32),
            pltpu.VMEM((bands, face_pad), BF),
            pltpu.VMEM((bands, face_pad), BF),
            pltpu.VMEM((bands, face_pad), BF),
            pltpu.VMEM((bands, face_pad), BF),
            pltpu.VMEM((bands, face_pad), BF),
            pltpu.VMEM((bands, face_pad), BF),
            pltpu.VMEM((bands, face_pad), BF),
            pltpu.VMEM((bands, face_pad), BF),
            pltpu.VMEM((groups, bands, width), BF),
            pltpu.VMEM((wide, width), BF),
            pltpu.VMEM((CORES, groups, unit, 128), F32),
            pltpu.VMEM((CORES * groups - 1, unit, 128), F32),
            pltpu.VMEM((YS, unit, 128), F32),
            pltpu.VMEM((ZS, unit, 128), F32),
            pltpu.VMEM((CORES, groups, unit, 128), F32),
            pltpu.VMEM((count, wide), F32),
            pltpu.VMEM((groups, bands, width), BF),
            dma((3,)), dma((HAM_PARTS,)), dma,
            dma((4,)), dma((4,)),
            dma((groups - 1,)), dma((groups - 1,)),
            dma((CORES * groups - 1,)), dma((CORES * groups - 1,)),
            dma((YS - 1,)), dma((YS - 1,)),
            dma((ZS - 1,)), dma((ZS - 1,)),
            dma((CORES * groups - 1,)), dma((CORES * groups - 1,)),
            dma((groups,)), dma((groups,)),
        ],
        compiler_params=pltpu.CompilerParams(
            collective_id=0, has_side_effects=True, vmem_limit_bytes=VMEM_LIMIT
        ),
        name="step",
    )(psi, ham, conn, face_rows)
    return result[:, 0:nodes].astype(F32)


def solution(mesh):
    placed = (P("band", "space"), P("space", None, None), P("space", None), P("space"))
    return jax.shard_map(
        per_device, mesh=mesh, in_specs=placed, out_specs=P("band", "space"), check_vma=False
    )
```

```python
import functools

import jax
import jax.numpy as jnp
from jax import lax
from jax.experimental import pallas as pl
from jax.experimental.pallas import tpu as pltpu
from jax.sharding import PartitionSpec as P

NODE_EL = 512
OWN_EL = 448
CENTER = 6.25
HALF_WIDTH = 7.5
LO = 256
TAIL = 128
MESH = pl.DeviceIdType.MESH
BF = jnp.bfloat16
F32 = jnp.float32
VMEM_LIMIT = 60 * 1024 * 1024

CORES, YS, ZS, BAND_Z = 2, 8, 4, 3
HAM_PARTS = 4
NT = (((1,), (1,)), ((), ()))
TN = (((0,), (0,)), ((), ()))


def nn(a, b):
    return jnp.dot(a, b, preferred_element_type=F32)


def nt(a, b):
    return lax.dot_general(a, b, NT, preferred_element_type=F32)


def remote(src, dst, send, recv, where):
    return pltpu.make_async_remote_copy(
        src_ref=src, dst_ref=dst, send_sem=send, recv_sem=recv, device_id=where, device_id_type=MESH
    )


def split(value):
    high = value.astype(BF)
    return high, (value - high.astype(F32)).astype(BF)


def split3(value):
    high = value.astype(BF)
    rest = value - high.astype(F32)
    middle = rest.astype(BF)
    return high, middle, (rest - middle.astype(F32)).astype(BF)


def lanes(start, size):
    return pl.ds(pl.multiple_of(start, 128), size)


def pick(table, which, first, count, total):
    bands = total.shape[0]
    for h in range(count):
        total = jnp.where(which == first + h, table[h * bands:(h + 1) * bands, :], total)
    return total


def place(part, which, first, count, columns):
    zero = jnp.zeros_like(part)
    rows = [jnp.where(which == first + h, part, zero) for h in range(count)]
    return nt(jnp.concatenate(rows, axis=0), columns)


def indicator(low, depth):
    shape = depth.shape
    return jnp.where(depth == jnp.broadcast_to(low, shape), jnp.ones(shape, BF), jnp.zeros(shape, BF))


def as_bf(value, rows):
    return jnp.broadcast_to(value.astype(F32), (rows, value.shape[1])).astype(BF)


def factor_inverse(mat, panel, beside, after):
    size, wide = mat.shape
    step = 8
    lane = lax.broadcasted_iota(jnp.int32, (step, 128), 1)
    sub = lax.broadcasted_iota(jnp.int32, (step, 128), 0)
    tiles = range(wide // 128)

    def spread_lane(value, j):
        return jnp.broadcast_to(value[:, j:j + 1], (step, 128))

    def spread_row(value, i):
        return jnp.broadcast_to(value[i:i + 1, :], (step, 128))

    for top in range(0, size, panel):
        if top > 0:
            beside(top - panel, top)
        groups = min(panel, size - top) // step
        block = [
            [mat[top + step * g:top + step * (g + 1), t * 128:(t + 1) * 128] for t in tiles] for g in range(groups)
        ]
        for s in range(groups):
            start = top + step * s
            tile, at = start // 128, start % 128
            columns = [spread_lane(block[s][tile], at + j) for j in range(step)]
            d = {(i, j): spread_row(columns[j], i) for j in range(step) for i in range(j, step)}
            below = [[spread_lane(block[g][tile], at + j) for j in range(step)] for g in range(s + 1, groups)]
            inside = (lane >= at) & (lane < at + step)
            base = [[spread_row(block[s][t], i) for i in range(step)] for t in tiles]
            for i in range(step):
                base[tile][i] = jnp.where(inside, jnp.where(lane == at + i, 1.0, 0.0), base[tile][i])
            rows = [[] for _ in tiles]
            for k in range(step):
                scale = lax.rsqrt(d[k, k])
                factor = {i: d[i, k] * scale for i in range(k + 1, step)}
                for i in range(k + 1, step):
                    for m in range(k + 1, i + 1):
                        d[i, m] = d[i, m] - factor[i] * factor[m]
                for t in tiles:
                    rows[t].append(base[t][k] * scale)
                    for i in range(k + 1, step):
                        base[t][i] = base[t][i] - factor[i] * rows[t][k]
                for part in below:
                    part[k] = part[k] * scale
                    for i in range(k + 1, step):
                        part[i] = part[i] - part[k] * factor[i]
            for t in tiles:
                fresh = rows[t][0]
                for i in range(1, step):
                    fresh = jnp.where(sub == i, rows[t][i], fresh)
                block[s][t] = fresh
            for n, g in enumerate(range(s + 1, groups)):
                for t in tiles:
                    value = block[g][t]
                    if t == tile:
                        value = jnp.where(inside, 0.0, value)
                    for k in range(step):
                        value = value - below[n][k] * rows[t][k]
                    block[g][t] = value
        for g in range(groups):
            for t in tiles:
                mat[top + step * g:top + step * (g + 1), t * 128:(t + 1) * 128] = block[g][t]
        end = top + step * groups
        if end < size:
            first = end // 128 * 128
            fresh = mat[top:end, :]
            row = top + lax.broadcasted_iota(jnp.int32, fresh.shape, 0)
            column = lax.broadcasted_iota(jnp.int32, fresh.shape, 1)
            a, b, c = split3(fresh[:, first:])
            d, e, f = split3(jnp.where((column > row) & (column < end), 0.0, fresh))
            update = lax.dot_general(
                jnp.concatenate([a, a, b, b, a, c], axis=0),
                jnp.concatenate([d, e, d, e, f, d], axis=0),
                TN,
                preferred_element_type=F32,
            )
            rest = mat[end:size, :]
            column = lax.broadcasted_iota(jnp.int32, rest.shape, 1)
            rest = jnp.where((column >= top) & (column < end), 0.0, rest)
            mat[end:size, :] = rest - update[end - first:size - first, :]
        if top > 0:
            after(top - panel, top)


def fold(matrix):
    rest = matrix.shape[0] - 128
    corner = pltpu.roll(matrix[128:, 128:], rest, 1)
    lane = lax.broadcasted_iota(jnp.int32, corner.shape, 1)
    first = jnp.where(lane < rest, matrix[0:rest, 0:128], corner)
    return jnp.concatenate([first, matrix[rest:, 0:128]], axis=0)


def unfold(folded):
    count = folded.shape[0]
    rest = count - 128
    turned = pltpu.roll(folded[rest:, :].T, rest, 1)
    lane = lax.broadcasted_iota(jnp.int32, folded.shape, 1)
    first = jnp.where(lane[0:rest] < rest, folded[0:rest, :], turned[0:rest, :])
    left = jnp.concatenate([first, folded[rest:, :]], axis=0)
    right = jnp.concatenate([turned, pltpu.roll(folded[0:rest, :], rest, 1)], axis=0)
    return jnp.concatenate([left, jnp.where(lane < rest, right, 0.0)], axis=1)


def step_kernel(
    total_nodes, psi_hbm, ham_hbm, conn_hbm, face_hbm, out_ref,
    psi_ref, conn_ref, face_ref, ham, onehot, onehot_ghost, onehot_face, hi_ref, hi_ghost, hi_face, base, field, xb, xg,
    gathered, ghosted, products, high_ref, low_ref, tail_high, kept,
    send1, send2, send3, send4, got1, got2, got3, got4,
    pieces, rows_all, gram, group_in, y_in, z_in, whole, mat, ortho,
    in_sem, ham_sem, own_sem, f_send, f_recv, a_send, a_recv, r_send, r_recv, y_send, y_recv, z_send, z_recv,
    g_send, g_recv, b_send, b_recv,
):
    bands, nodes = psi_ref.shape
    elems = conn_ref.shape[0]
    faces = face_ref.shape[0]
    own_blocks = pl.cdiv(nodes, LO)
    ghost_blocks = pl.cdiv(faces, LO)
    face_pad = got1.shape[1]
    shift = own_blocks * LO - nodes
    domains = lax.axis_size("space")
    space = lax.axis_index("space")
    band = lax.axis_index("band")
    groups, _, width = pieces.shape
    count = groups * bands
    wide = mat.shape[1]
    core = lax.rem(space, CORES)
    y = lax.rem(space // CORES, YS)
    z = space // (CORES * YS)
    below = {"space": lax.rem(space + domains - 1, domains)}
    above = {"space": lax.rem(space + 1, domains)}
    twin = {"space": space + 1 - 2 * core}

    inputs = [
        pltpu.make_async_copy(source, held, in_sem.at[n])
        for n, (source, held) in enumerate([(face_hbm, face_ref), (psi_hbm, psi_ref), (conn_hbm, conn_ref)])
    ]
    for c in inputs:
        c.start()

    band_x = groups // BAND_Z
    steps = [(i, k) for i in range(band_x) for k in range(BAND_Z) if i + k > 0]
    steps.sort(key=lambda step: -(min(step[0], band_x - step[0]) + 1.5 * (step[1] > 0)))

    def band_at(step):
        i, k = step
        return lax.rem(band // BAND_Z + i, band_x) * BAND_Z + lax.rem(lax.rem(band, BAND_Z) + k, BAND_Z)

    def band_peer(step):
        return {"band": band_at(step)}

    def y_peer(d):
        return {"space": (z * YS + lax.rem(y + d, YS)) * CORES + core}

    def z_peer(d):
        return {"space": (lax.rem(z + d, ZS) * YS + y) * CORES + core}

    def group_peer(c, step):
        there = {"band": band_at(step)}
        if c > 0:
            there["space"] = twin["space"]
        return there

    members = [(c, step) for step in steps for c in range(CORES)] + [(1, (0, 0))]
    y_steps = sorted(range(1, YS), key=lambda d: -min(d, YS - d))
    z_steps = sorted(range(1, ZS), key=lambda d: -min(d, ZS - d))
    peers = [below, above]
    peers += [group_peer(c, d) for c, d in members]
    peers += [y_peer(d) for d in y_steps]
    peers += [z_peer(d) for d in z_steps]
    barrier = pltpu.get_barrier_semaphore()
    for there in peers:
        pl.semaphore_signal(barrier, inc=1, device_id=there, device_id_type=MESH)

    per = elems // HAM_PARTS
    ham_copies = []
    for k in range(HAM_PARTS):
        part = slice(k * per, (k + 1) * per)
        ham_copies.append(pltpu.make_async_copy(ham_hbm.at[part], ham.at[part], ham_sem.at[k]))
        ham_copies[-1].start()

    inputs[0].wait()
    depth = lax.broadcasted_iota(jnp.int32, (LO, NODE_EL), 0).astype(F32).astype(BF)
    for k in range(face_pad // 128):
        size = min(128, faces - k * 128)
        named = jnp.full((1, 128), -1, jnp.int32)
        spot = lax.broadcasted_iota(jnp.int32, (1, 128), 1)
        if size == 128:
            named = face_ref[k * 128:(k + 1) * 128].reshape(1, 128)
        else:
            tail = face_ref[faces - 128:faces].reshape(1, 128)
            named = jnp.where(spot < size, pltpu.roll(tail, size, 1), -1)
        cols = slice(k * 128, (k + 1) * 128)
        onehot_face[:, cols] = indicator(as_bf(named & (LO - 1), 1), depth[:, 0:128])
        hi_face[:, cols] = as_bf(named >> 8, bands)

    def take_face(blocks):
        table = nn(blocks, onehot_face[...]).astype(BF)
        return pick(table, hi_face[...], 0, own_blocks, jnp.zeros((bands, face_pad), BF))

    inputs[1].wait()
    for h in range(own_blocks):
        rows = slice(h * bands, (h + 1) * bands)
        if (h + 1) * LO <= nodes:
            value = psi_ref[:, h * LO:(h + 1) * LO]
            base[rows, :] = value
            xb[rows, :] = value.astype(BF)
        else:
            base[rows, :] = jnp.zeros((bands, LO), F32)
            base[rows, 0:nodes - h * LO] = psi_ref[:, h * LO:nodes]
            xb[rows, :] = base[rows, :].astype(BF)
    send1[...] = take_face(xb[...])
    pl.semaphore_wait(barrier, len(peers))
    copy1 = remote(send1, got1, f_send.at[0], f_recv.at[0], below)
    copy1.start()

    inputs[2].wait()
    spot = lax.broadcasted_iota(jnp.int32, (1, NODE_EL), 1)

    def prepare(e, carry):
        named = conn_ref[pl.ds(e, 1), :]
        named = jnp.where(spot >= OWN_EL, named + shift, named)
        marks = indicator(as_bf(named & (LO - 1), 1), depth)
        which = as_bf(named >> 8, bands)
        cols = lanes(e * NODE_EL, NODE_EL)
        onehot[:, cols] = marks
        hi_ref[:, cols] = which
        cols = lanes(e * TAIL, TAIL)
        onehot_ghost[:, cols] = marks[:, NODE_EL - TAIL:]
        hi_ghost[:, cols] = which[:, NODE_EL - TAIL:]
        return carry

    lax.fori_loop(0, elems, prepare, 0, unroll=2)
    xg[...] = jnp.zeros(xg.shape, BF)
    rows_all[count:, :] = jnp.zeros((rows_all.shape[0] - count, width), BF)

    def gather_own():
        def body(e, carry):
            cols = lanes(e * NODE_EL, NODE_EL)
            table = nn(xb[...], onehot[:, cols]).astype(BF)
            gathered[:, cols] = pick(table, hi_ref[:, cols], 0, own_blocks, jnp.zeros((bands, NODE_EL), BF))
            return carry

        lax.fori_loop(0, elems, body, 0, unroll=12)

    def gather_ghost(values):
        for h in range(ghost_blocks):
            size = min(LO, face_pad - h * LO)
            xg[h * bands:(h + 1) * bands, 0:size] = values[:, h * LO:h * LO + size].astype(BF)
        table = nn(xg[...], onehot_ghost[...]).astype(BF)
        ghosted[...] = pick(table, hi_ghost[...], own_blocks, ghost_blocks, jnp.zeros((bands, elems * TAIL), BF))

    def multiply_own():
        def body(e, carry):
            cols = lanes(e * NODE_EL, NODE_EL)
            products[:, cols] = nn(gathered[:, cols], ham[e])
            return carry

        lax.fori_loop(0, elems, body, 0, unroll=4)

    def tail_cols(e):
        return slice((e + 1) * NODE_EL - TAIL, (e + 1) * NODE_EL)

    def multiply_tail():
        for e in range(elems):
            cols = slice(e * NODE_EL, (e + 1) * NODE_EL)
            products[:, tail_cols(e)] = nn(gathered[:, cols], ham[e, :, NODE_EL - TAIL:])

    def upper():
        for e in range(elems):
            some = slice(e * TAIL, (e + 1) * TAIL)
            cols = tail_cols(e)
            value = products[:, cols] + nn(ghosted[:, some], ham[e, NODE_EL - TAIL:, NODE_EL - TAIL:])
            high, low = split(value)
            tail_high[:, some] = high
            high_ref[:, cols], low_ref[:, cols] = high, low
        total = place(tail_high[...], hi_ghost[...], own_blocks, ghost_blocks, onehot_ghost[...])
        parts = [
            total[h * bands:(h + 1) * bands, 0:min(LO, face_pad - h * LO)] for h in range(ghost_blocks)
        ]
        return jnp.concatenate(parts, axis=1)

    def multiply_ghost():
        def body(e, carry):
            some = lanes(e * TAIL, TAIL)
            cols = lanes(e * NODE_EL, NODE_EL - TAIL)
            value = products[:, cols] + nn(ghosted[:, some], ham[e, NODE_EL - TAIL:, 0:NODE_EL - TAIL])
            high_ref[:, cols], low_ref[:, cols] = split(value)
            return carry

        lax.fori_loop(0, elems, body, 0, unroll=4)

    def multiply_rest():
        for e in range(elems):
            gathered[:, tail_cols(e)] = gathered[:, tail_cols(e)] + ghosted[:, e * TAIL:(e + 1) * TAIL]

        def body(e, carry):
            cols = lanes(e * NODE_EL, NODE_EL - TAIL)
            value = nn(gathered[:, lanes(e * NODE_EL, NODE_EL)], ham[e, :, 0:NODE_EL - TAIL])
            high_ref[:, cols], low_ref[:, cols] = split(value)
            return carry

        lax.fori_loop(0, elems, body, 0, unroll=4)

    def scatter_own(part):
        size = elems * NODE_EL // 4
        total = None
        for k in range(4):
            cols = slice(k * size, (k + 1) * size)
            value = place(part[:, cols], hi_ref[:, cols], 0, own_blocks, onehot[:, cols])
            total = value if total is None else total + value
        return total

    def put_face(received):
        return place(received, hi_face[...], 0, own_blocks, onehot_face[...])

    gather_own()
    for c in ham_copies:
        c.wait()
    multiply_own()
    copy1.wait()
    gather_ghost(got1[...])
    kept[...] = upper()
    send2[...] = kept[...].astype(BF)
    copy2 = remote(send2, got2, f_send.at[1], f_recv.at[1], above)
    copy2.start()
    multiply_ghost()
    partial_value = scatter_own(high_ref) - CENTER * base[...]
    field[...] = partial_value
    send3[...] = take_face((partial_value / HALF_WIDTH).astype(BF))
    copy3 = remote(send3, got3, f_send.at[2], f_recv.at[2], below)
    copy3.start()
    field[...] += scatter_own(low_ref)
    copy2.wait()
    field[...] = (field[...] + put_face(got2[...])) / HALF_WIDTH
    xb[...] = field[...].astype(BF)
    gather_own()
    multiply_tail()
    copy3.wait()
    gather_ghost(got3[...].astype(F32) + kept[...] / HALF_WIDTH)
    send4[...] = upper().astype(BF)
    copy4 = remote(send4, got4, f_send.at[3], f_recv.at[3], above)
    copy4.start()
    multiply_rest()
    partial_value = scatter_own(high_ref) + scatter_own(low_ref) - CENTER * field[...]
    copy4.wait()
    field[...] = 2.0 * ((partial_value + put_face(got4[...])) / HALF_WIDTH) - base[...]

    blocks = width // 128
    for piece in range(groups * blocks):
        dst = slice((piece % blocks) * 128, (piece % blocks + 1) * 128)
        if piece // 2 < own_blocks:
            rows = slice(piece // 2 * bands, (piece // 2 + 1) * bands)
            src = slice((piece % 2) * 128, (piece % 2 + 1) * 128)
            pieces[piece // blocks, :, dst] = field[rows, src].astype(BF)
        else:
            pieces[piece // blocks, :, dst] = jnp.zeros((bands, 128), BF)

    def finish(copies):
        for c in copies:
            c.wait()

    mine = pl.ds(pl.multiple_of(band * bands, bands), bands)
    copies = []
    for n, step in enumerate(steps):
        there = band_peer(step)
        copies.append(remote(pieces.at[there["band"]], rows_all.at[mine], a_send.at[n], a_recv.at[n], there))
        copies[-1].start()
    rows_all[mine, :] = pieces[band]
    finish(copies)

    folded = fold(nt(rows_all[0:count, :], rows_all[...]))
    gram[...] = folded.reshape(gram.shape)
    copies = []
    for n, (c, d) in enumerate(members):
        there = group_peer(c, d)
        tile = gram.at[core if c == 0 else 1 - core, there["band"]]
        copies.append(remote(tile, group_in.at[n], r_send.at[n], r_recv.at[n], there))
        copies[-1].start()
    finish(copies)
    value = gram[core, band]
    for n in range(len(members)):
        value = value + group_in[n]
    y_in[y] = value

    copies = []
    for d in y_steps:
        copies.append(remote(y_in.at[y], y_in.at[y], y_send.at[d - 1], y_recv.at[d - 1], y_peer(d)))
        copies[-1].start()
    finish(copies)
    value = y_in[0]
    for k in range(1, YS):
        value = value + y_in[k]
    z_in[z] = value

    copies = []
    for d in z_steps:
        copies.append(remote(z_in.at[z], z_in.at[z], z_send.at[d - 1], z_recv.at[d - 1], z_peer(d)))
        copies[-1].start()
    finish(copies)
    value = z_in[0]
    for k in range(1, ZS):
        value = value + z_in[k]
    whole[core, band] = value

    copies = []
    piece = whole.at[core, band]
    for n, (c, d) in enumerate(members):
        copies.append(remote(piece, piece, g_send.at[n], g_recv.at[n], group_peer(c, d)))
        copies[-1].start()
    finish(copies)

    mat[...] = unfold(whole[...].reshape(count, 128) / total_nodes)

    def landing(source):
        return out_ref.at[:, lanes(source * width, width)]

    def back(k):
        return remote(ortho.at[k], landing(band), b_send.at[k], b_recv.at[band], {"band": k})

    def keep(k):
        return pltpu.make_async_copy(ortho.at[k], landing(band), own_sem)

    def rows_of(start, end):
        value = mat[start:end, :]
        row = start + lax.broadcasted_iota(jnp.int32, value.shape, 0)
        column = lax.broadcasted_iota(jnp.int32, value.shape, 1)
        parts = jnp.concatenate(split(jnp.where(column <= row, value, 0.0)), axis=0)
        both = nn(parts, rows_all[...])
        value = (both[0:end - start] + both[end - start:]).astype(BF)
        ortho[start // bands:end // bands] = value.reshape((end - start) // bands, bands, width)

    def deliver(start, end):
        for k in range(start // bands, end // bands):
            @pl.when(band != k)
            def _():
                back(k).start()

            @pl.when(band == k)
            def _():
                keep(k).start()

    panel = 2 * bands
    factor_inverse(mat, panel, rows_of, deliver)
    rows_of(count - panel, count)
    deliver(count - panel, count)
    for k in range(groups):
        @pl.when(band != k)
        def _():
            back(k).wait_send()
            remote(ortho.at[k], landing(k), b_send.at[k], b_recv.at[k], {"band": k}).wait_recv()

        @pl.when(band == k)
        def _():
            keep(k).wait()


def per_device(psi, ham, conn, face_rows):
    bands, nodes = psi.shape
    elems = conn.shape[0]
    faces = face_rows.shape[0]
    groups = lax.axis_size("band")
    own_blocks = pl.cdiv(nodes, LO)
    ghost_blocks = pl.cdiv(faces, LO)
    face_pad = pl.cdiv(faces, 128) * 128
    width = pl.cdiv(pl.cdiv(nodes, 128), groups) * 128
    own = own_blocks * bands
    entries = elems * NODE_EL
    count = groups * bands
    wide = pl.cdiv(count, 128) * 128
    unit = count // 2 // groups
    anywhere = pl.BlockSpec(memory_space=pl.ANY)
    dma = pltpu.SemaphoreType.DMA

    result = pl.pallas_call(
        functools.partial(step_kernel, float(nodes * lax.axis_size("space"))),
        out_shape=pltpu.VMEM((bands, groups * width), BF),
        in_specs=[anywhere] * 4,
        out_specs=pl.BlockSpec(memory_space=pltpu.VMEM),
        scratch_shapes=[
            pltpu.VMEM(psi.shape, F32),
            pltpu.VMEM(conn.shape, jnp.int32),
            pltpu.VMEM(face_rows.shape, jnp.int32),
            pltpu.VMEM(ham.shape, BF),
            pltpu.VMEM((LO, entries), BF),
            pltpu.VMEM((LO, elems * TAIL), BF),
            pltpu.VMEM((LO, face_pad), BF),
            pltpu.VMEM((bands, entries), BF),
            pltpu.VMEM((bands, elems * TAIL), BF),
            pltpu.VMEM((bands, face_pad), BF),
            pltpu.VMEM((own, LO), F32),
            pltpu.VMEM((own, LO), F32),
            pltpu.VMEM((own, LO), BF),
            pltpu.VMEM((ghost_blocks * bands, LO), BF),
            pltpu.VMEM((bands, entries), BF),
            pltpu.VMEM((bands, elems * TAIL), BF),
            pltpu.VMEM((bands, entries), F32),
            pltpu.VMEM((bands, entries), BF),
            pltpu.VMEM((bands, entries), BF),
            pltpu.VMEM((bands, elems * TAIL), BF),
            pltpu.VMEM((bands, face_pad), F32),
            pltpu.VMEM((bands, face_pad), BF),
            pltpu.VMEM((bands, face_pad), BF),
            pltpu.VMEM((bands, face_pad), BF),
            pltpu.VMEM((bands, face_pad), BF),
            pltpu.VMEM((bands, face_pad), BF),
            pltpu.VMEM((bands, face_pad), BF),
            pltpu.VMEM((bands, face_pad), BF),
            pltpu.VMEM((bands, face_pad), BF),
            pltpu.VMEM((groups, bands, width), BF),
            pltpu.VMEM((wide, width), BF),
            pltpu.VMEM((CORES, groups, unit, 128), F32),
            pltpu.VMEM((CORES * groups - 1, unit, 128), F32),
            pltpu.VMEM((YS, unit, 128), F32),
            pltpu.VMEM((ZS, unit, 128), F32),
            pltpu.VMEM((CORES, groups, unit, 128), F32),
            pltpu.VMEM((count, wide), F32),
            pltpu.VMEM((groups, bands, width), BF),
            dma((3,)), dma((HAM_PARTS,)), dma,
            dma((4,)), dma((4,)),
            dma((groups - 1,)), dma((groups - 1,)),
            dma((CORES * groups - 1,)), dma((CORES * groups - 1,)),
            dma((YS - 1,)), dma((YS - 1,)),
            dma((ZS - 1,)), dma((ZS - 1,)),
            dma((CORES * groups - 1,)), dma((CORES * groups - 1,)),
            dma((groups,)), dma((groups,)),
        ],
        compiler_params=pltpu.CompilerParams(
            collective_id=0, has_side_effects=True, vmem_limit_bytes=VMEM_LIMIT
        ),
        name="step",
    )(psi, ham, conn, face_rows)
    return result[:, 0:nodes].astype(F32)


def solution(mesh):
    placed = (P("band", "space"), P("space", None, None), P("space", None), P("space"))
    return jax.shard_map(
        per_device, mesh=mesh, in_specs=placed, out_specs=P("band", "space"), check_vma=False
    )
```

```python
import functools

import jax
import jax.numpy as jnp
from jax import lax
from jax.experimental import pallas as pl
from jax.experimental.pallas import tpu as pltpu
from jax.sharding import PartitionSpec as P

NODE_EL = 512
OWN_EL = 448
CENTER = 6.25
HALF_WIDTH = 7.5
LO = 256
TAIL = 128
MESH = pl.DeviceIdType.MESH
BF = jnp.bfloat16
F32 = jnp.float32
VMEM_LIMIT = 60 * 1024 * 1024

CORES, YS, ZS, BAND_Z = 2, 8, 4, 3
HAM_PARTS = 4
NT = (((1,), (1,)), ((), ()))
TN = (((0,), (0,)), ((), ()))


def nn(a, b):
    return jnp.dot(a, b, preferred_element_type=F32)


def nt(a, b):
    return lax.dot_general(a, b, NT, preferred_element_type=F32)


def remote(src, dst, send, recv, where):
    return pltpu.make_async_remote_copy(
        src_ref=src, dst_ref=dst, send_sem=send, recv_sem=recv, device_id=where, device_id_type=MESH
    )


def split(value):
    high = value.astype(BF)
    return high, (value - high.astype(F32)).astype(BF)


def split3(value):
    high = value.astype(BF)
    rest = value - high.astype(F32)
    middle = rest.astype(BF)
    return high, middle, (rest - middle.astype(F32)).astype(BF)


def lanes(start, size):
    return pl.ds(pl.multiple_of(start, 128), size)


def pick(table, which, first, count, total):
    bands = total.shape[0]
    for h in range(count):
        total = jnp.where(which == first + h, table[h * bands:(h + 1) * bands, :], total)
    return total


def place(part, which, first, count, columns):
    zero = jnp.zeros_like(part)
    rows = [jnp.where(which == first + h, part, zero) for h in range(count)]
    return nt(jnp.concatenate(rows, axis=0), columns)


def indicator(low, depth):
    shape = depth.shape
    return jnp.where(depth == jnp.broadcast_to(low, shape), jnp.ones(shape, BF), jnp.zeros(shape, BF))


def as_bf(value, rows):
    return jnp.broadcast_to(value.astype(F32), (rows, value.shape[1])).astype(BF)


def factor_inverse(mat, tops, beside, after):
    size, wide = mat.shape
    step = 8
    lane = lax.broadcasted_iota(jnp.int32, (step, 128), 1)
    sub = lax.broadcasted_iota(jnp.int32, (step, 128), 0)
    tiles = range(wide // 128)

    def spread_lane(value, j):
        return jnp.broadcast_to(value[:, j:j + 1], (step, 128))

    def spread_row(value, i):
        return jnp.broadcast_to(value[i:i + 1, :], (step, 128))

    for number, top in enumerate(tops):
        if number > 0:
            beside(tops[number - 1], top)
        groups = (tops[number + 1] - top if number + 1 < len(tops) else size - top) // step
        block = [
            [mat[top + step * g:top + step * (g + 1), t * 128:(t + 1) * 128] for t in tiles] for g in range(groups)
        ]
        for s in range(groups):
            start = top + step * s
            tile, at = start // 128, start % 128
            columns = [spread_lane(block[s][tile], at + j) for j in range(step)]
            d = {(i, j): spread_row(columns[j], i) for j in range(step) for i in range(j, step)}
            below = [[spread_lane(block[g][tile], at + j) for j in range(step)] for g in range(s + 1, groups)]
            inside = (lane >= at) & (lane < at + step)
            base = [[spread_row(block[s][t], i) for i in range(step)] for t in tiles]
            for i in range(step):
                base[tile][i] = jnp.where(inside, jnp.where(lane == at + i, 1.0, 0.0), base[tile][i])
            rows = [[] for _ in tiles]
            for k in range(step):
                scale = lax.rsqrt(d[k, k])
                factor = {i: d[i, k] * scale for i in range(k + 1, step)}
                for i in range(k + 1, step):
                    for m in range(k + 1, i + 1):
                        d[i, m] = d[i, m] - factor[i] * factor[m]
                for t in tiles:
                    rows[t].append(base[t][k] * scale)
                    for i in range(k + 1, step):
                        base[t][i] = base[t][i] - factor[i] * rows[t][k]
                for part in below:
                    part[k] = part[k] * scale
                    for i in range(k + 1, step):
                        part[i] = part[i] - part[k] * factor[i]
            for t in tiles:
                fresh = rows[t][0]
                for i in range(1, step):
                    fresh = jnp.where(sub == i, rows[t][i], fresh)
                block[s][t] = fresh
            for n, g in enumerate(range(s + 1, groups)):
                for t in tiles:
                    value = block[g][t]
                    if t == tile:
                        value = jnp.where(inside, 0.0, value)
                    for k in range(step):
                        value = value - below[n][k] * rows[t][k]
                    block[g][t] = value
        for g in range(groups):
            for t in tiles:
                mat[top + step * g:top + step * (g + 1), t * 128:(t + 1) * 128] = block[g][t]
        end = top + step * groups
        if end < size:
            first = end // 128 * 128
            fresh = mat[top:end, :]
            row = top + lax.broadcasted_iota(jnp.int32, fresh.shape, 0)
            column = lax.broadcasted_iota(jnp.int32, fresh.shape, 1)
            a, b, c = split3(fresh[:, first:])
            d, e, f = split3(jnp.where((column > row) & (column < end), 0.0, fresh))
            update = lax.dot_general(
                jnp.concatenate([a, a, b, b, a, c], axis=0),
                jnp.concatenate([d, e, d, e, f, d], axis=0),
                TN,
                preferred_element_type=F32,
            )
            rest = mat[end:size, :]
            column = lax.broadcasted_iota(jnp.int32, rest.shape, 1)
            rest = jnp.where((column >= top) & (column < end), 0.0, rest)
            mat[end:size, :] = rest - update[end - first:size - first, :]
        if number > 0:
            after(tops[number - 1], top)


def fold(matrix):
    rest = matrix.shape[0] - 128
    corner = pltpu.roll(matrix[128:, 128:], rest, 1)
    lane = lax.broadcasted_iota(jnp.int32, corner.shape, 1)
    first = jnp.where(lane < rest, matrix[0:rest, 0:128], corner)
    return jnp.concatenate([first, matrix[rest:, 0:128]], axis=0)


def unfold(folded):
    count = folded.shape[0]
    rest = count - 128
    turned = pltpu.roll(folded[rest:, :].T, rest, 1)
    lane = lax.broadcasted_iota(jnp.int32, folded.shape, 1)
    first = jnp.where(lane[0:rest] < rest, folded[0:rest, :], turned[0:rest, :])
    left = jnp.concatenate([first, folded[rest:, :]], axis=0)
    right = jnp.concatenate([turned, pltpu.roll(folded[0:rest, :], rest, 1)], axis=0)
    return jnp.concatenate([left, jnp.where(lane < rest, right, 0.0)], axis=1)


def step_kernel(
    total_nodes, psi_hbm, ham_hbm, conn_hbm, face_hbm, out_ref,
    psi_ref, conn_ref, face_ref, ham, onehot, onehot_ghost, onehot_face, hi_ref, hi_ghost, hi_face, base, field, xb, xg,
    gathered, ghosted, products, high_ref, low_ref, tail_high, kept,
    send1, send2, send3, send4, got1, got2, got3, got4,
    pieces, rows_all, gram, group_in, y_in, z_in, whole, mat, ortho,
    in_sem, ham_sem, own_sem, f_send, f_recv, a_send, a_recv, r_send, r_recv, y_send, y_recv, z_send, z_recv,
    g_send, g_recv, b_send, b_recv,
):
    bands, nodes = psi_ref.shape
    elems = conn_ref.shape[0]
    faces = face_ref.shape[0]
    own_blocks = pl.cdiv(nodes, LO)
    ghost_blocks = pl.cdiv(faces, LO)
    face_pad = got1.shape[1]
    shift = own_blocks * LO - nodes
    domains = lax.axis_size("space")
    space = lax.axis_index("space")
    band = lax.axis_index("band")
    groups, _, width = pieces.shape
    count = groups * bands
    wide = mat.shape[1]
    core = lax.rem(space, CORES)
    y = lax.rem(space // CORES, YS)
    z = space // (CORES * YS)
    below = {"space": lax.rem(space + domains - 1, domains)}
    above = {"space": lax.rem(space + 1, domains)}
    twin = {"space": space + 1 - 2 * core}

    inputs = [
        pltpu.make_async_copy(source, held, in_sem.at[n])
        for n, (source, held) in enumerate([(face_hbm, face_ref), (psi_hbm, psi_ref), (conn_hbm, conn_ref)])
    ]
    for c in inputs:
        c.start()

    band_x = groups // BAND_Z
    steps = [(i, k) for i in range(band_x) for k in range(BAND_Z) if i + k > 0]
    steps.sort(key=lambda step: -(min(step[0], band_x - step[0]) + 1.5 * (step[1] > 0)))

    def band_at(step):
        i, k = step
        return lax.rem(band // BAND_Z + i, band_x) * BAND_Z + lax.rem(lax.rem(band, BAND_Z) + k, BAND_Z)

    def band_peer(step):
        return {"band": band_at(step)}

    def y_peer(d):
        return {"space": (z * YS + lax.rem(y + d, YS)) * CORES + core}

    def z_peer(d):
        return {"space": (lax.rem(z + d, ZS) * YS + y) * CORES + core}

    def group_peer(c, step):
        there = {"band": band_at(step)}
        if c > 0:
            there["space"] = twin["space"]
        return there

    members = [(c, step) for step in steps for c in range(CORES)] + [(1, (0, 0))]
    y_steps = sorted(range(1, YS), key=lambda d: -min(d, YS - d))
    z_steps = sorted(range(1, ZS), key=lambda d: -min(d, ZS - d))
    peers = [below, above]
    peers += [group_peer(c, d) for c, d in members]
    peers += [y_peer(d) for d in y_steps]
    peers += [z_peer(d) for d in z_steps]
    barrier = pltpu.get_barrier_semaphore()
    for there in peers:
        pl.semaphore_signal(barrier, inc=1, device_id=there, device_id_type=MESH)

    per = elems // HAM_PARTS
    ham_copies = []
    for k in range(HAM_PARTS):
        part = slice(k * per, (k + 1) * per)
        ham_copies.append(pltpu.make_async_copy(ham_hbm.at[part], ham.at[part], ham_sem.at[k]))
        ham_copies[-1].start()

    inputs[0].wait()
    depth = lax.broadcasted_iota(jnp.int32, (LO, NODE_EL), 0).astype(F32).astype(BF)
    for k in range(face_pad // 128):
        size = min(128, faces - k * 128)
        named = jnp.full((1, 128), -1, jnp.int32)
        spot = lax.broadcasted_iota(jnp.int32, (1, 128), 1)
        if size == 128:
            named = face_ref[k * 128:(k + 1) * 128].reshape(1, 128)
        else:
            tail = face_ref[faces - 128:faces].reshape(1, 128)
            named = jnp.where(spot < size, pltpu.roll(tail, size, 1), -1)
        cols = slice(k * 128, (k + 1) * 128)
        onehot_face[:, cols] = indicator(as_bf(named & (LO - 1), 1), depth[:, 0:128])
        hi_face[:, cols] = as_bf(named >> 8, bands)

    def take_face(blocks):
        table = nn(blocks, onehot_face[...]).astype(BF)
        return pick(table, hi_face[...], 0, own_blocks, jnp.zeros((bands, face_pad), BF))

    inputs[1].wait()
    for h in range(own_blocks):
        rows = slice(h * bands, (h + 1) * bands)
        if (h + 1) * LO <= nodes:
            value = psi_ref[:, h * LO:(h + 1) * LO]
            base[rows, :] = value
            xb[rows, :] = value.astype(BF)
        else:
            base[rows, :] = jnp.zeros((bands, LO), F32)
            base[rows, 0:nodes - h * LO] = psi_ref[:, h * LO:nodes]
            xb[rows, :] = base[rows, :].astype(BF)
    send1[...] = take_face(xb[...])
    pl.semaphore_wait(barrier, len(peers))
    copy1 = remote(send1, got1, f_send.at[0], f_recv.at[0], below)
    copy1.start()

    inputs[2].wait()
    spot = lax.broadcasted_iota(jnp.int32, (1, NODE_EL), 1)

    def prepare(e, carry):
        named = conn_ref[pl.ds(e, 1), :]
        named = jnp.where(spot >= OWN_EL, named + shift, named)
        marks = indicator(as_bf(named & (LO - 1), 1), depth)
        which = as_bf(named >> 8, bands)
        cols = lanes(e * NODE_EL, NODE_EL)
        onehot[:, cols] = marks
        hi_ref[:, cols] = which
        cols = lanes(e * TAIL, TAIL)
        onehot_ghost[:, cols] = marks[:, NODE_EL - TAIL:]
        hi_ghost[:, cols] = which[:, NODE_EL - TAIL:]
        return carry

    lax.fori_loop(0, elems, prepare, 0, unroll=2)
    xg[...] = jnp.zeros(xg.shape, BF)
    rows_all[count:, :] = jnp.zeros((rows_all.shape[0] - count, width), BF)

    def gather_own():
        def body(e, carry):
            cols = lanes(e * NODE_EL, NODE_EL)
            table = nn(xb[...], onehot[:, cols]).astype(BF)
            gathered[:, cols] = pick(table, hi_ref[:, cols], 0, own_blocks, jnp.zeros((bands, NODE_EL), BF))
            return carry

        lax.fori_loop(0, elems, body, 0, unroll=12)

    def gather_ghost(values):
        for h in range(ghost_blocks):
            size = min(LO, face_pad - h * LO)
            xg[h * bands:(h + 1) * bands, 0:size] = values[:, h * LO:h * LO + size].astype(BF)
        table = nn(xg[...], onehot_ghost[...]).astype(BF)
        ghosted[...] = pick(table, hi_ghost[...], own_blocks, ghost_blocks, jnp.zeros((bands, elems * TAIL), BF))

    def multiply_own():
        def body(e, carry):
            cols = lanes(e * NODE_EL, NODE_EL)
            products[:, cols] = nn(gathered[:, cols], ham[e])
            return carry

        lax.fori_loop(0, elems, body, 0, unroll=4)

    def tail_cols(e):
        return slice((e + 1) * NODE_EL - TAIL, (e + 1) * NODE_EL)

    def multiply_tail():
        for e in range(elems):
            cols = slice(e * NODE_EL, (e + 1) * NODE_EL)
            products[:, tail_cols(e)] = nn(gathered[:, cols], ham[e, :, NODE_EL - TAIL:])

    def upper():
        for e in range(elems):
            some = slice(e * TAIL, (e + 1) * TAIL)
            cols = tail_cols(e)
            value = products[:, cols] + nn(ghosted[:, some], ham[e, NODE_EL - TAIL:, NODE_EL - TAIL:])
            high, low = split(value)
            tail_high[:, some] = high
            high_ref[:, cols], low_ref[:, cols] = high, low
        total = place(tail_high[...], hi_ghost[...], own_blocks, ghost_blocks, onehot_ghost[...])
        parts = [
            total[h * bands:(h + 1) * bands, 0:min(LO, face_pad - h * LO)] for h in range(ghost_blocks)
        ]
        return jnp.concatenate(parts, axis=1)

    def multiply_ghost():
        def body(e, carry):
            some = lanes(e * TAIL, TAIL)
            cols = lanes(e * NODE_EL, NODE_EL - TAIL)
            value = products[:, cols] + nn(ghosted[:, some], ham[e, NODE_EL - TAIL:, 0:NODE_EL - TAIL])
            high_ref[:, cols], low_ref[:, cols] = split(value)
            return carry

        lax.fori_loop(0, elems, body, 0, unroll=4)

    def multiply_rest():
        for e in range(elems):
            gathered[:, tail_cols(e)] = gathered[:, tail_cols(e)] + ghosted[:, e * TAIL:(e + 1) * TAIL]

        def body(e, carry):
            cols = lanes(e * NODE_EL, NODE_EL - TAIL)
            value = nn(gathered[:, lanes(e * NODE_EL, NODE_EL)], ham[e, :, 0:NODE_EL - TAIL])
            high_ref[:, cols], low_ref[:, cols] = split(value)
            return carry

        lax.fori_loop(0, elems, body, 0, unroll=4)

    def scatter_own(part):
        size = elems * NODE_EL // 4
        total = None
        for k in range(4):
            cols = slice(k * size, (k + 1) * size)
            value = place(part[:, cols], hi_ref[:, cols], 0, own_blocks, onehot[:, cols])
            total = value if total is None else total + value
        return total

    def put_face(received):
        return place(received, hi_face[...], 0, own_blocks, onehot_face[...])

    gather_own()
    for c in ham_copies:
        c.wait()
    multiply_own()
    copy1.wait()
    gather_ghost(got1[...])
    kept[...] = upper()
    send2[...] = kept[...].astype(BF)
    copy2 = remote(send2, got2, f_send.at[1], f_recv.at[1], above)
    copy2.start()
    multiply_ghost()
    partial_value = scatter_own(high_ref) - CENTER * base[...]
    field[...] = partial_value
    send3[...] = take_face((partial_value / HALF_WIDTH).astype(BF))
    copy3 = remote(send3, got3, f_send.at[2], f_recv.at[2], below)
    copy3.start()
    field[...] += scatter_own(low_ref)
    copy2.wait()
    field[...] = (field[...] + put_face(got2[...])) / HALF_WIDTH
    xb[...] = field[...].astype(BF)
    gather_own()
    multiply_tail()
    copy3.wait()
    gather_ghost(got3[...].astype(F32) + kept[...] / HALF_WIDTH)
    send4[...] = upper().astype(BF)
    copy4 = remote(send4, got4, f_send.at[3], f_recv.at[3], above)
    copy4.start()
    multiply_rest()
    partial_value = scatter_own(high_ref) + scatter_own(low_ref) - CENTER * field[...]
    copy4.wait()
    field[...] = 2.0 * ((partial_value + put_face(got4[...])) / HALF_WIDTH) - base[...]

    blocks = width // 128
    for piece in range(groups * blocks):
        dst = slice((piece % blocks) * 128, (piece % blocks + 1) * 128)
        if piece // 2 < own_blocks:
            rows = slice(piece // 2 * bands, (piece // 2 + 1) * bands)
            src = slice((piece % 2) * 128, (piece % 2 + 1) * 128)
            pieces[piece // blocks, :, dst] = field[rows, src].astype(BF)
        else:
            pieces[piece // blocks, :, dst] = jnp.zeros((bands, 128), BF)

    def finish(copies):
        for c in copies:
            c.wait()

    mine = pl.ds(pl.multiple_of(band * bands, bands), bands)
    copies = []
    for n, step in enumerate(steps):
        there = band_peer(step)
        copies.append(remote(pieces.at[there["band"]], rows_all.at[mine], a_send.at[n], a_recv.at[n], there))
        copies[-1].start()
    rows_all[mine, :] = pieces[band]
    finish(copies)

    folded = fold(nt(rows_all[0:count, :], rows_all[...]))
    gram[...] = folded.reshape(gram.shape)
    copies = []
    for n, (c, d) in enumerate(members):
        there = group_peer(c, d)
        tile = gram.at[core if c == 0 else 1 - core, there["band"]]
        copies.append(remote(tile, group_in.at[n], r_send.at[n], r_recv.at[n], there))
        copies[-1].start()
    finish(copies)
    value = gram[core, band]
    for n in range(len(members)):
        value = value + group_in[n]
    y_in[y] = value

    copies = []
    for d in y_steps:
        copies.append(remote(y_in.at[y], y_in.at[y], y_send.at[d - 1], y_recv.at[d - 1], y_peer(d)))
        copies[-1].start()
    finish(copies)
    value = y_in[0]
    for k in range(1, YS):
        value = value + y_in[k]
    z_in[z] = value

    copies = []
    for d in z_steps:
        copies.append(remote(z_in.at[z], z_in.at[z], z_send.at[d - 1], z_recv.at[d - 1], z_peer(d)))
        copies[-1].start()
    finish(copies)
    value = z_in[0]
    for k in range(1, ZS):
        value = value + z_in[k]
    whole[core, band] = value

    copies = []
    piece = whole.at[core, band]
    for n, (c, d) in enumerate(members):
        copies.append(remote(piece, piece, g_send.at[n], g_recv.at[n], group_peer(c, d)))
        copies[-1].start()
    finish(copies)

    mat[...] = unfold(whole[...].reshape(count, 128) / total_nodes)

    def landing(source):
        return out_ref.at[:, lanes(source * width, width)]

    def back(k):
        return remote(ortho.at[k], landing(band), b_send.at[k], b_recv.at[band], {"band": k})

    def keep(k):
        return pltpu.make_async_copy(ortho.at[k], landing(band), own_sem)

    def rows_of(start, end):
        value = mat[start:end, :]
        row = start + lax.broadcasted_iota(jnp.int32, value.shape, 0)
        column = lax.broadcasted_iota(jnp.int32, value.shape, 1)
        parts = jnp.concatenate(split(jnp.where(column <= row, value, 0.0)), axis=0)
        both = nn(parts, rows_all[...])
        value = (both[0:end - start] + both[end - start:]).astype(BF)
        ortho[start // bands:end // bands] = value.reshape((end - start) // bands, bands, width)

    def deliver(start, end):
        for k in range(start // bands, end // bands):
            @pl.when(band != k)
            def _():
                back(k).start()

            @pl.when(band == k)
            def _():
                keep(k).start()

    tops = list(range(0, count, 2 * bands)) + [count - bands]
    factor_inverse(mat, tops, rows_of, deliver)
    rows_of(tops[-1], count)
    deliver(tops[-1], count)
    for k in range(groups):
        @pl.when(band != k)
        def _():
            back(k).wait_send()
            remote(ortho.at[k], landing(k), b_send.at[k], b_recv.at[k], {"band": k}).wait_recv()

        @pl.when(band == k)
        def _():
            keep(k).wait()


def per_device(psi, ham, conn, face_rows):
    bands, nodes = psi.shape
    elems = conn.shape[0]
    faces = face_rows.shape[0]
    groups = lax.axis_size("band")
    own_blocks = pl.cdiv(nodes, LO)
    ghost_blocks = pl.cdiv(faces, LO)
    face_pad = pl.cdiv(faces, 128) * 128
    width = pl.cdiv(pl.cdiv(nodes, 128), groups) * 128
    own = own_blocks * bands
    entries = elems * NODE_EL
    count = groups * bands
    wide = pl.cdiv(count, 128) * 128
    unit = count // 2 // groups
    anywhere = pl.BlockSpec(memory_space=pl.ANY)
    dma = pltpu.SemaphoreType.DMA

    result = pl.pallas_call(
        functools.partial(step_kernel, float(nodes * lax.axis_size("space"))),
        out_shape=pltpu.VMEM((bands, groups * width), BF),
        in_specs=[anywhere] * 4,
        out_specs=pl.BlockSpec(memory_space=pltpu.VMEM),
        scratch_shapes=[
            pltpu.VMEM(psi.shape, F32),
            pltpu.VMEM(conn.shape, jnp.int32),
            pltpu.VMEM(face_rows.shape, jnp.int32),
            pltpu.VMEM(ham.shape, BF),
            pltpu.VMEM((LO, entries), BF),
            pltpu.VMEM((LO, elems * TAIL), BF),
            pltpu.VMEM((LO, face_pad), BF),
            pltpu.VMEM((bands, entries), BF),
            pltpu.VMEM((bands, elems * TAIL), BF),
            pltpu.VMEM((bands, face_pad), BF),
            pltpu.VMEM((own, LO), F32),
            pltpu.VMEM((own, LO), F32),
            pltpu.VMEM((own, LO), BF),
            pltpu.VMEM((ghost_blocks * bands, LO), BF),
            pltpu.VMEM((bands, entries), BF),
            pltpu.VMEM((bands, elems * TAIL), BF),
            pltpu.VMEM((bands, entries), F32),
            pltpu.VMEM((bands, entries), BF),
            pltpu.VMEM((bands, entries), BF),
            pltpu.VMEM((bands, elems * TAIL), BF),
            pltpu.VMEM((bands, face_pad), F32),
            pltpu.VMEM((bands, face_pad), BF),
            pltpu.VMEM((bands, face_pad), BF),
            pltpu.VMEM((bands, face_pad), BF),
            pltpu.VMEM((bands, face_pad), BF),
            pltpu.VMEM((bands, face_pad), BF),
            pltpu.VMEM((bands, face_pad), BF),
            pltpu.VMEM((bands, face_pad), BF),
            pltpu.VMEM((bands, face_pad), BF),
            pltpu.VMEM((groups, bands, width), BF),
            pltpu.VMEM((wide, width), BF),
            pltpu.VMEM((CORES, groups, unit, 128), F32),
            pltpu.VMEM((CORES * groups - 1, unit, 128), F32),
            pltpu.VMEM((YS, unit, 128), F32),
            pltpu.VMEM((ZS, unit, 128), F32),
            pltpu.VMEM((CORES, groups, unit, 128), F32),
            pltpu.VMEM((count, wide), F32),
            pltpu.VMEM((groups, bands, width), BF),
            dma((3,)), dma((HAM_PARTS,)), dma,
            dma((4,)), dma((4,)),
            dma((groups - 1,)), dma((groups - 1,)),
            dma((CORES * groups - 1,)), dma((CORES * groups - 1,)),
            dma((YS - 1,)), dma((YS - 1,)),
            dma((ZS - 1,)), dma((ZS - 1,)),
            dma((CORES * groups - 1,)), dma((CORES * groups - 1,)),
            dma((groups,)), dma((groups,)),
        ],
        compiler_params=pltpu.CompilerParams(
            collective_id=0, has_side_effects=True, vmem_limit_bytes=VMEM_LIMIT
        ),
        name="step",
    )(psi, ham, conn, face_rows)
    return result[:, 0:nodes].astype(F32)


def solution(mesh):
    placed = (P("band", "space"), P("space", None, None), P("space", None), P("space"))
    return jax.shard_map(
        per_device, mesh=mesh, in_specs=placed, out_specs=P("band", "space"), check_vma=False
    )
```

```python
import functools

import jax
import jax.numpy as jnp
from jax import lax
from jax.experimental import pallas as pl
from jax.experimental.pallas import tpu as pltpu
from jax.sharding import PartitionSpec as P

NODE_EL = 512
OWN_EL = 448
CENTER = 6.25
HALF_WIDTH = 7.5
LO = 256
TAIL = 128
MESH = pl.DeviceIdType.MESH
BF = jnp.bfloat16
F32 = jnp.float32
VMEM_LIMIT = 60 * 1024 * 1024

CORES, YS, ZS, BAND_Z = 2, 8, 4, 3
HAM_PARTS = 4
NT = (((1,), (1,)), ((), ()))
TN = (((0,), (0,)), ((), ()))


def nn(a, b):
    return jnp.dot(a, b, preferred_element_type=F32)


def nt(a, b):
    return lax.dot_general(a, b, NT, preferred_element_type=F32)


def remote(src, dst, send, recv, where):
    return pltpu.make_async_remote_copy(
        src_ref=src, dst_ref=dst, send_sem=send, recv_sem=recv, device_id=where, device_id_type=MESH
    )


def split(value):
    high = value.astype(BF)
    return high, (value - high.astype(F32)).astype(BF)


def split3(value):
    high = value.astype(BF)
    rest = value - high.astype(F32)
    middle = rest.astype(BF)
    return high, middle, (rest - middle.astype(F32)).astype(BF)


def lanes(start, size):
    return pl.ds(pl.multiple_of(start, 128), size)


def pick(table, which, first, count, total):
    bands = total.shape[0]
    for h in range(count):
        total = jnp.where(which == first + h, table[h * bands:(h + 1) * bands, :], total)
    return total


def place(part, which, first, count, columns):
    zero = jnp.zeros_like(part)
    rows = [jnp.where(which == first + h, part, zero) for h in range(count)]
    return nt(jnp.concatenate(rows, axis=0), columns)


def indicator(low, depth):
    shape = depth.shape
    return jnp.where(depth == jnp.broadcast_to(low, shape), jnp.ones(shape, BF), jnp.zeros(shape, BF))


def as_bf(value, rows):
    return jnp.broadcast_to(value.astype(F32), (rows, value.shape[1])).astype(BF)


def factor_inverse(mat, panel, beside, after):
    size, wide = mat.shape
    step = 8
    lane = lax.broadcasted_iota(jnp.int32, (step, 128), 1)
    sub = lax.broadcasted_iota(jnp.int32, (step, 128), 0)
    tiles = range(wide // 128)

    def spread_lane(value, j):
        return jnp.broadcast_to(value[:, j:j + 1], (step, 128))

    def spread_row(value, i):
        return jnp.take_along_axis(value, jnp.full((step, 128), i, jnp.int32), axis=0)

    for top in range(0, size, panel):
        if top > 0:
            beside(top - panel, top)
        groups = min(panel, size - top) // step
        block = [
            [mat[top + step * g:top + step * (g + 1), t * 128:(t + 1) * 128] for t in tiles] for g in range(groups)
        ]
        for s in range(groups):
            start = top + step * s
            tile, at = start // 128, start % 128
            columns = [spread_lane(block[s][tile], at + j) for j in range(step)]
            d = {(i, j): spread_row(columns[j], i) for j in range(step) for i in range(j, step)}
            below = [[spread_lane(block[g][tile], at + j) for j in range(step)] for g in range(s + 1, groups)]
            inside = (lane >= at) & (lane < at + step)
            base = [[spread_row(block[s][t], i) for i in range(step)] for t in tiles]
            for i in range(step):
                base[tile][i] = jnp.where(inside, jnp.where(lane == at + i, 1.0, 0.0), base[tile][i])
            rows = [[] for _ in tiles]
            for k in range(step):
                scale = lax.rsqrt(d[k, k])
                factor = {i: d[i, k] * scale for i in range(k + 1, step)}
                for i in range(k + 1, step):
                    for m in range(k + 1, i + 1):
                        d[i, m] = d[i, m] - factor[i] * factor[m]
                for t in tiles:
                    rows[t].append(base[t][k] * scale)
                    for i in range(k + 1, step):
                        base[t][i] = base[t][i] - factor[i] * rows[t][k]
                for part in below:
                    part[k] = part[k] * scale
                    for i in range(k + 1, step):
                        part[i] = part[i] - part[k] * factor[i]
            for t in tiles:
                fresh = rows[t][0]
                for i in range(1, step):
                    fresh = jnp.where(sub == i, rows[t][i], fresh)
                block[s][t] = fresh
            for n, g in enumerate(range(s + 1, groups)):
                for t in tiles:
                    value = block[g][t]
                    if t == tile:
                        value = jnp.where(inside, 0.0, value)
                    for k in range(step):
                        value = value - below[n][k] * rows[t][k]
                    block[g][t] = value
        for g in range(groups):
            for t in tiles:
                mat[top + step * g:top + step * (g + 1), t * 128:(t + 1) * 128] = block[g][t]
        end = top + step * groups
        if end < size:
            first = end // 128 * 128
            fresh = mat[top:end, :]
            row = top + lax.broadcasted_iota(jnp.int32, fresh.shape, 0)
            column = lax.broadcasted_iota(jnp.int32, fresh.shape, 1)
            a, b, c = split3(fresh[:, first:])
            d, e, f = split3(jnp.where((column > row) & (column < end), 0.0, fresh))
            update = lax.dot_general(
                jnp.concatenate([a, a, b, b, a, c], axis=0),
                jnp.concatenate([d, e, d, e, f, d], axis=0),
                TN,
                preferred_element_type=F32,
            )
            rest = mat[end:size, :]
            column = lax.broadcasted_iota(jnp.int32, rest.shape, 1)
            rest = jnp.where((column >= top) & (column < end), 0.0, rest)
            mat[end:size, :] = rest - update[end - first:size - first, :]
        if top > 0:
            after(top - panel, top)


def fold(matrix):
    rest = matrix.shape[0] - 128
    corner = pltpu.roll(matrix[128:, 128:], rest, 1)
    lane = lax.broadcasted_iota(jnp.int32, corner.shape, 1)
    first = jnp.where(lane < rest, matrix[0:rest, 0:128], corner)
    return jnp.concatenate([first, matrix[rest:, 0:128]], axis=0)


def unfold(folded):
    count = folded.shape[0]
    rest = count - 128
    turned = pltpu.roll(folded[rest:, :].T, rest, 1)
    lane = lax.broadcasted_iota(jnp.int32, folded.shape, 1)
    first = jnp.where(lane[0:rest] < rest, folded[0:rest, :], turned[0:rest, :])
    left = jnp.concatenate([first, folded[rest:, :]], axis=0)
    right = jnp.concatenate([turned, pltpu.roll(folded[0:rest, :], rest, 1)], axis=0)
    return jnp.concatenate([left, jnp.where(lane < rest, right, 0.0)], axis=1)


def step_kernel(
    total_nodes, psi_hbm, ham_hbm, conn_hbm, face_hbm, out_ref,
    psi_ref, conn_ref, face_ref, ham, onehot, onehot_ghost, onehot_face, hi_ref, hi_ghost, hi_face, base, field, xb, xg,
    gathered, ghosted, products, high_ref, low_ref, tail_high, kept,
    send1, send2, send3, send4, got1, got2, got3, got4,
    pieces, rows_all, gram, group_in, y_in, z_in, whole, mat, ortho,
    in_sem, ham_sem, own_sem, f_send, f_recv, a_send, a_recv, r_send, r_recv, y_send, y_recv, z_send, z_recv,
    g_send, g_recv, b_send, b_recv,
):
    bands, nodes = psi_ref.shape
    elems = conn_ref.shape[0]
    faces = face_ref.shape[0]
    own_blocks = pl.cdiv(nodes, LO)
    ghost_blocks = pl.cdiv(faces, LO)
    face_pad = got1.shape[1]
    shift = own_blocks * LO - nodes
    domains = lax.axis_size("space")
    space = lax.axis_index("space")
    band = lax.axis_index("band")
    groups, _, width = pieces.shape
    count = groups * bands
    wide = mat.shape[1]
    core = lax.rem(space, CORES)
    y = lax.rem(space // CORES, YS)
    z = space // (CORES * YS)
    below = {"space": lax.rem(space + domains - 1, domains)}
    above = {"space": lax.rem(space + 1, domains)}
    twin = {"space": space + 1 - 2 * core}

    inputs = [
        pltpu.make_async_copy(source, held, in_sem.at[n])
        for n, (source, held) in enumerate([(face_hbm, face_ref), (psi_hbm, psi_ref), (conn_hbm, conn_ref)])
    ]
    for c in inputs:
        c.start()

    band_x = groups // BAND_Z
    steps = [(i, k) for i in range(band_x) for k in range(BAND_Z) if i + k > 0]
    steps.sort(key=lambda step: -(min(step[0], band_x - step[0]) + 1.5 * (step[1] > 0)))

    def band_at(step):
        i, k = step
        return lax.rem(band // BAND_Z + i, band_x) * BAND_Z + lax.rem(lax.rem(band, BAND_Z) + k, BAND_Z)

    def band_peer(step):
        return {"band": band_at(step)}

    def y_peer(d):
        return {"space": (z * YS + lax.rem(y + d, YS)) * CORES + core}

    def z_peer(d):
        return {"space": (lax.rem(z + d, ZS) * YS + y) * CORES + core}

    def group_peer(c, step):
        there = {"band": band_at(step)}
        if c > 0:
            there["space"] = twin["space"]
        return there

    members = [(c, step) for step in steps for c in range(CORES)] + [(1, (0, 0))]
    y_steps = sorted(range(1, YS), key=lambda d: -min(d, YS - d))
    z_steps = sorted(range(1, ZS), key=lambda d: -min(d, ZS - d))
    peers = [below, above]
    peers += [group_peer(c, d) for c, d in members]
    peers += [y_peer(d) for d in y_steps]
    peers += [z_peer(d) for d in z_steps]
    barrier = pltpu.get_barrier_semaphore()
    for there in peers:
        pl.semaphore_signal(barrier, inc=1, device_id=there, device_id_type=MESH)

    per = elems // HAM_PARTS
    ham_copies = []
    for k in range(HAM_PARTS):
        part = slice(k * per, (k + 1) * per)
        ham_copies.append(pltpu.make_async_copy(ham_hbm.at[part], ham.at[part], ham_sem.at[k]))
        ham_copies[-1].start()

    inputs[0].wait()
    depth = lax.broadcasted_iota(jnp.int32, (LO, NODE_EL), 0).astype(F32).astype(BF)
    for k in range(face_pad // 128):
        size = min(128, faces - k * 128)
        named = jnp.full((1, 128), -1, jnp.int32)
        spot = lax.broadcasted_iota(jnp.int32, (1, 128), 1)
        if size == 128:
            named = face_ref[k * 128:(k + 1) * 128].reshape(1, 128)
        else:
            tail = face_ref[faces - 128:faces].reshape(1, 128)
            named = jnp.where(spot < size, pltpu.roll(tail, size, 1), -1)
        cols = slice(k * 128, (k + 1) * 128)
        onehot_face[:, cols] = indicator(as_bf(named & (LO - 1), 1), depth[:, 0:128])
        hi_face[:, cols] = as_bf(named >> 8, bands)

    def take_face(blocks):
        table = nn(blocks, onehot_face[...]).astype(BF)
        return pick(table, hi_face[...], 0, own_blocks, jnp.zeros((bands, face_pad), BF))

    inputs[1].wait()
    for h in range(own_blocks):
        rows = slice(h * bands, (h + 1) * bands)
        if (h + 1) * LO <= nodes:
            value = psi_ref[:, h * LO:(h + 1) * LO]
            base[rows, :] = value
            xb[rows, :] = value.astype(BF)
        else:
            base[rows, :] = jnp.zeros((bands, LO), F32)
            base[rows, 0:nodes - h * LO] = psi_ref[:, h * LO:nodes]
            xb[rows, :] = base[rows, :].astype(BF)
    send1[...] = take_face(xb[...])
    pl.semaphore_wait(barrier, len(peers))
    copy1 = remote(send1, got1, f_send.at[0], f_recv.at[0], below)
    copy1.start()

    inputs[2].wait()
    spot = lax.broadcasted_iota(jnp.int32, (1, NODE_EL), 1)

    def prepare(e, carry):
        named = conn_ref[pl.ds(e, 1), :]
        named = jnp.where(spot >= OWN_EL, named + shift, named)
        marks = indicator(as_bf(named & (LO - 1), 1), depth)
        which = as_bf(named >> 8, bands)
        cols = lanes(e * NODE_EL, NODE_EL)
        onehot[:, cols] = marks
        hi_ref[:, cols] = which
        cols = lanes(e * TAIL, TAIL)
        onehot_ghost[:, cols] = marks[:, NODE_EL - TAIL:]
        hi_ghost[:, cols] = which[:, NODE_EL - TAIL:]
        return carry

    lax.fori_loop(0, elems, prepare, 0, unroll=2)
    xg[...] = jnp.zeros(xg.shape, BF)
    rows_all[count:, :] = jnp.zeros((rows_all.shape[0] - count, width), BF)

    def gather_own():
        def body(e, carry):
            cols = lanes(e * NODE_EL, NODE_EL)
            table = nn(xb[...], onehot[:, cols]).astype(BF)
            gathered[:, cols] = pick(table, hi_ref[:, cols], 0, own_blocks, jnp.zeros((bands, NODE_EL), BF))
            return carry

        lax.fori_loop(0, elems, body, 0, unroll=12)

    def gather_ghost(values):
        for h in range(ghost_blocks):
            size = min(LO, face_pad - h * LO)
            xg[h * bands:(h + 1) * bands, 0:size] = values[:, h * LO:h * LO + size].astype(BF)
        table = nn(xg[...], onehot_ghost[...]).astype(BF)
        ghosted[...] = pick(table, hi_ghost[...], own_blocks, ghost_blocks, jnp.zeros((bands, elems * TAIL), BF))

    def multiply_own():
        def body(e, carry):
            cols = lanes(e * NODE_EL, NODE_EL)
            products[:, cols] = nn(gathered[:, cols], ham[e])
            return carry

        lax.fori_loop(0, elems, body, 0, unroll=4)

    def tail_cols(e):
        return slice((e + 1) * NODE_EL - TAIL, (e + 1) * NODE_EL)

    def multiply_tail():
        for e in range(elems):
            cols = slice(e * NODE_EL, (e + 1) * NODE_EL)
            products[:, tail_cols(e)] = nn(gathered[:, cols], ham[e, :, NODE_EL - TAIL:])

    def upper():
        for e in range(elems):
            some = slice(e * TAIL, (e + 1) * TAIL)
            cols = tail_cols(e)
            value = products[:, cols] + nn(ghosted[:, some], ham[e, NODE_EL - TAIL:, NODE_EL - TAIL:])
            high, low = split(value)
            tail_high[:, some] = high
            high_ref[:, cols], low_ref[:, cols] = high, low
        total = place(tail_high[...], hi_ghost[...], own_blocks, ghost_blocks, onehot_ghost[...])
        parts = [
            total[h * bands:(h + 1) * bands, 0:min(LO, face_pad - h * LO)] for h in range(ghost_blocks)
        ]
        return jnp.concatenate(parts, axis=1)

    def multiply_ghost():
        def body(e, carry):
            some = lanes(e * TAIL, TAIL)
            cols = lanes(e * NODE_EL, NODE_EL - TAIL)
            value = products[:, cols] + nn(ghosted[:, some], ham[e, NODE_EL - TAIL:, 0:NODE_EL - TAIL])
            high_ref[:, cols], low_ref[:, cols] = split(value)
            return carry

        lax.fori_loop(0, elems, body, 0, unroll=4)

    def multiply_rest():
        for e in range(elems):
            gathered[:, tail_cols(e)] = gathered[:, tail_cols(e)] + ghosted[:, e * TAIL:(e + 1) * TAIL]

        def body(e, carry):
            cols = lanes(e * NODE_EL, NODE_EL - TAIL)
            value = nn(gathered[:, lanes(e * NODE_EL, NODE_EL)], ham[e, :, 0:NODE_EL - TAIL])
            high_ref[:, cols], low_ref[:, cols] = split(value)
            return carry

        lax.fori_loop(0, elems, body, 0, unroll=4)

    def scatter_own(part):
        size = elems * NODE_EL // 4
        total = None
        for k in range(4):
            cols = slice(k * size, (k + 1) * size)
            value = place(part[:, cols], hi_ref[:, cols], 0, own_blocks, onehot[:, cols])
            total = value if total is None else total + value
        return total

    def put_face(received):
        return place(received, hi_face[...], 0, own_blocks, onehot_face[...])

    gather_own()
    for c in ham_copies:
        c.wait()
    multiply_own()
    copy1.wait()
    gather_ghost(got1[...])
    kept[...] = upper()
    send2[...] = kept[...].astype(BF)
    copy2 = remote(send2, got2, f_send.at[1], f_recv.at[1], above)
    copy2.start()
    multiply_ghost()
    partial_value = scatter_own(high_ref) - CENTER * base[...]
    field[...] = partial_value
    send3[...] = take_face((partial_value / HALF_WIDTH).astype(BF))
    copy3 = remote(send3, got3, f_send.at[2], f_recv.at[2], below)
    copy3.start()
    field[...] += scatter_own(low_ref)
    copy2.wait()
    field[...] = (field[...] + put_face(got2[...])) / HALF_WIDTH
    xb[...] = field[...].astype(BF)
    gather_own()
    multiply_tail()
    copy3.wait()
    gather_ghost(got3[...].astype(F32) + kept[...] / HALF_WIDTH)
    send4[...] = upper().astype(BF)
    copy4 = remote(send4, got4, f_send.at[3], f_recv.at[3], above)
    copy4.start()
    multiply_rest()
    partial_value = scatter_own(high_ref) + scatter_own(low_ref) - CENTER * field[...]
    copy4.wait()
    field[...] = 2.0 * ((partial_value + put_face(got4[...])) / HALF_WIDTH) - base[...]

    blocks = width // 128
    for piece in range(groups * blocks):
        dst = slice((piece % blocks) * 128, (piece % blocks + 1) * 128)
        if piece // 2 < own_blocks:
            rows = slice(piece // 2 * bands, (piece // 2 + 1) * bands)
            src = slice((piece % 2) * 128, (piece % 2 + 1) * 128)
            pieces[piece // blocks, :, dst] = field[rows, src].astype(BF)
        else:
            pieces[piece // blocks, :, dst] = jnp.zeros((bands, 128), BF)

    def finish(copies):
        for c in copies:
            c.wait()

    mine = pl.ds(pl.multiple_of(band * bands, bands), bands)
    copies = []
    for n, step in enumerate(steps):
        there = band_peer(step)
        copies.append(remote(pieces.at[there["band"]], rows_all.at[mine], a_send.at[n], a_recv.at[n], there))
        copies[-1].start()
    rows_all[mine, :] = pieces[band]
    finish(copies)

    folded = fold(nt(rows_all[0:count, :], rows_all[...]))
    gram[...] = folded.reshape(gram.shape)
    copies = []
    for n, (c, d) in enumerate(members):
        there = group_peer(c, d)
        tile = gram.at[core if c == 0 else 1 - core, there["band"]]
        copies.append(remote(tile, group_in.at[n], r_send.at[n], r_recv.at[n], there))
        copies[-1].start()
    finish(copies)
    value = gram[core, band]
    for n in range(len(members)):
        value = value + group_in[n]
    y_in[y] = value

    copies = []
    for d in y_steps:
        copies.append(remote(y_in.at[y], y_in.at[y], y_send.at[d - 1], y_recv.at[d - 1], y_peer(d)))
        copies[-1].start()
    finish(copies)
    value = y_in[0]
    for k in range(1, YS):
        value = value + y_in[k]
    z_in[z] = value

    copies = []
    for d in z_steps:
        copies.append(remote(z_in.at[z], z_in.at[z], z_send.at[d - 1], z_recv.at[d - 1], z_peer(d)))
        copies[-1].start()
    finish(copies)
    value = z_in[0]
    for k in range(1, ZS):
        value = value + z_in[k]
    whole[core, band] = value

    copies = []
    piece = whole.at[core, band]
    for n, (c, d) in enumerate(members):
        copies.append(remote(piece, piece, g_send.at[n], g_recv.at[n], group_peer(c, d)))
        copies[-1].start()
    finish(copies)

    mat[...] = unfold(whole[...].reshape(count, 128) / total_nodes)

    def landing(source):
        return out_ref.at[:, lanes(source * width, width)]

    def back(k):
        return remote(ortho.at[k], landing(band), b_send.at[k], b_recv.at[band], {"band": k})

    def keep(k):
        return pltpu.make_async_copy(ortho.at[k], landing(band), own_sem)

    def rows_of(start, end):
        value = mat[start:end, :]
        row = start + lax.broadcasted_iota(jnp.int32, value.shape, 0)
        column = lax.broadcasted_iota(jnp.int32, value.shape, 1)
        parts = jnp.concatenate(split(jnp.where(column <= row, value, 0.0)), axis=0)
        both = nn(parts, rows_all[...])
        value = (both[0:end - start] + both[end - start:]).astype(BF)
        ortho[start // bands:end // bands] = value.reshape((end - start) // bands, bands, width)

    def deliver(start, end):
        for k in range(start // bands, end // bands):
            @pl.when(band != k)
            def _():
                back(k).start()

            @pl.when(band == k)
            def _():
                keep(k).start()

    panel = 2 * bands
    factor_inverse(mat, panel, rows_of, deliver)
    rows_of(count - panel, count)
    deliver(count - panel, count)
    for k in range(groups):
        @pl.when(band != k)
        def _():
            back(k).wait_send()
            remote(ortho.at[k], landing(k), b_send.at[k], b_recv.at[k], {"band": k}).wait_recv()

        @pl.when(band == k)
        def _():
            keep(k).wait()


def per_device(psi, ham, conn, face_rows):
    bands, nodes = psi.shape
    elems = conn.shape[0]
    faces = face_rows.shape[0]
    groups = lax.axis_size("band")
    own_blocks = pl.cdiv(nodes, LO)
    ghost_blocks = pl.cdiv(faces, LO)
    face_pad = pl.cdiv(faces, 128) * 128
    width = pl.cdiv(pl.cdiv(nodes, 128), groups) * 128
    own = own_blocks * bands
    entries = elems * NODE_EL
    count = groups * bands
    wide = pl.cdiv(count, 128) * 128
    unit = count // 2 // groups
    anywhere = pl.BlockSpec(memory_space=pl.ANY)
    dma = pltpu.SemaphoreType.DMA

    result = pl.pallas_call(
        functools.partial(step_kernel, float(nodes * lax.axis_size("space"))),
        out_shape=pltpu.VMEM((bands, groups * width), BF),
        in_specs=[anywhere] * 4,
        out_specs=pl.BlockSpec(memory_space=pltpu.VMEM),
        scratch_shapes=[
            pltpu.VMEM(psi.shape, F32),
            pltpu.VMEM(conn.shape, jnp.int32),
            pltpu.VMEM(face_rows.shape, jnp.int32),
            pltpu.VMEM(ham.shape, BF),
            pltpu.VMEM((LO, entries), BF),
            pltpu.VMEM((LO, elems * TAIL), BF),
            pltpu.VMEM((LO, face_pad), BF),
            pltpu.VMEM((bands, entries), BF),
            pltpu.VMEM((bands, elems * TAIL), BF),
            pltpu.VMEM((bands, face_pad), BF),
            pltpu.VMEM((own, LO), F32),
            pltpu.VMEM((own, LO), F32),
            pltpu.VMEM((own, LO), BF),
            pltpu.VMEM((ghost_blocks * bands, LO), BF),
            pltpu.VMEM((bands, entries), BF),
            pltpu.VMEM((bands, elems * TAIL), BF),
            pltpu.VMEM((bands, entries), F32),
            pltpu.VMEM((bands, entries), BF),
            pltpu.VMEM((bands, entries), BF),
            pltpu.VMEM((bands, elems * TAIL), BF),
            pltpu.VMEM((bands, face_pad), F32),
            pltpu.VMEM((bands, face_pad), BF),
            pltpu.VMEM((bands, face_pad), BF),
            pltpu.VMEM((bands, face_pad), BF),
            pltpu.VMEM((bands, face_pad), BF),
            pltpu.VMEM((bands, face_pad), BF),
            pltpu.VMEM((bands, face_pad), BF),
            pltpu.VMEM((bands, face_pad), BF),
            pltpu.VMEM((bands, face_pad), BF),
            pltpu.VMEM((groups, bands, width), BF),
            pltpu.VMEM((wide, width), BF),
            pltpu.VMEM((CORES, groups, unit, 128), F32),
            pltpu.VMEM((CORES * groups - 1, unit, 128), F32),
            pltpu.VMEM((YS, unit, 128), F32),
            pltpu.VMEM((ZS, unit, 128), F32),
            pltpu.VMEM((CORES, groups, unit, 128), F32),
            pltpu.VMEM((count, wide), F32),
            pltpu.VMEM((groups, bands, width), BF),
            dma((3,)), dma((HAM_PARTS,)), dma,
            dma((4,)), dma((4,)),
            dma((groups - 1,)), dma((groups - 1,)),
            dma((CORES * groups - 1,)), dma((CORES * groups - 1,)),
            dma((YS - 1,)), dma((YS - 1,)),
            dma((ZS - 1,)), dma((ZS - 1,)),
            dma((CORES * groups - 1,)), dma((CORES * groups - 1,)),
            dma((groups,)), dma((groups,)),
        ],
        compiler_params=pltpu.CompilerParams(
            collective_id=0, has_side_effects=True, vmem_limit_bytes=VMEM_LIMIT
        ),
        name="step",
    )(psi, ham, conn, face_rows)
    return result[:, 0:nodes].astype(F32)


def solution(mesh):
    placed = (P("band", "space"), P("space", None, None), P("space", None), P("space"))
    return jax.shard_map(
        per_device, mesh=mesh, in_specs=placed, out_specs=P("band", "space"), check_vma=False
    )
```

```python
import functools

import jax
import jax.numpy as jnp
from jax import lax
from jax.experimental import pallas as pl
from jax.experimental.pallas import tpu as pltpu
from jax.sharding import PartitionSpec as P

NODE_EL = 512
OWN_EL = 448
CENTER = 6.25
HALF_WIDTH = 7.5
LO = 256
TAIL = 128
MESH = pl.DeviceIdType.MESH
BF = jnp.bfloat16
F32 = jnp.float32
VMEM_LIMIT = 60 * 1024 * 1024

CORES, YS, ZS, BAND_Z = 2, 8, 4, 3
HAM_PARTS = 4
NT = (((1,), (1,)), ((), ()))
TN = (((0,), (0,)), ((), ()))


def nn(a, b):
    return jnp.dot(a, b, preferred_element_type=F32)


def nt(a, b):
    return lax.dot_general(a, b, NT, preferred_element_type=F32)


def remote(src, dst, send, recv, where):
    return pltpu.make_async_remote_copy(
        src_ref=src, dst_ref=dst, send_sem=send, recv_sem=recv, device_id=where, device_id_type=MESH
    )


def split(value):
    high = value.astype(BF)
    return high, (value - high.astype(F32)).astype(BF)


def split3(value):
    high = value.astype(BF)
    rest = value - high.astype(F32)
    middle = rest.astype(BF)
    return high, middle, (rest - middle.astype(F32)).astype(BF)


def lanes(start, size):
    return pl.ds(pl.multiple_of(start, 128), size)


def pick(table, which, first, count, total):
    bands = total.shape[0]
    for h in range(count):
        total = jnp.where(which == first + h, table[h * bands:(h + 1) * bands, :], total)
    return total


def place(part, which, first, count, columns):
    zero = jnp.zeros_like(part)
    rows = [jnp.where(which == first + h, part, zero) for h in range(count)]
    return nt(jnp.concatenate(rows, axis=0), columns)


def indicator(low, depth):
    shape = depth.shape
    return jnp.where(depth == jnp.broadcast_to(low, shape), jnp.ones(shape, BF), jnp.zeros(shape, BF))


def as_bf(value, rows):
    return jnp.broadcast_to(value.astype(F32), (rows, value.shape[1])).astype(BF)


def factor_inverse(mat, tops, beside, after):
    size, wide = mat.shape
    step = 8
    lane = lax.broadcasted_iota(jnp.int32, (step, 128), 1)
    sub = lax.broadcasted_iota(jnp.int32, (step, 128), 0)
    tiles = range(wide // 128)

    def spread_lane(value, j):
        return jnp.broadcast_to(value[:, j:j + 1], (step, 128))

    def spread_row(value, i):
        return jnp.take_along_axis(value, jnp.full((step, 128), i, jnp.int32), axis=0)

    for number, top in enumerate(tops):
        if number > 0:
            beside(tops[number - 1], top)
        groups = (tops[number + 1] - top if number + 1 < len(tops) else size - top) // step
        block = [
            [mat[top + step * g:top + step * (g + 1), t * 128:(t + 1) * 128] for t in tiles] for g in range(groups)
        ]
        for s in range(groups):
            start = top + step * s
            tile, at = start // 128, start % 128
            columns = [spread_lane(block[s][tile], at + j) for j in range(step)]
            d = {(i, j): spread_row(columns[j], i) for j in range(step) for i in range(j, step)}
            below = [[spread_lane(block[g][tile], at + j) for j in range(step)] for g in range(s + 1, groups)]
            inside = (lane >= at) & (lane < at + step)
            base = [[spread_row(block[s][t], i) for i in range(step)] for t in tiles]
            for i in range(step):
                base[tile][i] = jnp.where(inside, jnp.where(lane == at + i, 1.0, 0.0), base[tile][i])
            rows = [[] for _ in tiles]
            for k in range(step):
                scale = lax.rsqrt(d[k, k])
                factor = {i: d[i, k] * scale for i in range(k + 1, step)}
                for i in range(k + 1, step):
                    for m in range(k + 1, i + 1):
                        d[i, m] = d[i, m] - factor[i] * factor[m]
                for t in tiles:
                    rows[t].append(base[t][k] * scale)
                    for i in range(k + 1, step):
                        base[t][i] = base[t][i] - factor[i] * rows[t][k]
                for part in below:
                    part[k] = part[k] * scale
                    for i in range(k + 1, step):
                        part[i] = part[i] - part[k] * factor[i]
            for t in tiles:
                fresh = rows[t][0]
                for i in range(1, step):
                    fresh = jnp.where(sub == i, rows[t][i], fresh)
                block[s][t] = fresh
            for n, g in enumerate(range(s + 1, groups)):
                for t in tiles:
                    value = block[g][t]
                    if t == tile:
                        value = jnp.where(inside, 0.0, value)
                    for k in range(step):
                        value = value - below[n][k] * rows[t][k]
                    block[g][t] = value
        for g in range(groups):
            for t in tiles:
                mat[top + step * g:top + step * (g + 1), t * 128:(t + 1) * 128] = block[g][t]
        end = top + step * groups
        if end < size:
            first = end // 128 * 128
            fresh = mat[top:end, :]
            row = top + lax.broadcasted_iota(jnp.int32, fresh.shape, 0)
            column = lax.broadcasted_iota(jnp.int32, fresh.shape, 1)
            a, b, c = split3(fresh[:, first:])
            d, e, f = split3(jnp.where((column > row) & (column < end), 0.0, fresh))
            update = lax.dot_general(
                jnp.concatenate([a, a, b, b, a, c], axis=0),
                jnp.concatenate([d, e, d, e, f, d], axis=0),
                TN,
                preferred_element_type=F32,
            )
            rest = mat[end:size, :]
            column = lax.broadcasted_iota(jnp.int32, rest.shape, 1)
            rest = jnp.where((column >= top) & (column < end), 0.0, rest)
            mat[end:size, :] = rest - update[end - first:size - first, :]
        if number > 0:
            after(tops[number - 1], top)


def fold(matrix):
    rest = matrix.shape[0] - 128
    corner = pltpu.roll(matrix[128:, 128:], rest, 1)
    lane = lax.broadcasted_iota(jnp.int32, corner.shape, 1)
    first = jnp.where(lane < rest, matrix[0:rest, 0:128], corner)
    return jnp.concatenate([first, matrix[rest:, 0:128]], axis=0)


def unfold(folded):
    count = folded.shape[0]
    rest = count - 128
    turned = pltpu.roll(folded[rest:, :].T, rest, 1)
    lane = lax.broadcasted_iota(jnp.int32, folded.shape, 1)
    first = jnp.where(lane[0:rest] < rest, folded[0:rest, :], turned[0:rest, :])
    left = jnp.concatenate([first, folded[rest:, :]], axis=0)
    right = jnp.concatenate([turned, pltpu.roll(folded[0:rest, :], rest, 1)], axis=0)
    return jnp.concatenate([left, jnp.where(lane < rest, right, 0.0)], axis=1)


def step_kernel(
    total_nodes, psi_hbm, ham_hbm, conn_hbm, face_hbm, out_ref,
    psi_ref, conn_ref, face_ref, ham, onehot, onehot_ghost, onehot_face, hi_ref, hi_ghost, hi_face, base, field, xb, xg,
    gathered, ghosted, products, high_ref, low_ref, tail_high, kept,
    send1, send2, send3, send4, got1, got2, got3, got4,
    pieces, rows_all, gram, group_in, y_in, z_in, whole, mat, ortho,
    in_sem, ham_sem, own_sem, f_send, f_recv, a_send, a_recv, r_send, r_recv, y_send, y_recv, z_send, z_recv,
    g_send, g_recv, b_send, b_recv,
):
    bands, nodes = psi_ref.shape
    elems = conn_ref.shape[0]
    faces = face_ref.shape[0]
    own_blocks = pl.cdiv(nodes, LO)
    ghost_blocks = pl.cdiv(faces, LO)
    face_pad = got1.shape[1]
    shift = own_blocks * LO - nodes
    domains = lax.axis_size("space")
    space = lax.axis_index("space")
    band = lax.axis_index("band")
    groups, _, width = pieces.shape
    count = groups * bands
    wide = mat.shape[1]
    core = lax.rem(space, CORES)
    y = lax.rem(space // CORES, YS)
    z = space // (CORES * YS)
    below = {"space": lax.rem(space + domains - 1, domains)}
    above = {"space": lax.rem(space + 1, domains)}
    twin = {"space": space + 1 - 2 * core}

    inputs = [
        pltpu.make_async_copy(source, held, in_sem.at[n])
        for n, (source, held) in enumerate([(face_hbm, face_ref), (psi_hbm, psi_ref), (conn_hbm, conn_ref)])
    ]
    for c in inputs:
        c.start()

    band_x = groups // BAND_Z
    steps = [(i, k) for i in range(band_x) for k in range(BAND_Z) if i + k > 0]
    steps.sort(key=lambda step: -(min(step[0], band_x - step[0]) + 1.5 * (step[1] > 0)))

    def band_at(step):
        i, k = step
        return lax.rem(band // BAND_Z + i, band_x) * BAND_Z + lax.rem(lax.rem(band, BAND_Z) + k, BAND_Z)

    def band_peer(step):
        return {"band": band_at(step)}

    def y_peer(d):
        return {"space": (z * YS + lax.rem(y + d, YS)) * CORES + core}

    def z_peer(d):
        return {"space": (lax.rem(z + d, ZS) * YS + y) * CORES + core}

    def group_peer(c, step):
        there = {"band": band_at(step)}
        if c > 0:
            there["space"] = twin["space"]
        return there

    members = [(c, step) for step in steps for c in range(CORES)] + [(1, (0, 0))]
    y_steps = sorted(range(1, YS), key=lambda d: -min(d, YS - d))
    z_steps = sorted(range(1, ZS), key=lambda d: -min(d, ZS - d))
    peers = [below, above]
    peers += [group_peer(c, d) for c, d in members]
    peers += [y_peer(d) for d in y_steps]
    peers += [z_peer(d) for d in z_steps]
    barrier = pltpu.get_barrier_semaphore()
    for there in peers:
        pl.semaphore_signal(barrier, inc=1, device_id=there, device_id_type=MESH)

    per = elems // HAM_PARTS
    ham_copies = []
    for k in range(HAM_PARTS):
        part = slice(k * per, (k + 1) * per)
        ham_copies.append(pltpu.make_async_copy(ham_hbm.at[part], ham.at[part], ham_sem.at[k]))
        ham_copies[-1].start()

    inputs[0].wait()
    depth = lax.broadcasted_iota(jnp.int32, (LO, NODE_EL), 0).astype(F32).astype(BF)
    for k in range(face_pad // 128):
        size = min(128, faces - k * 128)
        named = jnp.full((1, 128), -1, jnp.int32)
        spot = lax.broadcasted_iota(jnp.int32, (1, 128), 1)
        if size == 128:
            named = face_ref[k * 128:(k + 1) * 128].reshape(1, 128)
        else:
            tail = face_ref[faces - 128:faces].reshape(1, 128)
            named = jnp.where(spot < size, pltpu.roll(tail, size, 1), -1)
        cols = slice(k * 128, (k + 1) * 128)
        onehot_face[:, cols] = indicator(as_bf(named & (LO - 1), 1), depth[:, 0:128])
        hi_face[:, cols] = as_bf(named >> 8, bands)

    def take_face(blocks):
        table = nn(blocks, onehot_face[...]).astype(BF)
        return pick(table, hi_face[...], 0, own_blocks, jnp.zeros((bands, face_pad), BF))

    inputs[1].wait()
    for h in range(own_blocks):
        rows = slice(h * bands, (h + 1) * bands)
        if (h + 1) * LO <= nodes:
            value = psi_ref[:, h * LO:(h + 1) * LO]
            base[rows, :] = value
            xb[rows, :] = value.astype(BF)
        else:
            base[rows, :] = jnp.zeros((bands, LO), F32)
            base[rows, 0:nodes - h * LO] = psi_ref[:, h * LO:nodes]
            xb[rows, :] = base[rows, :].astype(BF)
    send1[...] = take_face(xb[...])
    pl.semaphore_wait(barrier, len(peers))
    copy1 = remote(send1, got1, f_send.at[0], f_recv.at[0], below)
    copy1.start()

    inputs[2].wait()
    spot = lax.broadcasted_iota(jnp.int32, (1, NODE_EL), 1)

    def prepare(e, carry):
        named = conn_ref[pl.ds(e, 1), :]
        named = jnp.where(spot >= OWN_EL, named + shift, named)
        marks = indicator(as_bf(named & (LO - 1), 1), depth)
        which = as_bf(named >> 8, bands)
        cols = lanes(e * NODE_EL, NODE_EL)
        onehot[:, cols] = marks
        hi_ref[:, cols] = which
        cols = lanes(e * TAIL, TAIL)
        onehot_ghost[:, cols] = marks[:, NODE_EL - TAIL:]
        hi_ghost[:, cols] = which[:, NODE_EL - TAIL:]
        return carry

    lax.fori_loop(0, elems, prepare, 0, unroll=2)
    xg[...] = jnp.zeros(xg.shape, BF)
    rows_all[count:, :] = jnp.zeros((rows_all.shape[0] - count, width), BF)

    def gather_own():
        def body(e, carry):
            cols = lanes(e * NODE_EL, NODE_EL)
            table = nn(xb[...], onehot[:, cols]).astype(BF)
            gathered[:, cols] = pick(table, hi_ref[:, cols], 0, own_blocks, jnp.zeros((bands, NODE_EL), BF))
            return carry

        lax.fori_loop(0, elems, body, 0, unroll=12)

    def gather_ghost(values):
        for h in range(ghost_blocks):
            size = min(LO, face_pad - h * LO)
            xg[h * bands:(h + 1) * bands, 0:size] = values[:, h * LO:h * LO + size].astype(BF)
        table = nn(xg[...], onehot_ghost[...]).astype(BF)
        ghosted[...] = pick(table, hi_ghost[...], own_blocks, ghost_blocks, jnp.zeros((bands, elems * TAIL), BF))

    def multiply_own():
        def body(e, carry):
            cols = lanes(e * NODE_EL, NODE_EL)
            products[:, cols] = nn(gathered[:, cols], ham[e])
            return carry

        lax.fori_loop(0, elems, body, 0, unroll=4)

    def tail_cols(e):
        return slice((e + 1) * NODE_EL - TAIL, (e + 1) * NODE_EL)

    def multiply_tail():
        for e in range(elems):
            cols = slice(e * NODE_EL, (e + 1) * NODE_EL)
            products[:, tail_cols(e)] = nn(gathered[:, cols], ham[e, :, NODE_EL - TAIL:])

    def upper():
        for e in range(elems):
            some = slice(e * TAIL, (e + 1) * TAIL)
            cols = tail_cols(e)
            value = products[:, cols] + nn(ghosted[:, some], ham[e, NODE_EL - TAIL:, NODE_EL - TAIL:])
            high, low = split(value)
            tail_high[:, some] = high
            high_ref[:, cols], low_ref[:, cols] = high, low
        total = place(tail_high[...], hi_ghost[...], own_blocks, ghost_blocks, onehot_ghost[...])
        parts = [
            total[h * bands:(h + 1) * bands, 0:min(LO, face_pad - h * LO)] for h in range(ghost_blocks)
        ]
        return jnp.concatenate(parts, axis=1)

    def multiply_ghost():
        def body(e, carry):
            some = lanes(e * TAIL, TAIL)
            cols = lanes(e * NODE_EL, NODE_EL - TAIL)
            value = products[:, cols] + nn(ghosted[:, some], ham[e, NODE_EL - TAIL:, 0:NODE_EL - TAIL])
            high_ref[:, cols], low_ref[:, cols] = split(value)
            return carry

        lax.fori_loop(0, elems, body, 0, unroll=4)

    def multiply_rest():
        for e in range(elems):
            gathered[:, tail_cols(e)] = gathered[:, tail_cols(e)] + ghosted[:, e * TAIL:(e + 1) * TAIL]

        def body(e, carry):
            cols = lanes(e * NODE_EL, NODE_EL - TAIL)
            value = nn(gathered[:, lanes(e * NODE_EL, NODE_EL)], ham[e, :, 0:NODE_EL - TAIL])
            high_ref[:, cols], low_ref[:, cols] = split(value)
            return carry

        lax.fori_loop(0, elems, body, 0, unroll=4)

    def scatter_own(part):
        size = elems * NODE_EL // 4
        total = None
        for k in range(4):
            cols = slice(k * size, (k + 1) * size)
            value = place(part[:, cols], hi_ref[:, cols], 0, own_blocks, onehot[:, cols])
            total = value if total is None else total + value
        return total

    def put_face(received):
        return place(received, hi_face[...], 0, own_blocks, onehot_face[...])

    gather_own()
    for c in ham_copies:
        c.wait()
    multiply_own()
    copy1.wait()
    gather_ghost(got1[...])
    kept[...] = upper()
    send2[...] = kept[...].astype(BF)
    copy2 = remote(send2, got2, f_send.at[1], f_recv.at[1], above)
    copy2.start()
    multiply_ghost()
    partial_value = scatter_own(high_ref) - CENTER * base[...]
    field[...] = partial_value
    send3[...] = take_face((partial_value / HALF_WIDTH).astype(BF))
    copy3 = remote(send3, got3, f_send.at[2], f_recv.at[2], below)
    copy3.start()
    field[...] += scatter_own(low_ref)
    copy2.wait()
    field[...] = (field[...] + put_face(got2[...])) / HALF_WIDTH
    xb[...] = field[...].astype(BF)
    gather_own()
    multiply_tail()
    copy3.wait()
    gather_ghost(got3[...].astype(F32) + kept[...] / HALF_WIDTH)
    send4[...] = upper().astype(BF)
    copy4 = remote(send4, got4, f_send.at[3], f_recv.at[3], above)
    copy4.start()
    multiply_rest()
    partial_value = scatter_own(high_ref) + scatter_own(low_ref) - CENTER * field[...]
    copy4.wait()
    field[...] = 2.0 * ((partial_value + put_face(got4[...])) / HALF_WIDTH) - base[...]

    blocks = width // 128
    for piece in range(groups * blocks):
        dst = slice((piece % blocks) * 128, (piece % blocks + 1) * 128)
        if piece // 2 < own_blocks:
            rows = slice(piece // 2 * bands, (piece // 2 + 1) * bands)
            src = slice((piece % 2) * 128, (piece % 2 + 1) * 128)
            pieces[piece // blocks, :, dst] = field[rows, src].astype(BF)
        else:
            pieces[piece // blocks, :, dst] = jnp.zeros((bands, 128), BF)

    def finish(copies):
        for c in copies:
            c.wait()

    mine = pl.ds(pl.multiple_of(band * bands, bands), bands)
    copies = []
    for n, step in enumerate(steps):
        there = band_peer(step)
        copies.append(remote(pieces.at[there["band"]], rows_all.at[mine], a_send.at[n], a_recv.at[n], there))
        copies[-1].start()
    rows_all[mine, :] = pieces[band]
    finish(copies)

    folded = fold(nt(rows_all[0:count, :], rows_all[...]))
    gram[...] = folded.reshape(gram.shape)
    copies = []
    for n, (c, d) in enumerate(members):
        there = group_peer(c, d)
        tile = gram.at[core if c == 0 else 1 - core, there["band"]]
        copies.append(remote(tile, group_in.at[n], r_send.at[n], r_recv.at[n], there))
        copies[-1].start()
    finish(copies)
    value = gram[core, band]
    for n in range(len(members)):
        value = value + group_in[n]
    y_in[y] = value

    copies = []
    for d in y_steps:
        copies.append(remote(y_in.at[y], y_in.at[y], y_send.at[d - 1], y_recv.at[d - 1], y_peer(d)))
        copies[-1].start()
    finish(copies)
    value = y_in[0]
    for k in range(1, YS):
        value = value + y_in[k]
    z_in[z] = value

    copies = []
    for d in z_steps:
        copies.append(remote(z_in.at[z], z_in.at[z], z_send.at[d - 1], z_recv.at[d - 1], z_peer(d)))
        copies[-1].start()
    finish(copies)
    value = z_in[0]
    for k in range(1, ZS):
        value = value + z_in[k]
    whole[core, band] = value

    copies = []
    piece = whole.at[core, band]
    for n, (c, d) in enumerate(members):
        copies.append(remote(piece, piece, g_send.at[n], g_recv.at[n], group_peer(c, d)))
        copies[-1].start()
    finish(copies)

    mat[...] = unfold(whole[...].reshape(count, 128) / total_nodes)

    def landing(source):
        return out_ref.at[:, lanes(source * width, width)]

    def back(k):
        return remote(ortho.at[k], landing(band), b_send.at[k], b_recv.at[band], {"band": k})

    def keep(k):
        return pltpu.make_async_copy(ortho.at[k], landing(band), own_sem)

    def rows_of(start, end):
        value = mat[start:end, :]
        row = start + lax.broadcasted_iota(jnp.int32, value.shape, 0)
        column = lax.broadcasted_iota(jnp.int32, value.shape, 1)
        parts = jnp.concatenate(split(jnp.where(column <= row, value, 0.0)), axis=0)
        both = nn(parts, rows_all[...])
        value = (both[0:end - start] + both[end - start:]).astype(BF)
        ortho[start // bands:end // bands] = value.reshape((end - start) // bands, bands, width)

    def deliver(start, end):
        for k in range(start // bands, end // bands):
            @pl.when(band != k)
            def _():
                back(k).start()

            @pl.when(band == k)
            def _():
                keep(k).start()

    tops = [0, 4 * bands, 8 * bands, 10 * bands]
    factor_inverse(mat, tops, rows_of, deliver)
    rows_of(tops[-1], count)
    deliver(tops[-1], count)
    for k in range(groups):
        @pl.when(band != k)
        def _():
            back(k).wait_send()
            remote(ortho.at[k], landing(k), b_send.at[k], b_recv.at[k], {"band": k}).wait_recv()

        @pl.when(band == k)
        def _():
            keep(k).wait()


def per_device(psi, ham, conn, face_rows):
    bands, nodes = psi.shape
    elems = conn.shape[0]
    faces = face_rows.shape[0]
    groups = lax.axis_size("band")
    own_blocks = pl.cdiv(nodes, LO)
    ghost_blocks = pl.cdiv(faces, LO)
    face_pad = pl.cdiv(faces, 128) * 128
    width = pl.cdiv(pl.cdiv(nodes, 128), groups) * 128
    own = own_blocks * bands
    entries = elems * NODE_EL
    count = groups * bands
    wide = pl.cdiv(count, 128) * 128
    unit = count // 2 // groups
    anywhere = pl.BlockSpec(memory_space=pl.ANY)
    dma = pltpu.SemaphoreType.DMA

    result = pl.pallas_call(
        functools.partial(step_kernel, float(nodes * lax.axis_size("space"))),
        out_shape=pltpu.VMEM((bands, groups * width), BF),
        in_specs=[anywhere] * 4,
        out_specs=pl.BlockSpec(memory_space=pltpu.VMEM),
        scratch_shapes=[
            pltpu.VMEM(psi.shape, F32),
            pltpu.VMEM(conn.shape, jnp.int32),
            pltpu.VMEM(face_rows.shape, jnp.int32),
            pltpu.VMEM(ham.shape, BF),
            pltpu.VMEM((LO, entries), BF),
            pltpu.VMEM((LO, elems * TAIL), BF),
            pltpu.VMEM((LO, face_pad), BF),
            pltpu.VMEM((bands, entries), BF),
            pltpu.VMEM((bands, elems * TAIL), BF),
            pltpu.VMEM((bands, face_pad), BF),
            pltpu.VMEM((own, LO), F32),
            pltpu.VMEM((own, LO), F32),
            pltpu.VMEM((own, LO), BF),
            pltpu.VMEM((ghost_blocks * bands, LO), BF),
            pltpu.VMEM((bands, entries), BF),
            pltpu.VMEM((bands, elems * TAIL), BF),
            pltpu.VMEM((bands, entries), F32),
            pltpu.VMEM((bands, entries), BF),
            pltpu.VMEM((bands, entries), BF),
            pltpu.VMEM((bands, elems * TAIL), BF),
            pltpu.VMEM((bands, face_pad), F32),
            pltpu.VMEM((bands, face_pad), BF),
            pltpu.VMEM((bands, face_pad), BF),
            pltpu.VMEM((bands, face_pad), BF),
            pltpu.VMEM((bands, face_pad), BF),
            pltpu.VMEM((bands, face_pad), BF),
            pltpu.VMEM((bands, face_pad), BF),
            pltpu.VMEM((bands, face_pad), BF),
            pltpu.VMEM((bands, face_pad), BF),
            pltpu.VMEM((groups, bands, width), BF),
            pltpu.VMEM((wide, width), BF),
            pltpu.VMEM((CORES, groups, unit, 128), F32),
            pltpu.VMEM((CORES * groups - 1, unit, 128), F32),
            pltpu.VMEM((YS, unit, 128), F32),
            pltpu.VMEM((ZS, unit, 128), F32),
            pltpu.VMEM((CORES, groups, unit, 128), F32),
            pltpu.VMEM((count, wide), F32),
            pltpu.VMEM((groups, bands, width), BF),
            dma((3,)), dma((HAM_PARTS,)), dma,
            dma((4,)), dma((4,)),
            dma((groups - 1,)), dma((groups - 1,)),
            dma((CORES * groups - 1,)), dma((CORES * groups - 1,)),
            dma((YS - 1,)), dma((YS - 1,)),
            dma((ZS - 1,)), dma((ZS - 1,)),
            dma((CORES * groups - 1,)), dma((CORES * groups - 1,)),
            dma((groups,)), dma((groups,)),
        ],
        compiler_params=pltpu.CompilerParams(
            collective_id=0, has_side_effects=True, vmem_limit_bytes=VMEM_LIMIT
        ),
        name="step",
    )(psi, ham, conn, face_rows)
    return result[:, 0:nodes].astype(F32)


def solution(mesh):
    placed = (P("band", "space"), P("space", None, None), P("space", None), P("space"))
    return jax.shard_map(
        per_device, mesh=mesh, in_specs=placed, out_specs=P("band", "space"), check_vma=False
    )
```
